256 devices in a mesh: cfg: 8 (over y, core), node: 32 (over z, x).
Axes of the slice: x: 4, y: 4, z: 8, core: 2. Of those that a mesh axis runs over, the one named last changes fastest.
Arguments:
- node_feats: bfloat16 [1048576, 256], P(('cfg', 'node')), may hold values from -6 to 6
- neighbors: int32 [1048576, 4], P(('cfg', 'node')), may hold values from 0 to 5119
- self_weight: bfloat16 [256, 256], replicated, may hold values from -0.375 to 0.375
- neighbor_weight: bfloat16 [256, 256], replicated, may hold values from -0.375 to 0.375
- sage_bias: float32 [256], replicated, may hold values from -3 to 3
- conf_index: int32 [32768], P(('cfg', 'node')), may hold values from 0 to 4095
- layout_ids: int32 [128, 32768], P('cfg', 'node'), may hold values from 0 to 127
- join_weight: bfloat16 [256, 256], replicated, may hold values from -0.375 to 0.375
- layout_table: bfloat16 [128, 256], replicated, may hold values from -6 to 6
- join_bias: float32 [256], replicated, may hold values from -3 to 3
- mid_weight: bfloat16 [256, 256], replicated, may hold values from -0.375 to 0.375
- mid_bias: float32 [256], replicated, may hold values from -3 to 3
- score_weight: float32 [256], replicated, may hold values from -0.375 to 0.375
- config_pairs: int32 [512, 2], replicated, may hold values from 0 to 127
Outputs:
- node_embed: bfloat16 [1048576, 256], P(('cfg', 'node'))
- pair_loss: float32 [], replicated
- conf_grad: float32 [32768, 256], P(('cfg', 'node'))
The draws below stay inside these ranges and needn't reach their ends.
All inputs are finite; a program needn't handle non-finite values.
Results may differ from the reference program's by a relative error of at most 0.028.
Values may be sent and summed in bfloat16 or wider, within the bound.
No kernel may reach another device: no remote copies, remote signals or barrier semaphores. Data moves between devices by JAX's collectives and lax.ppermute only.
A program may use at most 64 MiB of HBM per device.

```python
import math
import jax
import jax.numpy as jnp
from jax import lax

D = 256
H = 256
LAYOUTS = 128
K = 4
NODE_DEV = 4096
CF_DEV = 128
CFG_DEV = 16
PAIRS = 512
HALO = 512
NODES = 1048576
CONF = 32768
CONFIGS = 128
N_CFG = 8
N_NODE = 32


def touch_ends(entries, own_key, low, largest):
    longest = entries.shape.index(max(entries.shape))
    spots = []
    for shift in (0, 1):
        where = [jax.random.randint(jax.random.fold_in(own_key, axis), (), 0, length) for axis, length in enumerate(entries.shape)]
        where[longest] = (where[longest] + shift) % entries.shape[longest]
        spots.append(tuple(where))
    return entries.at[spots[0]].set(low).at[spots[1]].set(largest)


def levels(own_key, extent, split, smallest, largest):
    loudness, own = 1.0, jax.random.fold_in(own_key, 6)
    for dim, blocks in split:
        heights = jnp.exp(jax.random.uniform(jax.random.fold_in(own, dim), (blocks,), jnp.float32, smallest / len(split), largest / len(split)))
        loudness = loudness * jnp.repeat(heights, extent[dim] // blocks).reshape([-1 if axis == dim else 1 for axis in range(len(extent))])
    return loudness


def noise(rng, dims, scale, limit, cuts=(), kind=jnp.bfloat16):
    entries = jax.random.normal(rng, dims, jnp.float32) * scale
    if len(cuts) > 0:
        entries = levels(rng, dims, cuts, -0.22, 0.18) * entries
    return jnp.clip(entries, min=-limit, max=limit).astype(kind)


def setup_inputs(seed: int = 0) -> dict:
    arg_keys = jax.random.split(jax.random.key(seed), 15)
    node_feats = noise(arg_keys[0], (NODES, D), 1.0, 6.0, ((0, 256),))
    neighbors = touch_ends(jax.random.randint(arg_keys[1], (NODES, K), 0, NODE_DEV + 2 * HALO), jax.random.fold_in(arg_keys[1], 1), 0, (NODE_DEV + 2 * HALO) - 1).astype(jnp.int32)
    self_weight = noise(arg_keys[2], (D, D), D ** -0.5, 0.375)
    neighbor_weight = noise(arg_keys[3], (D, D), D ** -0.5, 0.375)
    sage_bias = noise(arg_keys[4], (D,), 0.5, 3.0, (), jnp.float32)
    conf_index = touch_ends(jax.random.randint(arg_keys[5], (CONF,), 0, NODE_DEV), jax.random.fold_in(arg_keys[5], 1), 0, NODE_DEV - 1).astype(jnp.int32)
    layout_ids = touch_ends(jax.random.randint(arg_keys[6], (CONFIGS, CONF), 0, LAYOUTS), jax.random.fold_in(arg_keys[6], 1), 0, LAYOUTS - 1).astype(jnp.int32)
    join_weight = noise(arg_keys[7], (D, H), D ** -0.5, 0.375)
    layout_table = noise(arg_keys[8], (LAYOUTS, H), 1.0, 6.0)
    join_bias = noise(arg_keys[9], (H,), 0.5, 3.0, (), jnp.float32)
    mid_weight = noise(arg_keys[10], (H, H), H ** -0.5, 0.375)
    mid_bias = noise(arg_keys[11], (H,), 0.5, 3.0, (), jnp.float32)
    score_weight = noise(arg_keys[12], (H,), H ** -0.5, 0.375, (), jnp.float32)
    config_pairs = touch_ends(jax.random.randint(arg_keys[13], (PAIRS, 2), 0, CONFIGS), jax.random.fold_in(arg_keys[13], 1), 0, CONFIGS - 1).astype(jnp.int32)
    return dict(node_feats=node_feats, neighbors=neighbors, self_weight=self_weight, neighbor_weight=neighbor_weight, sage_bias=sage_bias, conf_index=conf_index, layout_ids=layout_ids, join_weight=join_weight, layout_table=layout_table, join_bias=join_bias, mid_weight=mid_weight, mid_bias=mid_bias, score_weight=score_weight, config_pairs=config_pairs)


def silu_slope(value):
    sigma = jax.nn.sigmoid(value)
    return sigma * (1.0 + value * (1.0 - sigma))

def reference(node_feats, neighbors, self_weight, neighbor_weight, sage_bias, conf_index, layout_ids, join_weight, layout_table, join_bias, mid_weight, mid_bias, score_weight, config_pairs):
    devices = N_CFG * N_NODE
    zero_rim = jnp.zeros((HALO, D), node_feats.dtype)
    padded = jnp.concatenate([zero_rim, node_feats, zero_rim], axis=0)
    neighbor_ids = neighbors.reshape(devices, NODE_DEV, K)
    conf_blocks = conf_index.reshape(devices, CF_DEV)

    def layer_block(inputs):
        block_index, block_nbrs, block_conf = inputs
        start_row = block_index * NODE_DEV
        window = lax.dynamic_slice_in_dim(padded, start_row, NODE_DEV + 2 * HALO, 0)
        own_rows = lax.dynamic_slice_in_dim(node_feats, start_row, NODE_DEV, 0)
        summed = jnp.zeros((NODE_DEV, D), jnp.float32)
        for neighbor in range(K):
            summed = summed + jnp.take(window, block_nbrs[:, neighbor], axis=0).astype(jnp.float32)
        mean_rows = (summed / K).astype(jnp.bfloat16)
        pre_act = jnp.dot(own_rows, self_weight, preferred_element_type=jnp.float32) + jnp.dot(mean_rows, neighbor_weight, preferred_element_type=jnp.float32) + sage_bias
        act_out = jax.nn.silu(pre_act).astype(jnp.bfloat16)
        return (act_out, jnp.take(act_out, block_conf, axis=0))
    layer_out, conf_src = lax.map(layer_block, (jnp.arange(devices, dtype=jnp.int32), neighbor_ids, conf_blocks))
    per_peer = CF_DEV // N_NODE
    conf_rows = conf_src.reshape(N_CFG, N_NODE, N_NODE, per_peer, D).transpose(2, 0, 1, 3, 4).reshape(-1, D)
    row_count = conf_rows.shape[0]
    base = jnp.dot(conf_rows, join_weight, preferred_element_type=jnp.float32)
    norm_scale = 1.0 / math.sqrt(row_count)

    def hidden_pair(row_ids):
        inner_pre = base + jnp.take(layout_table, row_ids, axis=0).astype(jnp.float32) + join_bias
        inner_act = jax.nn.silu(inner_pre).astype(jnp.bfloat16)
        outer_pre = jnp.dot(inner_act, mid_weight, preferred_element_type=jnp.float32) + mid_bias
        return (inner_pre, outer_pre)

    def config_total(row_ids):
        inner_pre, outer_pre = hidden_pair(row_ids)
        scores = jnp.dot(jax.nn.silu(outer_pre), score_weight, precision=lax.Precision.HIGHEST)
        return jnp.sum(scores) * norm_scale
    config_score = lax.map(config_total, layout_ids)
    pair_first = config_pairs[:, 0]
    pair_second = config_pairs[:, 1]
    score_gap = jnp.take(config_score, pair_second) - jnp.take(config_score, pair_first)
    pair_loss = jnp.mean(jax.nn.softplus(score_gap))
    pair_slope = jax.nn.sigmoid(score_gap) / config_pairs.shape[0]
    columns = jnp.arange(CONFIGS, dtype=jnp.int32)
    signed = (pair_second[:, None] == columns[None, :]).astype(jnp.float32) - (pair_first[:, None] == columns[None, :]).astype(jnp.float32)
    score_grad = 65536.0 * jnp.dot(pair_slope, signed, precision=lax.Precision.HIGHEST)

    def config_step(carried, inputs):
        row_ids, config_grad = inputs
        inner_pre, outer_pre = hidden_pair(row_ids)
        outer_grad = (config_grad * norm_scale * score_weight * silu_slope(outer_pre)).astype(jnp.bfloat16)
        inner_grad = lax.dot_general(outer_grad, mid_weight, (((1,), (1,)), ((), ())), preferred_element_type=jnp.float32) * silu_slope(inner_pre)
        return (carried + inner_grad, None)

    def group_step(carried, inputs):
        group_ids, group_grads = inputs
        zero_rows = jnp.zeros((row_count, H), jnp.float32)
        group_part, unused = lax.scan(config_step, zero_rows, (group_ids, group_grads))
        rounded = lax.optimization_barrier(group_part.astype(jnp.bfloat16))
        return (carried + rounded.astype(jnp.float32), None)
    start_rows = jnp.zeros((row_count, H), jnp.float32)
    row_total, unused = lax.scan(group_step, start_rows, (layout_ids.reshape(N_CFG, CFG_DEV, row_count), score_grad.reshape(N_CFG, CFG_DEV)))
    row_grad = row_total.astype(jnp.bfloat16)
    conf_rows_grad = lax.dot_general(row_grad, join_weight, (((1,), (1,)), ((), ())), preferred_element_type=jnp.float32)
    conf_grad = conf_rows_grad.reshape(N_NODE, N_CFG, N_NODE, per_peer, D).transpose(1, 2, 0, 3, 4).reshape(-1, D)
    return (layer_out.reshape(-1, D), pair_loss, conf_grad)
```

```python
import functools
import math

import jax
import jax.numpy as jnp
from jax import lax
from jax.experimental import pallas as pl
from jax.experimental.pallas import tpu as pltpu
from jax.sharding import PartitionSpec as P

HALO = 512
f32 = jnp.float32
bf16 = jnp.bfloat16
VMEM = pl.BlockSpec(memory_space=pltpu.VMEM)
SMEM = pl.BlockSpec(memory_space=pltpu.SMEM)


def half_silu(half):
    tanh = jnp.tanh(half)
    scaled = half * tanh
    return half + scaled, tanh, scaled


def twice_slope(half, tanh, scaled):
    inner = 1.0 + half - scaled
    return inner + tanh * inner


def build_table(table, before, feats, after):
    offset = 0
    for source in (before, feats, after):
        rows = source.shape[0]
        step = min(rows, 512)
        for start in range(0, rows, step):
            value = source[start : start + step, :].astype(f32)
            table[pl.ds(2 * (offset + start), step, stride=2), :] = value[:, :128]
            table[pl.ds(2 * (offset + start) + 1, step, stride=2), :] = value[:, 128:]
        offset += rows


def conf_kernel(nodes, nbrs, picks, before, feats, after, sw, nw, bias, out, table, own, acc):
    build_table(table, before, feats, after)
    count = picks.shape[0]
    rows = table.reshape(table.shape[0] // 2, 2, 128)
    own3 = own.reshape(count, 2, 128)
    acc3 = acc.reshape(count, 2, 128)

    def body(block, carry):
        values = []
        for j in range(8):
            g = picks[block * 8 + j]
            near = [rows[nbrs[k * nodes + g]] for k in range(4)]
            values.append((rows[HALO + g], (near[0] + near[1]) + (near[2] + near[3])))
        for j in range(8):
            own3[block * 8 + j], acc3[block * 8 + j] = values[j]
        return carry

    lax.fori_loop(0, count // 8, body, 0)
    halves = [ref[pl.ds(side, count, stride=2), :] for ref in (own, acc) for side in (0, 1)]
    out[...] = layer_rows(
        halves[0].astype(bf16),
        halves[1].astype(bf16),
        (halves[2] * 0.25).astype(bf16),
        (halves[3] * 0.25).astype(bf16),
        sw,
        nw,
        bias,
    )


def layer_rows(own_left, own_right, left, right, sw, nw, bias):
    pre = jnp.dot(own_left, sw[:128, :], preferred_element_type=f32)
    pre += jnp.dot(own_right, sw[128:, :], preferred_element_type=f32)
    pre += jnp.dot(left, nw[:128, :], preferred_element_type=f32)
    pre += jnp.dot(right, nw[128:, :], preferred_element_type=f32)
    return half_silu(0.5 * (pre + bias[...]))[0].astype(bf16)


def conf_rows_of(nbrs, picks, before, feats, after, sw, nw, bias):
    nodes, width = feats.shape
    count = picks.shape[0]
    window = nodes + 2 * HALO
    return pl.pallas_call(
        functools.partial(conf_kernel, nodes),
        out_shape=jax.ShapeDtypeStruct((count, width), bf16),
        in_specs=[SMEM, SMEM] + [VMEM] * 6,
        out_specs=VMEM,
        scratch_shapes=[
            pltpu.VMEM((2 * window, 128), f32),
            pltpu.VMEM((2 * count, 128), f32),
            pltpu.VMEM((2 * count, 128), f32),
        ],
        cost_estimate=pl.CostEstimate(
            flops=4 * count * width * width, transcendentals=0, bytes_accessed=6 << 20
        ),
        compiler_params=pltpu.CompilerParams(vmem_limit_bytes=24 << 20),
        name="conf_rows",
    )(nbrs, picks, before, feats, after, sw, nw, bias)


def layer_kernel(tile, nodes, nbrs, before, feats, after, sw, nw, bias, out, table, acc):
    step = pl.program_id(0)

    @pl.when(step == 0)
    def _():
        build_table(table, before, feats, after)

    rows = table.reshape(table.shape[0] // 2, 2, 128)
    acc3 = acc.reshape(tile, 2, 128)
    unroll = 16

    def body(block, carry):
        values = []
        for j in range(unroll):
            g = step * tile + block * unroll + j
            near = [rows[nbrs[k * nodes + g]] for k in range(4)]
            values.append((near[0] + near[1]) + (near[2] + near[3]))
        for j in range(unroll):
            acc3[block * unroll + j] = values[j]
        return carry

    lax.fori_loop(0, tile // unroll, body, 0)
    own = feats[pl.ds(pl.multiple_of(step * tile, tile), tile), :]
    out[...] = layer_rows(
        own[:, :128],
        own[:, 128:],
        (acc[pl.ds(0, tile, stride=2), :] * 0.25).astype(bf16),
        (acc[pl.ds(1, tile, stride=2), :] * 0.25).astype(bf16),
        sw,
        nw,
        bias,
    )


def layer_of(nbrs, before, feats, after, sw, nw, bias):
    nodes, width = feats.shape
    tile = 512
    window = nodes + 2 * HALO
    return pl.pallas_call(
        functools.partial(layer_kernel, tile, nodes),
        out_shape=jax.ShapeDtypeStruct((nodes, width), bf16),
        grid=(nodes // tile,),
        in_specs=[SMEM] + [VMEM] * 6,
        out_specs=pl.BlockSpec((tile, width), lambda i: (i, 0)),
        scratch_shapes=[
            pltpu.VMEM((2 * window, 128), f32),
            pltpu.VMEM((2 * tile, 128), f32),
        ],
        cost_estimate=pl.CostEstimate(
            flops=4 * nodes * width * width, transcendentals=0, bytes_accessed=64 << 20
        ),
        compiler_params=pltpu.CompilerParams(vmem_limit_bytes=24 << 20),
        name="graph_layer",
    )(nbrs, before, feats, after, sw, nw, bias)


def scorer_kernel(groups, order, where, *refs):
    xs, refs = refs[:groups], refs[groups:]
    ids, join, table, jbias, mid, mbias, weight, grads, sent = refs[:9]
    base, tabh, midh, back, total = refs[9:]
    step = pl.program_id(0)
    chunk = xs[0].shape[0]
    configs = ids.shape[0]
    layouts = table.shape[0]

    @pl.when(step == 0)
    def _():
        for i in range(groups):
            base[i] = 0.5 * (
                jnp.dot(xs[i][...], join[...], preferred_element_type=f32) + jbias[...]
            )
        tabh[...] = (table[...].astype(f32) * 0.5).astype(bf16)
        middle = mid[...].astype(f32)
        midh[...] = (middle * 0.5).astype(bf16)
        back[...] = jnp.transpose(middle * (weight[...] * 0.25)).astype(bf16)
        total[...] = jnp.zeros_like(total)

    columns = jnp.transpose(ids[...].astype(f32))
    lanes = lax.broadcasted_iota(jnp.int32, (chunk, layouts), 1).astype(f32)
    rows = base[step]
    some = 4
    for first in range(0, configs, some):
        picks = jnp.concatenate(
            [
                jnp.where(columns[:, k : k + 1] == lanes, 1.0, 0.0).astype(bf16)
                for k in range(first, first + some)
            ],
            axis=0,
        )
        half = jnp.dot(picks, tabh[...], preferred_element_type=f32)
        half = half + jnp.concatenate([rows] * some, axis=0)
        act, tanh, scaled = half_silu(half)
        outer = jnp.dot(act.astype(bf16), midh[...], preferred_element_type=f32)
        outer = outer + 0.5 * mbias[...]
        act2, tanh2, scaled2 = half_silu(outer)
        for q in range(some):
            part = act2[q * chunk : (q + 1) * chunk, :]
            total[first + q : first + q + 1, :] += jnp.sum(part, axis=0, keepdims=True)
        slope2 = twice_slope(outer, tanh2, scaled2).astype(bf16)
        grad = jnp.dot(slope2, back[...], preferred_element_type=f32)
        grad = grad * twice_slope(half, tanh, scaled)
        for q in range(some):
            grads[0, first + q] = grad[q * chunk : (q + 1) * chunk, :].astype(bf16)

    @pl.when(step == groups - 1)
    def _():
        scores = jnp.sum(total[...] * weight[...], axis=1, keepdims=True)
        lane = lax.broadcasted_iota(jnp.int32, (configs, 128), 1)
        sub = lax.broadcasted_iota(jnp.int32, (configs, 128), 0)
        spread = jnp.where(lane == sub + where[0] * configs, scores, 0.0)
        sent[...] = jnp.broadcast_to(jnp.sum(spread, axis=0, keepdims=True), sent.shape)


def scorer_of(order, where, xs, ids, join, table, jbias, mid, mbias, weight, devices):
    groups = len(xs)
    configs = ids.shape[0]
    chunk, width = xs[0].shape
    whole = lambda i, *_: (0, 0)
    hidden = join.shape[1]
    return pl.pallas_call(
        functools.partial(scorer_kernel, groups),
        out_shape=(
            jax.ShapeDtypeStruct((groups, configs, chunk, hidden), bf16),
            jax.ShapeDtypeStruct((devices, 128), f32),
        ),
        grid_spec=pltpu.PrefetchScalarGridSpec(
            num_scalar_prefetch=2,
            grid=(groups,),
            in_specs=[VMEM] * groups
            + [pl.BlockSpec((configs, chunk), lambda i, order, where: (0, order[i]))]
            + [VMEM] * 6,
            out_specs=(
                pl.BlockSpec((1, configs, chunk, hidden), lambda i, *_: (i, 0, 0, 0)),
                pl.BlockSpec((devices, 128), whole),
            ),
            scratch_shapes=[
                pltpu.VMEM((groups, chunk, hidden), f32),
                pltpu.VMEM(table.shape, bf16),
                pltpu.VMEM(mid.shape, bf16),
                pltpu.VMEM(mid.shape, bf16),
                pltpu.VMEM((configs, hidden), f32),
            ],
        ),
        cost_estimate=pl.CostEstimate(
            flops=6 * groups * configs * chunk * width * width,
            transcendentals=2 * groups * configs * chunk * width,
            bytes_accessed=10 << 20,
        ),
        compiler_params=pltpu.CompilerParams(vmem_limit_bytes=24 << 20),
        name="scorer",
    )(order, where, *xs, ids, join, table, jbias, mid, mbias, weight)


def weighted(coef, grads, configs):
    rows = grads[0, 0].astype(f32) * coef[0:1, :]
    for k in range(1, configs):
        rows = rows + grads[0, k].astype(f32) * coef[k : k + 1, :]
    return rows


def ranking_kernel(scale, where, got, pairs, grads, loss, coef, out):
    configs = coef.shape[0]

    @pl.when(pl.program_id(0) == 0)
    def _():
        score = jnp.sum(got[...], axis=0, keepdims=True) * scale
        count = pairs.shape[0]
        lane = lax.broadcasted_iota(jnp.int32, (count, 128), 1)
        second = jnp.where(pairs[:, 1:2] == lane, 1.0, 0.0)
        signed = second - jnp.where(pairs[:, 0:1] == lane, 1.0, 0.0)
        gap = jnp.sum(signed * score, axis=1, keepdims=True)
        fade = jnp.exp(-jnp.abs(gap))
        soft = jnp.maximum(gap, 0.0) + jnp.log1p(fade)
        loss[...] = jnp.sum(soft, axis=0, keepdims=True) * (1.0 / count)
        slope = jnp.where(gap >= 0.0, 1.0, fade) / (1.0 + fade)
        grad = jnp.sum(slope * signed, axis=0, keepdims=True) * (65536.0 / count)
        lanes = lax.broadcasted_iota(jnp.int32, (configs, 128), 1)
        subs = lax.broadcasted_iota(jnp.int32, (configs, 128), 0)
        mine = jnp.where(lanes == subs + where[0] * configs, grad * scale, 0.0)
        own = jnp.sum(mine, axis=1, keepdims=True)
        coef[...] = jnp.broadcast_to(own, coef.shape)

    out[0] = weighted(coef, grads, configs).astype(bf16)


def ranking_of(scale, where, got, pairs, grads, first):
    groups, configs, chunk, hidden = grads.shape
    half = groups // 2
    return pl.pallas_call(
        functools.partial(ranking_kernel, scale),
        out_shape=(
            jax.ShapeDtypeStruct((1, 1), f32),
            jax.ShapeDtypeStruct((configs, hidden), f32),
            jax.ShapeDtypeStruct((half, chunk, hidden), bf16),
        ),
        grid=(half,),
        in_specs=[
            SMEM,
            VMEM,
            VMEM,
            pl.BlockSpec(
                (1, configs, chunk, hidden), lambda d: (first + (half - d) % half, 0, 0, 0)
            ),
        ],
        out_specs=(
            pl.BlockSpec((1, 1), lambda d: (0, 0)),
            pl.BlockSpec((configs, hidden), lambda d: (0, 0)),
            pl.BlockSpec((1, chunk, hidden), lambda d: (d, 0, 0)),
        ),
        cost_estimate=pl.CostEstimate(flops=1 << 24, transcendentals=0, bytes_accessed=6 << 20),
        name="ranking",
    )(where, got, pairs, grads)


def rest_kernel(coef, grads, out):
    out[0] = weighted(coef, grads, coef.shape[0]).astype(bf16)


def rest_of(coef, grads, first):
    groups, configs, chunk, hidden = grads.shape
    half = groups // 2
    return pl.pallas_call(
        rest_kernel,
        out_shape=jax.ShapeDtypeStruct((half, chunk, hidden), bf16),
        grid=(half,),
        in_specs=[
            VMEM,
            pl.BlockSpec(
                (1, configs, chunk, hidden), lambda d: (first + (half - d) % half, 0, 0, 0)
            ),
        ],
        out_specs=pl.BlockSpec((1, chunk, hidden), lambda d: (d, 0, 0)),
        cost_estimate=pl.CostEstimate(flops=1 << 24, transcendentals=0, bytes_accessed=6 << 20),
        name="rest",
    )(coef, grads)


def shards(
    node_feats,
    neighbors,
    self_weight,
    neighbor_weight,
    sage_bias,
    conf_index,
    layout_ids,
    join_weight,
    layout_table,
    join_bias,
    mid_weight,
    mid_bias,
    score_weight,
    config_pairs,
):
    both = ("cfg", "node")
    devices = lax.axis_size(both)
    node_count = lax.axis_size("node")
    group_count = lax.axis_size("cfg")
    rings = group_count // 2
    local_conf = conf_index.shape[0]
    width = node_feats.shape[1]
    per_peer = local_conf // node_count
    scale = 1.0 / math.sqrt(layout_ids.shape[1] * node_count)
    group = lax.axis_index("cfg")

    up = [(i, i + 1) for i in range(devices - 1)]
    down = [(i + 1, i) for i in range(devices - 1)]
    before = lax.ppermute(node_feats[-HALO:], both, up)
    after = lax.ppermute(node_feats[:HALO], both, down)
    nbrs = neighbors.T.reshape(-1)
    bias = sage_bias.reshape(1, -1)

    conf_src = conf_rows_of(
        nbrs, conf_index, before, node_feats, after, self_weight, neighbor_weight, bias
    )
    node_embed = layer_of(nbrs, before, node_feats, after, self_weight, neighbor_weight, bias)

    swap = [(i, i ^ 1) for i in range(group_count)]

    def shift(value, by):
        perm = [(i, (i // 2 + by) % rings * 2 + i % 2) for i in range(group_count)]
        return lax.ppermute(value, "cfg", perm)

    mine = lax.all_to_all(
        conf_src.reshape(node_count, per_peer, width), "node", 0, 0, tiled=True
    ).reshape(local_conf, width)
    xs = [mine] + [shift(mine, by) for by in range(1, rings)]
    xs = xs + [lax.ppermute(x, "cfg", swap) for x in xs]
    ring, core = group // 2, group % 2
    turns = jnp.arange(group_count, dtype=jnp.int32)
    order = (ring + rings - turns % rings) % rings * 2 + (core + turns // rings) % 2
    where = group.reshape(1)

    grads, sent = scorer_of(
        order,
        where,
        xs,
        layout_ids,
        join_weight,
        layout_table,
        join_bias.reshape(1, -1),
        mid_weight,
        mid_bias.reshape(1, -1),
        score_weight.reshape(1, -1),
        devices,
    )
    got = lax.all_to_all(sent.reshape(devices, 1, 128), both, 0, 0, tiled=True)
    loss, coef, away = ranking_of(
        scale, where, got.reshape(devices, 128), config_pairs, grads, rings
    )
    came = lax.ppermute(away, "cfg", swap)
    kept = rest_of(coef, grads, 0)
    sums = [kept[d].astype(f32) + came[d].astype(f32) for d in range(rings)]
    arrived = [shift(sums[d].astype(bf16), d) for d in range(1, rings)]
    row_grad = sums[0]
    for part in arrived:
        row_grad = row_grad + part.astype(f32)
    local_grad = lax.dot_general(
        row_grad.astype(bf16),
        join_weight,
        (((1,), (1,)), ((), ())),
        preferred_element_type=f32,
    )
    conf_grad = lax.all_to_all(
        local_grad.astype(bf16).reshape(node_count, per_peer, width), "node", 0, 0, tiled=True
    )
    conf_grad = conf_grad.astype(f32).reshape(local_conf, width)
    return (node_embed, loss.reshape(()), conf_grad)


def solution(mesh):
    split = P(("cfg", "node"), None)
    placed = (split, split, P(), P(), P(), P(("cfg", "node")), P("cfg", "node")) + (P(),) * 7
    return jax.shard_map(
        shards,
        mesh=mesh,
        in_specs=placed,
        out_specs=(split, P(), split),
        check_vma=False,
    )
```

```python
import functools
import math

import jax
import jax.numpy as jnp
from jax import lax
from jax.experimental import pallas as pl
from jax.experimental.pallas import tpu as pltpu
from jax.sharding import PartitionSpec as P

HALO = 512
f32 = jnp.float32
bf16 = jnp.bfloat16
VMEM = pl.BlockSpec(memory_space=pltpu.VMEM)
SMEM = pl.BlockSpec(memory_space=pltpu.SMEM)
HBM = pl.BlockSpec(memory_space=pltpu.HBM)


def in_hbm(value):
    return pltpu.with_memory_space_constraint(value, pltpu.HBM)


def half_silu(half):
    tanh = jnp.tanh(half)
    scaled = half * tanh
    return half + scaled, tanh, scaled


def twice_slope(half, tanh, scaled):
    inner = 1.0 + half - scaled
    return inner + tanh * inner


def put_rows(table, first, source):
    rows = source.shape[0]
    value = source[...].astype(f32)
    table[pl.ds(2 * first, rows, stride=2), :] = value[:, :128]
    table[pl.ds(2 * first + 1, rows, stride=2), :] = value[:, 128:]


def pair_at(table, at):
    return table[pl.ds(pl.multiple_of(at, 2), 2), :]


def table_kernel(feats, table):
    rows = feats.shape[0]
    put_rows(table, HALO + pl.multiple_of(pl.program_id(0) * rows, rows), feats)


def table_of(feats):
    nodes, width = feats.shape
    tile = 512
    return pl.pallas_call(
        table_kernel,
        out_shape=jax.ShapeDtypeStruct((2 * (nodes + 2 * HALO), 128), f32),
        grid=(nodes // tile,),
        in_specs=[pl.BlockSpec((tile, width), lambda i: (i, 0))],
        out_specs=VMEM,
        cost_estimate=pl.CostEstimate(flops=1 << 20, transcendentals=0, bytes_accessed=6 << 20),
        compiler_params=pltpu.CompilerParams(vmem_limit_bytes=16 << 20),
        name="window_rows",
    )(feats)


def layer_rows(own_left, own_right, left, right, sw, nw, bias):
    pre = jnp.dot(own_left, sw[:128, :], preferred_element_type=f32)
    pre += jnp.dot(own_right, sw[128:, :], preferred_element_type=f32)
    pre += jnp.dot(left, nw[:128, :], preferred_element_type=f32)
    pre += jnp.dot(right, nw[128:, :], preferred_element_type=f32)
    return half_silu(0.5 * (pre + bias[...]))[0].astype(bf16)


def conf_kernel(
    nbrs, picks, before, after, sw_hbm, nw_hbm, bias_hbm, given, out, table, own, acc, sw, nw, bias, sems
):
    copies = [
        pltpu.make_async_copy(source, target, sems.at[i])
        for i, (source, target) in enumerate(((sw_hbm, sw), (nw_hbm, nw), (bias_hbm, bias)))
    ]
    for copy in copies:
        copy.start()
    window = table.shape[0] // 2
    put_rows(table, 0, before)
    put_rows(table, window - HALO, after)
    count = picks.shape[0]
    own3 = own.reshape(count, 2, 128)
    acc3 = acc.reshape(count, 2, 128)

    def body(block, carry):
        values = []
        for j in range(8):
            g = picks[block * 8 + j]
            at = (g >> 7) * 512 + (g & 127)
            near = [pair_at(table, nbrs[at + 128 * k]) for k in range(4)]
            values.append((pair_at(table, 2 * (HALO + g)), (near[0] + near[1]) + (near[2] + near[3])))
        for j in range(8):
            own3[block * 8 + j], acc3[block * 8 + j] = values[j]
        return carry

    lax.fori_loop(0, count // 8, body, 0)
    halves = [ref[pl.ds(side, count, stride=2), :] for ref in (own, acc) for side in (0, 1)]
    for copy in copies:
        copy.wait()
    out[...] = layer_rows(
        halves[0].astype(bf16),
        halves[1].astype(bf16),
        (halves[2] * 0.25).astype(bf16),
        (halves[3] * 0.25).astype(bf16),
        sw,
        nw,
        bias,
    )


def conf_rows_of(nbrs, picks, before, after, sw, nw, bias, table):
    count = picks.shape[0]
    width = before.shape[1]
    return pl.pallas_call(
        conf_kernel,
        out_shape=(
            jax.ShapeDtypeStruct((count, width), bf16),
            jax.ShapeDtypeStruct(table.shape, f32),
        ),
        in_specs=[SMEM, SMEM, VMEM, VMEM] + [HBM] * 3 + [VMEM],
        out_specs=(VMEM, VMEM),
        input_output_aliases={7: 1},
        scratch_shapes=[
            pltpu.VMEM((2 * count, 128), f32),
            pltpu.VMEM((2 * count, 128), f32),
            pltpu.VMEM(sw.shape, bf16),
            pltpu.VMEM(nw.shape, bf16),
            pltpu.VMEM(bias.shape, f32),
            pltpu.SemaphoreType.DMA((3,)),
        ],
        cost_estimate=pl.CostEstimate(
            flops=4 * count * width * width, transcendentals=0, bytes_accessed=6 << 20
        ),
        compiler_params=pltpu.CompilerParams(vmem_limit_bytes=16 << 20),
        name="conf_rows",
    )(nbrs, picks, before, after, in_hbm(sw), in_hbm(nw), in_hbm(bias), table)


def layer_kernel(nbrs, before, feats, after, own, sw, nw, bias, *refs):
    out, table, acc = refs[-3:]
    tile = own.shape[0]
    nodes = feats.shape[0]

    @pl.when(pl.program_id(0) == 0)
    def _():
        put_rows(table, 0, before)
        for start in range(0, nodes, 512):
            put_rows(table, HALO + start, feats.at[start : start + 512, :])
        put_rows(table, HALO + nodes, after)

    acc3 = acc.reshape(tile, 2, 128)

    def body(block, carry):
        values = []
        for j in range(128):
            near = [pair_at(table, nbrs[block * 512 + (128 * k + j)]) for k in range(4)]
            values.append((near[0] + near[1]) + (near[2] + near[3]))
        for j in range(128):
            acc3[block * 128 + j] = values[j]
        return carry

    lax.fori_loop(0, tile // 128, body, 0)
    rows = own[...]
    out[...] = layer_rows(
        rows[:, :128],
        rows[:, 128:],
        (acc[pl.ds(0, tile, stride=2), :] * 0.25).astype(bf16),
        (acc[pl.ds(1, tile, stride=2), :] * 0.25).astype(bf16),
        sw,
        nw,
        bias,
    )


def layer_of(first, steps, nbrs, before, feats, after, sw, nw, bias, given):
    nodes, width = feats.shape
    tile = 1024
    ahead = [] if given is None else [given]
    return pl.pallas_call(
        layer_kernel,
        out_shape=jax.ShapeDtypeStruct((nodes, width), bf16),
        grid=(steps,),
        in_specs=[
            pl.BlockSpec((4 * tile,), lambda i: (first + i,), memory_space=pltpu.SMEM),
            VMEM,
            VMEM,
            VMEM,
            pl.BlockSpec((tile, width), lambda i: (first + i, 0)),
            VMEM,
            VMEM,
            VMEM,
        ]
        + [HBM] * len(ahead),
        out_specs=pl.BlockSpec((tile, width), lambda i: (first + i, 0)),
        input_output_aliases={8: 0} if ahead else {},
        scratch_shapes=[
            pltpu.VMEM((2 * (nodes + 2 * HALO), 128), f32),
            pltpu.VMEM((2 * tile, 128), f32),
        ],
        cost_estimate=pl.CostEstimate(
            flops=steps * 4 * tile * width * width, transcendentals=0, bytes_accessed=steps << 23
        ),
        compiler_params=pltpu.CompilerParams(vmem_limit_bytes=24 << 20),
        name="graph_layer",
    )(nbrs, before, feats, after, feats, sw, nw, bias, *ahead)


def place_of(group, turn):
    return (((group >> 1) + 4 - (turn & 3)) & 3) * 2 + ((group ^ (turn >> 2)) & 1)


def scorer_kernel(groups, where, *refs):
    xs, refs = refs[:groups], refs[groups:]
    ids, join, table, jbias, mid, mbias, weight, grads_hbm, sent = refs[:9]
    base, tabh, midh, back, total, grads, sems = refs[9:]
    step = pl.program_id(0)
    slot = step & 1
    chunk = xs[0].shape[0]
    configs = ids.shape[0]
    layouts = table.shape[0]
    one = jnp.asarray(1.0, bf16)

    @pl.when(step == 0)
    def _():
        for i in range(groups):
            base[i] = 0.5 * (
                jnp.dot(xs[i][...], join[...], preferred_element_type=f32) + jbias[...]
            )
        tabh[...] = (table[...].astype(f32) * 0.5).astype(bf16)
        middle = mid[...].astype(f32)
        midh[...] = (middle * 0.5).astype(bf16)
        back[...] = jnp.transpose(middle * (weight[...] * 0.25)).astype(bf16)
        total[...] = jnp.zeros_like(total)

    def copy_of(turn, place):
        return pltpu.make_async_copy(grads.at[place], grads_hbm.at[turn], sems.at[place])

    @pl.when(step >= 2)
    def _():
        copy_of(step - 2, slot).wait()

    columns = jnp.transpose(ids[...].astype(f32))
    lanes = lax.broadcasted_iota(jnp.int32, (chunk, layouts), 1).astype(f32)
    rows = base[step]
    some = 8
    for first in range(0, configs, some):
        picks = jnp.concatenate(
            [
                jnp.where(columns[:, k : k + 1] == lanes, 1.0, 0.0).astype(bf16)
                for k in range(first, first + some)
            ],
            axis=0,
        )
        half = jnp.dot(picks, tabh[...], preferred_element_type=f32)
        half = (half + jnp.concatenate([rows] * some, axis=0)).astype(bf16)
        tanh = jnp.tanh(half)
        act = half + half * tanh
        slope = (one + tanh) * (one + half * (one - tanh))
        outer = jnp.dot(act, midh[...], preferred_element_type=f32)
        outer = (outer + 0.5 * mbias[...]).astype(bf16)
        tanh2 = jnp.tanh(outer)
        act2 = (outer + outer * tanh2).astype(f32)
        slope2 = (one + tanh2) * (one + outer * (one - tanh2))
        for q in range(some):
            part = act2[q * chunk : (q + 1) * chunk, :]
            total[first + q : first + q + 1, :] += jnp.sum(part, axis=0, keepdims=True)
        grad = jnp.dot(slope2, back[...], preferred_element_type=f32).astype(bf16) * slope
        for q in range(some):
            grads[slot, first + q] = grad[q * chunk : (q + 1) * chunk, :]

    copy_of(step, slot).start()

    @pl.when(step == groups - 1)
    def _():
        scores = jnp.sum(total[...] * weight[...], axis=1, keepdims=True)
        lane = lax.broadcasted_iota(jnp.int32, (configs, 128), 1)
        sub = lax.broadcasted_iota(jnp.int32, (configs, 128), 0)
        spread = jnp.where(lane == sub + where[0] * configs, scores, 0.0)
        sent[...] = jnp.broadcast_to(jnp.sum(spread, axis=0, keepdims=True), sent.shape)
        copy_of(step - 1, 1 - slot).wait()
        copy_of(step, slot).wait()


def scorer_of(where, xs, ids, join, table, jbias, mid, mbias, weight, devices):
    groups = len(xs)
    configs = ids.shape[0]
    chunk, width = xs[0].shape
    hidden = join.shape[1]
    return pl.pallas_call(
        functools.partial(scorer_kernel, groups),
        out_shape=(
            pltpu.HBM((groups, configs, chunk, hidden), bf16),
            jax.ShapeDtypeStruct((devices, 128), f32),
        ),
        grid_spec=pltpu.PrefetchScalarGridSpec(
            num_scalar_prefetch=1,
            grid=(groups,),
            in_specs=[VMEM] * groups
            + [pl.BlockSpec((configs, chunk), lambda i, where: (0, place_of(where[0], i)))]
            + [VMEM] * 6,
            out_specs=(HBM, VMEM),
            scratch_shapes=[
                pltpu.VMEM((groups, chunk, hidden), f32),
                pltpu.VMEM(table.shape, bf16),
                pltpu.VMEM(mid.shape, bf16),
                pltpu.VMEM(mid.shape, bf16),
                pltpu.VMEM((configs, hidden), f32),
                pltpu.VMEM((2, configs, chunk, hidden), bf16),
                pltpu.SemaphoreType.DMA((2,)),
            ],
        ),
        cost_estimate=pl.CostEstimate(
            flops=6 * groups * configs * chunk * width * width,
            transcendentals=2 * groups * configs * chunk * width,
            bytes_accessed=10 << 20,
        ),
        compiler_params=pltpu.CompilerParams(vmem_limit_bytes=30 << 20),
        name="scorer",
    )(where, *xs, ids, join, table, jbias, mid, mbias, weight)


def weighted(coef, grads, out):
    configs, chunk, hidden = grads.shape
    some = 32
    for start in range(0, chunk, some):
        rows = grads[0, start : start + some, :].astype(f32) * coef[0:1, :]
        for k in range(1, configs):
            rows = rows + grads[k, start : start + some, :].astype(f32) * coef[k : k + 1, :]
        out[start : start + some, :] = rows.astype(bf16)


def fetches(grads_hbm, grads, sems, first):
    half = grads.shape[0]
    return [
        pltpu.make_async_copy(
            grads_hbm.at[first + (half - d) % half], grads.at[d], sems.at[d]
        )
        for d in range(half)
    ]


def ranking_kernel(scale, where, got, pairs, grads_hbm, loss, coef, out, column, grads, sems):
    half, configs, chunk, hidden = grads.shape
    copies = fetches(grads_hbm, grads, sems, half)
    for copy in copies:
        copy.start()
    score = jnp.sum(got[...], axis=0, keepdims=True) * scale
    lane = lax.broadcasted_iota(jnp.int32, (128, 128), 1)
    sub = lax.broadcasted_iota(jnp.int32, (128, 128), 0)
    score = jnp.sum(jnp.where(lane == sub, score, 0.0), axis=1, keepdims=True)
    count = pairs.shape[1]
    ids = lax.broadcasted_iota(jnp.int32, (128, count), 0)
    second = jnp.where(pairs[1:2, :] == ids, 1.0, 0.0)
    signed = second - jnp.where(pairs[0:1, :] == ids, 1.0, 0.0)
    gap = jnp.sum(signed * score, axis=0, keepdims=True)
    fade = jnp.exp(-jnp.abs(gap))
    soft = jnp.maximum(gap, 0.0) + jnp.log1p(fade)
    loss[...] = jnp.sum(soft, axis=1, keepdims=True) * (1.0 / count)
    slope = jnp.where(gap >= 0.0, 1.0, fade) / (1.0 + fade)
    grad = jnp.sum(slope * signed, axis=1, keepdims=True) * (65536.0 * scale / count)
    column[...] = jnp.broadcast_to(grad, column.shape)
    coef[...] = column[pl.ds(pl.multiple_of(where[0] * configs, configs), configs), :]
    for d in range(half):
        copies[d].wait()
        weighted(coef, grads.at[d], out.at[d])


def ranking_of(scale, where, got, pairs, grads):
    groups, configs, chunk, hidden = grads.shape
    half = groups // 2
    return pl.pallas_call(
        functools.partial(ranking_kernel, scale),
        out_shape=(
            jax.ShapeDtypeStruct((1, 1), f32),
            jax.ShapeDtypeStruct((configs, hidden), f32),
            jax.ShapeDtypeStruct((half, chunk, hidden), bf16),
        ),
        in_specs=[SMEM, VMEM, VMEM, HBM],
        out_specs=(VMEM, VMEM, VMEM),
        scratch_shapes=[
            pltpu.VMEM((128, hidden), f32),
            pltpu.VMEM((half, configs, chunk, hidden), bf16),
            pltpu.SemaphoreType.DMA((half,)),
        ],
        cost_estimate=pl.CostEstimate(flops=1 << 24, transcendentals=0, bytes_accessed=6 << 20),
        compiler_params=pltpu.CompilerParams(vmem_limit_bytes=16 << 20),
        name="ranking",
    )(where, got, pairs, in_hbm(grads))


def rest_kernel(coef, grads_hbm, out, grads, sems):
    copies = fetches(grads_hbm, grads, sems, 0)
    for copy in copies:
        copy.start()
    for d, copy in enumerate(copies):
        copy.wait()
        weighted(coef, grads.at[d], out.at[d])


def rest_of(coef, grads):
    groups, configs, chunk, hidden = grads.shape
    half = groups // 2
    return pl.pallas_call(
        rest_kernel,
        out_shape=jax.ShapeDtypeStruct((half, chunk, hidden), bf16),
        in_specs=[VMEM, HBM],
        out_specs=VMEM,
        scratch_shapes=[
            pltpu.VMEM((half, configs, chunk, hidden), bf16),
            pltpu.SemaphoreType.DMA((half,)),
        ],
        cost_estimate=pl.CostEstimate(flops=1 << 24, transcendentals=0, bytes_accessed=6 << 20),
        compiler_params=pltpu.CompilerParams(vmem_limit_bytes=16 << 20),
        name="rest",
    )(coef, in_hbm(grads))


def shards(
    node_feats,
    neighbors,
    self_weight,
    neighbor_weight,
    sage_bias,
    conf_index,
    layout_ids,
    join_weight,
    layout_table,
    join_bias,
    mid_weight,
    mid_bias,
    score_weight,
    config_pairs,
):
    both = ("cfg", "node")
    devices = lax.axis_size(both)
    node_count = lax.axis_size("node")
    group_count = lax.axis_size("cfg")
    rings = group_count // 2
    local_conf = conf_index.shape[0]
    width = node_feats.shape[1]
    per_peer = local_conf // node_count
    scale = 1.0 / math.sqrt(layout_ids.shape[1] * node_count)
    group = lax.axis_index("cfg")

    up = [(i, i + 1) for i in range(devices - 1)]
    down = [(i + 1, i) for i in range(devices - 1)]
    before = lax.ppermute(node_feats[-HALO:], both, up)
    after = lax.ppermute(node_feats[:HALO], both, down)
    nodes, near = neighbors.shape
    nbrs = (2 * neighbors).T.reshape(near, nodes // 128, 128).transpose(1, 0, 2).reshape(-1)
    bias = sage_bias.reshape(1, -1)
    hold = lax.optimization_barrier

    table = table_of(node_feats)
    conf_src, _ = conf_rows_of(
        nbrs, conf_index, before, after, self_weight, neighbor_weight, bias, table
    )

    def layer(first, steps, given):
        return layer_of(
            first,
            steps,
            nbrs,
            before,
            node_feats,
            after,
            self_weight,
            neighbor_weight,
            bias,
            given,
        )

    swap = [(i, i ^ 1) for i in range(group_count)]

    def shift(value, by):
        perm = [(i, (i // 2 + by) % rings * 2 + i % 2) for i in range(group_count)]
        return lax.ppermute(value, "cfg", perm)

    mine = lax.all_to_all(
        conf_src.reshape(node_count, per_peer, width), "node", 0, 0, tiled=True
    )
    embed = layer(0, 1, None)
    mine, embed = hold((mine, embed))
    mine = mine.reshape(local_conf, width)
    xs = [mine] + [shift(mine, by) for by in range(1, rings)]
    xs = xs + [lax.ppermute(x, "cfg", swap) for x in xs]
    where = group.reshape(1)

    grads, sent = scorer_of(
        where,
        xs,
        layout_ids,
        join_weight,
        layout_table,
        join_bias.reshape(1, -1),
        mid_weight,
        mid_bias.reshape(1, -1),
        score_weight.reshape(1, -1),
        devices,
    )
    sent, embed = hold((sent, embed))
    got = lax.all_to_all(sent.reshape(devices, 1, 128), both, 0, 0, tiled=True)
    embed = layer(1, 1, embed)
    got, embed = hold((got, embed))
    loss, coef, away = ranking_of(scale, where, got.reshape(devices, 128), config_pairs.T, grads)
    came = lax.ppermute(away, "cfg", swap)
    kept = rest_of(coef, grads)
    sums = [kept[d].astype(f32) + came[d].astype(f32) for d in range(rings)]
    arrived = [shift(sums[d].astype(bf16), d) for d in range(1, rings)]
    row_grad = sums[0]
    for part in arrived:
        row_grad = row_grad + part.astype(f32)
    local_grad = lax.dot_general(
        row_grad.astype(bf16),
        join_weight,
        (((1,), (1,)), ((), ())),
        preferred_element_type=f32,
    )
    local_grad, embed = hold((local_grad.astype(bf16), embed))
    conf_grad = lax.all_to_all(
        local_grad.reshape(node_count, per_peer, width), "node", 0, 0, tiled=True
    )
    embed = layer(2, 2, embed)
    conf_grad = conf_grad.astype(f32).reshape(local_conf, width)
    return (embed, loss.reshape(()), conf_grad)


def solution(mesh):
    split = P(("cfg", "node"), None)
    placed = (split, split, P(), P(), P(), P(("cfg", "node")), P("cfg", "node")) + (P(),) * 7
    return jax.shard_map(
        shards,
        mesh=mesh,
        in_specs=placed,
        out_specs=(split, P(), split),
        check_vma=False,
    )
```

```python
import functools
import math

import jax
import jax.numpy as jnp
from jax import lax
from jax.experimental import pallas as pl
from jax.experimental.pallas import tpu as pltpu
from jax.sharding import PartitionSpec as P

HALO = 512
f32 = jnp.float32
bf16 = jnp.bfloat16
VMEM = pl.BlockSpec(memory_space=pltpu.VMEM)
SMEM = pl.BlockSpec(memory_space=pltpu.SMEM)
HBM = pl.BlockSpec(memory_space=pltpu.HBM)


def in_hbm(value):
    return pltpu.with_memory_space_constraint(value, pltpu.HBM)


def half_silu(half):
    tanh = jnp.tanh(half)
    scaled = half * tanh
    return half + scaled, tanh, scaled


def twice_slope(half, tanh, scaled):
    inner = 1.0 + half - scaled
    return inner + tanh * inner


def put_rows(table, first, source):
    rows = source.shape[0]
    value = source[...].astype(f32)
    table[pl.ds(2 * first, rows, stride=2), :] = value[:, :128]
    table[pl.ds(2 * first + 1, rows, stride=2), :] = value[:, 128:]


def put_halo(table, spot, peers, near, far):
    before, after = near
    first, last = far
    end = table.shape[0] // 2 - HALO

    @pl.when(spot[0] == 0)
    def _():
        put_rows(table, 0, first)

    @pl.when(spot[0] != 0)
    def _():
        put_rows(table, 0, before)

    @pl.when(spot[0] == peers - 1)
    def _():
        put_rows(table, end, last)

    @pl.when(spot[0] != peers - 1)
    def _():
        put_rows(table, end, after)


def pair_at(table, at):
    return table[pl.ds(pl.multiple_of(at, 2), 2), :]


def table_kernel(feats, table):
    rows = feats.shape[0]
    put_rows(table, HALO + pl.multiple_of(pl.program_id(0) * rows, rows), feats)


def table_of(feats):
    nodes, width = feats.shape
    tile = 512
    return pl.pallas_call(
        table_kernel,
        out_shape=jax.ShapeDtypeStruct((2 * (nodes + 2 * HALO), 128), f32),
        grid=(nodes // tile,),
        in_specs=[pl.BlockSpec((tile, width), lambda i: (i, 0))],
        out_specs=VMEM,
        cost_estimate=pl.CostEstimate(flops=1 << 20, transcendentals=0, bytes_accessed=6 << 20),
        compiler_params=pltpu.CompilerParams(vmem_limit_bytes=16 << 20),
        name="window_rows",
    )(feats)


def layer_rows(own_left, own_right, left, right, sw, nw, bias):
    pre = jnp.dot(own_left, sw[:128, :], preferred_element_type=f32)
    pre += jnp.dot(own_right, sw[128:, :], preferred_element_type=f32)
    pre += jnp.dot(left, nw[:128, :], preferred_element_type=f32)
    pre += jnp.dot(right, nw[128:, :], preferred_element_type=f32)
    return half_silu(0.5 * (pre + bias[...]))[0].astype(bf16)


def conf_kernel(peers, spot, nbrs, picks, *refs):
    near, far, refs = refs[:2], refs[2:4], refs[4:]
    sw_hbm, nw_hbm, bias_hbm, given, out, table, own, acc, sw, nw, bias, sems = refs
    copies = [
        pltpu.make_async_copy(source, target, sems.at[i])
        for i, (source, target) in enumerate(((sw_hbm, sw), (nw_hbm, nw), (bias_hbm, bias)))
    ]
    for copy in copies:
        copy.start()
    put_halo(table, spot, peers, near, far)
    count = picks.shape[0]
    own3 = own.reshape(count, 2, 128)
    acc3 = acc.reshape(count, 2, 128)

    def body(block, carry):
        values = []
        for j in range(8):
            g = picks[block * 8 + j]
            at = (g >> 7) * 512 + (g & 127)
            near = [pair_at(table, nbrs[at + 128 * k]) for k in range(4)]
            values.append((pair_at(table, 2 * (HALO + g)), (near[0] + near[1]) + (near[2] + near[3])))
        for j in range(8):
            own3[block * 8 + j], acc3[block * 8 + j] = values[j]
        return carry

    lax.fori_loop(0, count // 8, body, 0)
    halves = [ref[pl.ds(side, count, stride=2), :] for ref in (own, acc) for side in (0, 1)]
    for copy in copies:
        copy.wait()
    out[...] = layer_rows(
        halves[0].astype(bf16),
        halves[1].astype(bf16),
        (halves[2] * 0.25).astype(bf16),
        (halves[3] * 0.25).astype(bf16),
        sw,
        nw,
        bias,
    )


def conf_rows_of(peers, spot, nbrs, picks, rims, sw, nw, bias, table):
    count = picks.shape[0]
    width = sw.shape[0]
    return pl.pallas_call(
        functools.partial(conf_kernel, peers),
        out_shape=(
            jax.ShapeDtypeStruct((count, width), bf16),
            jax.ShapeDtypeStruct(table.shape, f32),
        ),
        in_specs=[SMEM] * 3 + [VMEM] * 4 + [HBM] * 3 + [VMEM],
        out_specs=(VMEM, VMEM),
        input_output_aliases={10: 1},
        scratch_shapes=[
            pltpu.VMEM((2 * count, 128), f32),
            pltpu.VMEM((2 * count, 128), f32),
            pltpu.VMEM(sw.shape, bf16),
            pltpu.VMEM(nw.shape, bf16),
            pltpu.VMEM(bias.shape, f32),
            pltpu.SemaphoreType.DMA((3,)),
        ],
        cost_estimate=pl.CostEstimate(
            flops=4 * count * width * width, transcendentals=0, bytes_accessed=6 << 20
        ),
        compiler_params=pltpu.CompilerParams(vmem_limit_bytes=16 << 20),
        name="conf_rows",
    )(spot, nbrs, picks, *rims, in_hbm(sw), in_hbm(nw), in_hbm(bias), table)


def layer_kernel(peers, spot, nbrs, *refs):
    near, far, (feats, own, sw, nw, bias) = refs[:2], refs[2:4], refs[4:9]
    out, table, acc = refs[-3:]
    tile = own.shape[0]
    nodes = feats.shape[0]

    @pl.when(pl.program_id(0) == 0)
    def _():
        put_halo(table, spot, peers, near, far)
        for start in range(0, nodes, 512):
            put_rows(table, HALO + start, feats.at[start : start + 512, :])

    acc3 = acc.reshape(tile, 2, 128)

    def body(block, carry):
        values = []
        for j in range(128):
            near = [pair_at(table, nbrs[block * 512 + (128 * k + j)]) for k in range(4)]
            values.append((near[0] + near[1]) + (near[2] + near[3]))
        for j in range(128):
            acc3[block * 128 + j] = values[j]
        return carry

    lax.fori_loop(0, tile // 128, body, 0)
    rows = own[...]
    out[...] = layer_rows(
        rows[:, :128],
        rows[:, 128:],
        (acc[pl.ds(0, tile, stride=2), :] * 0.25).astype(bf16),
        (acc[pl.ds(1, tile, stride=2), :] * 0.25).astype(bf16),
        sw,
        nw,
        bias,
    )


def layer_of(first, steps, peers, spot, nbrs, rims, feats, sw, nw, bias, given):
    nodes, width = feats.shape
    tile = 1024
    ahead = [] if given is None else [given]
    return pl.pallas_call(
        functools.partial(layer_kernel, peers),
        out_shape=jax.ShapeDtypeStruct((nodes, width), bf16),
        grid=(steps,),
        in_specs=[
            SMEM,
            pl.BlockSpec((4 * tile,), lambda i: (first + i,), memory_space=pltpu.SMEM),
        ]
        + [VMEM] * 5
        + [
            pl.BlockSpec((tile, width), lambda i: (first + i, 0)),
            VMEM,
            VMEM,
            VMEM,
        ]
        + [HBM] * len(ahead),
        out_specs=pl.BlockSpec((tile, width), lambda i: (first + i, 0)),
        input_output_aliases={11: 0} if ahead else {},
        scratch_shapes=[
            pltpu.VMEM((2 * (nodes + 2 * HALO), 128), f32),
            pltpu.VMEM((2 * tile, 128), f32),
        ],
        cost_estimate=pl.CostEstimate(
            flops=steps * 4 * tile * width * width, transcendentals=0, bytes_accessed=steps << 23
        ),
        compiler_params=pltpu.CompilerParams(vmem_limit_bytes=24 << 20),
        name="graph_layer",
    )(spot, nbrs, *rims, feats, feats, sw, nw, bias, *ahead)


def place_of(group, turn):
    return (((group >> 1) + 4 - (turn & 3)) & 3) * 2 + ((group ^ (turn >> 2)) & 1)


def scorer_kernel(groups, where, *refs):
    xs, refs = refs[:groups], refs[groups:]
    ids, join, table, jbias, mid, mbias, weight, grads_hbm, sent = refs[:9]
    base, tabh, midh, back, total, grads, sems = refs[9:]
    step = pl.program_id(0)
    slot = step & 1
    chunk = xs[0].shape[0]
    configs = ids.shape[0]
    layouts = table.shape[0]
    one = jnp.asarray(1.0, bf16)

    @pl.when(step == 0)
    def _():
        for i in range(groups):
            base[i] = 0.5 * (
                jnp.dot(xs[i][...], join[...], preferred_element_type=f32) + jbias[...]
            )
        tabh[...] = (table[...].astype(f32) * 0.5).astype(bf16)
        middle = mid[...].astype(f32)
        midh[...] = (middle * 0.5).astype(bf16)
        back[...] = jnp.transpose(middle * (weight[...] * 0.25)).astype(bf16)
        total[...] = jnp.zeros_like(total)

    def copy_of(turn, place):
        return pltpu.make_async_copy(grads.at[place], grads_hbm.at[turn], sems.at[place])

    @pl.when(step >= 2)
    def _():
        copy_of(step - 2, slot).wait()

    columns = jnp.transpose(ids[...].astype(f32))
    lanes = lax.broadcasted_iota(jnp.int32, (chunk, layouts), 1).astype(f32)
    rows = base[step]
    some = 8
    for first in range(0, configs, some):
        picks = jnp.concatenate(
            [
                jnp.where(columns[:, k : k + 1] == lanes, 1.0, 0.0).astype(bf16)
                for k in range(first, first + some)
            ],
            axis=0,
        )
        half = jnp.dot(picks, tabh[...], preferred_element_type=f32)
        half = (half + jnp.concatenate([rows] * some, axis=0)).astype(bf16)
        tanh = jnp.tanh(half)
        act = half + half * tanh
        slope = (one + tanh) * (one + half * (one - tanh))
        outer = jnp.dot(act, midh[...], preferred_element_type=f32)
        outer = (outer + 0.5 * mbias[...]).astype(bf16)
        tanh2 = jnp.tanh(outer)
        act2 = (outer + outer * tanh2).astype(f32)
        slope2 = (one + tanh2) * (one + outer * (one - tanh2))
        for q in range(some):
            part = act2[q * chunk : (q + 1) * chunk, :]
            total[first + q : first + q + 1, :] += jnp.sum(part, axis=0, keepdims=True)
        grad = jnp.dot(slope2, back[...], preferred_element_type=f32).astype(bf16) * slope
        for q in range(some):
            grads[slot, first + q] = grad[q * chunk : (q + 1) * chunk, :]

    copy_of(step, slot).start()

    @pl.when(step == groups - 1)
    def _():
        scores = jnp.sum(total[...] * weight[...], axis=1, keepdims=True)
        lane = lax.broadcasted_iota(jnp.int32, (configs, 128), 1)
        sub = lax.broadcasted_iota(jnp.int32, (configs, 128), 0)
        spread = jnp.where(lane == sub + where[0] * configs, scores, 0.0)
        sent[...] = jnp.broadcast_to(jnp.sum(spread, axis=0, keepdims=True), sent.shape)
        copy_of(step - 1, 1 - slot).wait()
        copy_of(step, slot).wait()


def scorer_of(where, xs, ids, join, table, jbias, mid, mbias, weight, devices):
    groups = len(xs)
    configs = ids.shape[0]
    chunk, width = xs[0].shape
    hidden = join.shape[1]
    return pl.pallas_call(
        functools.partial(scorer_kernel, groups),
        out_shape=(
            pltpu.HBM((groups, configs, chunk, hidden), bf16),
            jax.ShapeDtypeStruct((devices, 128), f32),
        ),
        grid_spec=pltpu.PrefetchScalarGridSpec(
            num_scalar_prefetch=1,
            grid=(groups,),
            in_specs=[VMEM] * groups
            + [pl.BlockSpec((configs, chunk), lambda i, where: (0, place_of(where[0], i)))]
            + [VMEM] * 6,
            out_specs=(HBM, VMEM),
            scratch_shapes=[
                pltpu.VMEM((groups, chunk, hidden), f32),
                pltpu.VMEM(table.shape, bf16),
                pltpu.VMEM(mid.shape, bf16),
                pltpu.VMEM(mid.shape, bf16),
                pltpu.VMEM((configs, hidden), f32),
                pltpu.VMEM((2, configs, chunk, hidden), bf16),
                pltpu.SemaphoreType.DMA((2,)),
            ],
        ),
        cost_estimate=pl.CostEstimate(
            flops=6 * groups * configs * chunk * width * width,
            transcendentals=2 * groups * configs * chunk * width,
            bytes_accessed=10 << 20,
        ),
        compiler_params=pltpu.CompilerParams(vmem_limit_bytes=30 << 20),
        name="scorer",
    )(where, *xs, ids, join, table, jbias, mid, mbias, weight)


def weighted(coef, grads, out):
    configs, chunk, hidden = grads.shape
    some = 32
    for start in range(0, chunk, some):
        rows = grads[0, start : start + some, :].astype(f32) * coef[0:1, :]
        for k in range(1, configs):
            rows = rows + grads[k, start : start + some, :].astype(f32) * coef[k : k + 1, :]
        out[start : start + some, :] = rows.astype(bf16)


def fetches(grads_hbm, grads, sems, first):
    half = grads.shape[0]
    return [
        pltpu.make_async_copy(
            grads_hbm.at[first + (half - d) % half], grads.at[d], sems.at[d]
        )
        for d in range(half)
    ]


def ranking_kernel(scale, where, got, pairs, grads_hbm, loss, coef, out, column, grads, sems):
    half, configs, chunk, hidden = grads.shape
    copies = fetches(grads_hbm, grads, sems, half)
    for copy in copies:
        copy.start()
    score = jnp.sum(got[...], axis=0, keepdims=True) * scale
    lane = lax.broadcasted_iota(jnp.int32, (128, 128), 1)
    sub = lax.broadcasted_iota(jnp.int32, (128, 128), 0)
    score = jnp.sum(jnp.where(lane == sub, score, 0.0), axis=1, keepdims=True)
    count = pairs.shape[1]
    ids = lax.broadcasted_iota(jnp.int32, (128, count), 0)
    second = jnp.where(pairs[1:2, :] == ids, 1.0, 0.0)
    signed = second - jnp.where(pairs[0:1, :] == ids, 1.0, 0.0)
    gap = jnp.sum(signed * score, axis=0, keepdims=True)
    fade = jnp.exp(-jnp.abs(gap))
    soft = jnp.maximum(gap, 0.0) + jnp.log1p(fade)
    loss[...] = jnp.sum(soft, axis=1, keepdims=True) * (1.0 / count)
    slope = jnp.where(gap >= 0.0, 1.0, fade) / (1.0 + fade)
    grad = jnp.sum(slope * signed, axis=1, keepdims=True) * (65536.0 * scale / count)
    column[...] = jnp.broadcast_to(grad, column.shape)
    coef[...] = column[pl.ds(pl.multiple_of(where[0] * configs, configs), configs), :]
    for d in range(half):
        copies[d].wait()
        weighted(coef, grads.at[d], out.at[d])


def ranking_of(scale, where, got, pairs, grads):
    groups, configs, chunk, hidden = grads.shape
    half = groups // 2
    return pl.pallas_call(
        functools.partial(ranking_kernel, scale),
        out_shape=(
            jax.ShapeDtypeStruct((1, 1), f32),
            jax.ShapeDtypeStruct((configs, hidden), f32),
            jax.ShapeDtypeStruct((half, chunk, hidden), bf16),
        ),
        in_specs=[SMEM, VMEM, VMEM, HBM],
        out_specs=(VMEM, VMEM, VMEM),
        scratch_shapes=[
            pltpu.VMEM((128, hidden), f32),
            pltpu.VMEM((half, configs, chunk, hidden), bf16),
            pltpu.SemaphoreType.DMA((half,)),
        ],
        cost_estimate=pl.CostEstimate(flops=1 << 24, transcendentals=0, bytes_accessed=6 << 20),
        compiler_params=pltpu.CompilerParams(vmem_limit_bytes=16 << 20),
        name="ranking",
    )(where, got, pairs, in_hbm(grads))


def rest_kernel(coef, grads_hbm, out, grads, sems):
    copies = fetches(grads_hbm, grads, sems, 0)
    for copy in copies:
        copy.start()
    for d, copy in enumerate(copies):
        copy.wait()
        weighted(coef, grads.at[d], out.at[d])


def rest_of(coef, grads):
    groups, configs, chunk, hidden = grads.shape
    half = groups // 2
    return pl.pallas_call(
        rest_kernel,
        out_shape=jax.ShapeDtypeStruct((half, chunk, hidden), bf16),
        in_specs=[VMEM, HBM],
        out_specs=VMEM,
        scratch_shapes=[
            pltpu.VMEM((half, configs, chunk, hidden), bf16),
            pltpu.SemaphoreType.DMA((half,)),
        ],
        cost_estimate=pl.CostEstimate(flops=1 << 24, transcendentals=0, bytes_accessed=6 << 20),
        compiler_params=pltpu.CompilerParams(vmem_limit_bytes=16 << 20),
        name="rest",
    )(coef, in_hbm(grads))


def shards(
    node_feats,
    neighbors,
    self_weight,
    neighbor_weight,
    sage_bias,
    conf_index,
    layout_ids,
    join_weight,
    layout_table,
    join_bias,
    mid_weight,
    mid_bias,
    score_weight,
    config_pairs,
):
    both = ("cfg", "node")
    devices = lax.axis_size(both)
    node_count = lax.axis_size("node")
    group_count = lax.axis_size("cfg")
    rings = group_count // 2
    local_conf = conf_index.shape[0]
    width = node_feats.shape[1]
    per_peer = local_conf // node_count
    scale = 1.0 / math.sqrt(layout_ids.shape[1] * node_count)
    group = lax.axis_index("cfg")

    up = [(i, (i + 1) % node_count) for i in range(node_count)]
    down = [(i, j) for j, i in up]
    before = lax.ppermute(node_feats[-HALO:], "node", up)
    after = lax.ppermute(node_feats[:HALO], "node", down)
    starts = [c * node_count for c in range(group_count)]
    first = lax.ppermute(before, both, list(zip(starts[:-1], starts[1:])))
    ends = [start + node_count - 1 for start in starts]
    last = lax.ppermute(after, both, list(zip(ends[1:], ends[:-1])))
    rims = (before, after, first, last)
    spot = lax.axis_index("node").reshape(1)
    nodes, near = neighbors.shape
    nbrs = (2 * neighbors).T.reshape(near, nodes // 128, 128).transpose(1, 0, 2).reshape(-1)
    bias = sage_bias.reshape(1, -1)
    hold = lax.optimization_barrier

    table = table_of(node_feats)
    conf_src, _ = conf_rows_of(
        node_count, spot, nbrs, conf_index, rims, self_weight, neighbor_weight, bias, table
    )

    def layer(first, steps, given):
        return layer_of(
            first,
            steps,
            node_count,
            spot,
            nbrs,
            rims,
            node_feats,
            self_weight,
            neighbor_weight,
            bias,
            given,
        )

    swap = [(i, i ^ 1) for i in range(group_count)]

    def shift(value, by):
        perm = [(i, (i // 2 + by) % rings * 2 + i % 2) for i in range(group_count)]
        return lax.ppermute(value, "cfg", perm)

    mine = lax.all_to_all(
        conf_src.reshape(node_count, per_peer, width), "node", 0, 0, tiled=True
    )
    embed = layer(0, 1, None)
    mine, embed = hold((mine, embed))
    mine = mine.reshape(local_conf, width)
    xs = [mine] + [shift(mine, by) for by in range(1, rings)]
    xs = xs + [lax.ppermute(x, "cfg", swap) for x in xs]
    where = group.reshape(1)

    grads, sent = scorer_of(
        where,
        xs,
        layout_ids,
        join_weight,
        layout_table,
        join_bias.reshape(1, -1),
        mid_weight,
        mid_bias.reshape(1, -1),
        score_weight.reshape(1, -1),
        devices,
    )
    sent, embed = hold((sent, embed))
    got = lax.all_to_all(sent.reshape(devices, 1, 128), both, 0, 0, tiled=True)
    embed = layer(1, 1, embed)
    got, embed = hold((got, embed))
    loss, coef, away = ranking_of(scale, where, got.reshape(devices, 128), config_pairs.T, grads)
    came = lax.ppermute(away, "cfg", swap)
    kept = rest_of(coef, grads)
    sums = [kept[d].astype(f32) + came[d].astype(f32) for d in range(rings)]
    arrived = [shift(sums[d].astype(bf16), d) for d in range(1, rings)]
    row_grad = sums[0]
    for part in arrived:
        row_grad = row_grad + part.astype(f32)
    local_grad = lax.dot_general(
        row_grad.astype(bf16),
        join_weight,
        (((1,), (1,)), ((), ())),
        preferred_element_type=f32,
    )
    local_grad, embed = hold((local_grad.astype(bf16), embed))
    conf_grad = lax.all_to_all(
        local_grad.reshape(node_count, per_peer, width), "node", 0, 0, tiled=True
    )
    embed = layer(2, 2, embed)
    conf_grad = conf_grad.astype(f32).reshape(local_conf, width)
    return (embed, loss.reshape(()), conf_grad)


def solution(mesh):
    split = P(("cfg", "node"), None)
    placed = (split, split, P(), P(), P(), P(("cfg", "node")), P("cfg", "node")) + (P(),) * 7
    return jax.shard_map(
        shards,
        mesh=mesh,
        in_specs=placed,
        out_specs=(split, P(), split),
        check_vma=False,
    )
```

```python
import functools
import math

import jax
import jax.numpy as jnp
from jax import lax
from jax.experimental import pallas as pl
from jax.experimental.pallas import tpu as pltpu
from jax.sharding import PartitionSpec as P

HALO = 512
f32 = jnp.float32
bf16 = jnp.bfloat16
VMEM = pl.BlockSpec(memory_space=pltpu.VMEM)
SMEM = pl.BlockSpec(memory_space=pltpu.SMEM)
HBM = pl.BlockSpec(memory_space=pltpu.HBM)


def in_hbm(value):
    return pltpu.with_memory_space_constraint(value, pltpu.HBM)


def half_silu(half):
    tanh = jnp.tanh(half)
    scaled = half * tanh
    return half + scaled, tanh, scaled


def twice_slope(half, tanh, scaled):
    inner = 1.0 + half - scaled
    return inner + tanh * inner


def put_rows(table, first, source):
    rows = source.shape[0]
    value = source[...].astype(f32)
    table[pl.ds(2 * first, rows, stride=2), :] = value[:, :128]
    table[pl.ds(2 * first + 1, rows, stride=2), :] = value[:, 128:]


def put_rims(table, flip, inner, outer):
    end = table.shape[0] // 2 - HALO
    put_rows(table, pl.multiple_of((1 - flip[0]) * end, HALO), inner)
    put_rows(table, pl.multiple_of(flip[0] * end, HALO), outer)


def pair_at(table, at):
    return table[pl.ds(pl.multiple_of(at, 2), 2), :]


def table_kernel(feats, table):
    rows = feats.shape[0]
    put_rows(table, HALO + pl.multiple_of(pl.program_id(0) * rows, rows), feats)


def table_of(feats):
    nodes, width = feats.shape
    tile = 512
    return pl.pallas_call(
        table_kernel,
        out_shape=jax.ShapeDtypeStruct((2 * (nodes + 2 * HALO), 128), f32),
        grid=(nodes // tile,),
        in_specs=[pl.BlockSpec((tile, width), lambda i: (i, 0))],
        out_specs=VMEM,
        cost_estimate=pl.CostEstimate(flops=1 << 20, transcendentals=0, bytes_accessed=6 << 20),
        compiler_params=pltpu.CompilerParams(vmem_limit_bytes=16 << 20),
        name="window_rows",
    )(feats)


def layer_rows(own_left, own_right, left, right, sw, nw, bias):
    pre = jnp.dot(own_left, sw[:128, :], preferred_element_type=f32)
    pre += jnp.dot(own_right, sw[128:, :], preferred_element_type=f32)
    pre += jnp.dot(left, nw[:128, :], preferred_element_type=f32)
    pre += jnp.dot(right, nw[128:, :], preferred_element_type=f32)
    return half_silu(0.5 * (pre + bias[...]))[0].astype(bf16)


def conf_kernel(flip, nbrs, picks, inner, outer, *refs):
    sw_hbm, nw_hbm, bias_hbm, given, out, table, own, acc, sw, nw, bias, sems = refs
    copies = [
        pltpu.make_async_copy(source, target, sems.at[i])
        for i, (source, target) in enumerate(((sw_hbm, sw), (nw_hbm, nw), (bias_hbm, bias)))
    ]
    for copy in copies:
        copy.start()
    put_rims(table, flip, inner, outer)
    count = picks.shape[0]
    own3 = own.reshape(count, 2, 128)
    acc3 = acc.reshape(count, 2, 128)

    def body(block, carry):
        values = []
        for j in range(8):
            g = picks[block * 8 + j]
            at = (g >> 7) * 512 + (g & 127)
            near = [pair_at(table, nbrs[at + 128 * k]) for k in range(4)]
            values.append((pair_at(table, 2 * (HALO + g)), (near[0] + near[1]) + (near[2] + near[3])))
        for j in range(8):
            own3[block * 8 + j], acc3[block * 8 + j] = values[j]
        return carry

    lax.fori_loop(0, count // 8, body, 0)
    halves = [ref[pl.ds(side, count, stride=2), :] for ref in (own, acc) for side in (0, 1)]
    for copy in copies:
        copy.wait()
    out[...] = layer_rows(
        halves[0].astype(bf16),
        halves[1].astype(bf16),
        (halves[2] * 0.25).astype(bf16),
        (halves[3] * 0.25).astype(bf16),
        sw,
        nw,
        bias,
    )


def conf_rows_of(flip, nbrs, picks, inner, outer, sw, nw, bias, table):
    count = picks.shape[0]
    width = sw.shape[0]
    return pl.pallas_call(
        conf_kernel,
        out_shape=(
            jax.ShapeDtypeStruct((count, width), bf16),
            jax.ShapeDtypeStruct(table.shape, f32),
        ),
        in_specs=[SMEM] * 3 + [VMEM] * 2 + [HBM] * 3 + [VMEM],
        out_specs=(VMEM, VMEM),
        input_output_aliases={8: 1},
        scratch_shapes=[
            pltpu.VMEM((2 * count, 128), f32),
            pltpu.VMEM((2 * count, 128), f32),
            pltpu.VMEM(sw.shape, bf16),
            pltpu.VMEM(nw.shape, bf16),
            pltpu.VMEM(bias.shape, f32),
            pltpu.SemaphoreType.DMA((3,)),
        ],
        cost_estimate=pl.CostEstimate(
            flops=4 * count * width * width, transcendentals=0, bytes_accessed=6 << 20
        ),
        compiler_params=pltpu.CompilerParams(vmem_limit_bytes=16 << 20),
        name="conf_rows",
    )(flip, nbrs, picks, inner, outer, in_hbm(sw), in_hbm(nw), in_hbm(bias), table)


def layer_kernel(flip, nbrs, inner, outer, feats, own, sw, nw, bias, *refs):
    out, table, acc = refs[-3:]
    tile = own.shape[0]
    nodes = feats.shape[0]

    @pl.when(pl.program_id(0) == 0)
    def _():
        put_rims(table, flip, inner, outer)
        for start in range(0, nodes, 512):
            put_rows(table, HALO + start, feats.at[start : start + 512, :])

    acc3 = acc.reshape(tile, 2, 128)

    def body(block, carry):
        values = []
        for j in range(128):
            near = [pair_at(table, nbrs[block * 512 + (128 * k + j)]) for k in range(4)]
            values.append((near[0] + near[1]) + (near[2] + near[3]))
        for j in range(128):
            acc3[block * 128 + j] = values[j]
        return carry

    lax.fori_loop(0, tile // 128, body, 0)
    rows = own[...]
    out[...] = layer_rows(
        rows[:, :128],
        rows[:, 128:],
        (acc[pl.ds(0, tile, stride=2), :] * 0.25).astype(bf16),
        (acc[pl.ds(1, tile, stride=2), :] * 0.25).astype(bf16),
        sw,
        nw,
        bias,
    )


def layer_of(first, steps, flip, nbrs, inner, outer, feats, sw, nw, bias, given):
    nodes, width = feats.shape
    tile = 1024
    ahead = [] if given is None else [given]
    return pl.pallas_call(
        layer_kernel,
        out_shape=jax.ShapeDtypeStruct((nodes, width), bf16),
        grid=(steps,),
        in_specs=[
            SMEM,
            pl.BlockSpec((4 * tile,), lambda i: (first + i,), memory_space=pltpu.SMEM),
            VMEM,
            VMEM,
            VMEM,
            pl.BlockSpec((tile, width), lambda i: (first + i, 0)),
            VMEM,
            VMEM,
            VMEM,
        ]
        + [HBM] * len(ahead),
        out_specs=pl.BlockSpec((tile, width), lambda i: (first + i, 0)),
        input_output_aliases={9: 0} if ahead else {},
        scratch_shapes=[
            pltpu.VMEM((2 * (nodes + 2 * HALO), 128), f32),
            pltpu.VMEM((2 * tile, 128), f32),
        ],
        cost_estimate=pl.CostEstimate(
            flops=steps * 4 * tile * width * width, transcendentals=0, bytes_accessed=steps << 23
        ),
        compiler_params=pltpu.CompilerParams(vmem_limit_bytes=24 << 20),
        name="graph_layer",
    )(flip, nbrs, inner, outer, feats, feats, sw, nw, bias, *ahead)


def place_of(group, turn):
    return group ^ (2 * (turn & 3) + (turn >> 2))


def scorer_kernel(groups, where, *refs):
    xs, refs = refs[:groups], refs[groups:]
    ids, join, table, jbias, mid, mbias, weight, grads_hbm, sent = refs[:9]
    base, tabh, midh, back, total, grads, sems = refs[9:]
    step = pl.program_id(0)
    slot = step & 1
    chunk = xs[0].shape[0]
    configs = ids.shape[0]
    layouts = table.shape[0]
    one = jnp.asarray(1.0, bf16)

    @pl.when(step == 0)
    def _():
        for i in range(groups):
            base[i] = 0.5 * (
                jnp.dot(xs[i][...], join[...], preferred_element_type=f32) + jbias[...]
            )
        tabh[...] = (table[...].astype(f32) * 0.5).astype(bf16)
        middle = mid[...].astype(f32)
        midh[...] = (middle * 0.5).astype(bf16)
        back[...] = jnp.transpose(middle * (weight[...] * 0.25)).astype(bf16)
        total[...] = jnp.zeros_like(total)

    def copy_of(turn, place):
        return pltpu.make_async_copy(grads.at[place], grads_hbm.at[turn], sems.at[place])

    @pl.when(step >= 2)
    def _():
        copy_of(step - 2, slot).wait()

    columns = jnp.transpose(ids[...].astype(f32))
    lanes = lax.broadcasted_iota(jnp.int32, (chunk, layouts), 1).astype(f32)
    rows = base[step]
    some = 8
    for first in range(0, configs, some):
        picks = jnp.concatenate(
            [
                jnp.where(columns[:, k : k + 1] == lanes, 1.0, 0.0).astype(bf16)
                for k in range(first, first + some)
            ],
            axis=0,
        )
        half = jnp.dot(picks, tabh[...], preferred_element_type=f32)
        half = (half + jnp.concatenate([rows] * some, axis=0)).astype(bf16)
        tanh = jnp.tanh(half)
        act = half + half * tanh
        slope = (one + tanh) * (one + half * (one - tanh))
        outer = jnp.dot(act, midh[...], preferred_element_type=f32)
        outer = (outer + 0.5 * mbias[...]).astype(bf16)
        tanh2 = jnp.tanh(outer)
        act2 = (outer + outer * tanh2).astype(f32)
        slope2 = (one + tanh2) * (one + outer * (one - tanh2))
        for q in range(some):
            part = act2[q * chunk : (q + 1) * chunk, :]
            total[first + q : first + q + 1, :] += jnp.sum(part, axis=0, keepdims=True)
        grad = jnp.dot(slope2, back[...], preferred_element_type=f32).astype(bf16) * slope
        for q in range(some):
            grads[slot, first + q] = grad[q * chunk : (q + 1) * chunk, :]

    copy_of(step, slot).start()

    @pl.when(step == groups - 1)
    def _():
        scores = jnp.sum(total[...] * weight[...], axis=1, keepdims=True)
        lane = lax.broadcasted_iota(jnp.int32, (configs, 128), 1)
        sub = lax.broadcasted_iota(jnp.int32, (configs, 128), 0)
        spread = jnp.where(lane == sub + where[0] * configs, scores, 0.0)
        sent[...] = jnp.broadcast_to(jnp.sum(spread, axis=0, keepdims=True), sent.shape)
        copy_of(step - 1, 1 - slot).wait()
        copy_of(step, slot).wait()


def scorer_of(where, xs, ids, join, table, jbias, mid, mbias, weight, devices):
    groups = len(xs)
    configs = ids.shape[0]
    chunk, width = xs[0].shape
    hidden = join.shape[1]
    return pl.pallas_call(
        functools.partial(scorer_kernel, groups),
        out_shape=(
            pltpu.HBM((groups, configs, chunk, hidden), bf16),
            jax.ShapeDtypeStruct((devices, 128), f32),
        ),
        grid_spec=pltpu.PrefetchScalarGridSpec(
            num_scalar_prefetch=1,
            grid=(groups,),
            in_specs=[VMEM] * groups
            + [pl.BlockSpec((configs, chunk), lambda i, where: (0, place_of(where[0], i)))]
            + [VMEM] * 6,
            out_specs=(HBM, VMEM),
            scratch_shapes=[
                pltpu.VMEM((groups, chunk, hidden), f32),
                pltpu.VMEM(table.shape, bf16),
                pltpu.VMEM(mid.shape, bf16),
                pltpu.VMEM(mid.shape, bf16),
                pltpu.VMEM((configs, hidden), f32),
                pltpu.VMEM((2, configs, chunk, hidden), bf16),
                pltpu.SemaphoreType.DMA((2,)),
            ],
        ),
        cost_estimate=pl.CostEstimate(
            flops=6 * groups * configs * chunk * width * width,
            transcendentals=2 * groups * configs * chunk * width,
            bytes_accessed=10 << 20,
        ),
        compiler_params=pltpu.CompilerParams(vmem_limit_bytes=30 << 20),
        name="scorer",
    )(where, *xs, ids, join, table, jbias, mid, mbias, weight)


def weighted(coef, grads, out):
    configs, chunk, hidden = grads.shape
    some = 32
    for start in range(0, chunk, some):
        rows = grads[0, start : start + some, :].astype(f32) * coef[0:1, :]
        for k in range(1, configs):
            rows = rows + grads[k, start : start + some, :].astype(f32) * coef[k : k + 1, :]
        out[start : start + some, :] = rows.astype(bf16)


def fetches(grads_hbm, grads, sems, first):
    half = grads.shape[0]
    return [
        pltpu.make_async_copy(grads_hbm.at[first + d], grads.at[d], sems.at[d])
        for d in range(half)
    ]


def ranking_kernel(scale, where, got, pairs, grads_hbm, loss, coef, out, column, grads, sems):
    half, configs, chunk, hidden = grads.shape
    copies = fetches(grads_hbm, grads, sems, half)
    for copy in copies:
        copy.start()
    score = jnp.sum(got[...], axis=0, keepdims=True) * scale
    lane = lax.broadcasted_iota(jnp.int32, (128, 128), 1)
    sub = lax.broadcasted_iota(jnp.int32, (128, 128), 0)
    score = jnp.sum(jnp.where(lane == sub, score, 0.0), axis=1, keepdims=True)
    count = pairs.shape[1]
    ids = lax.broadcasted_iota(jnp.int32, (128, count), 0)
    second = jnp.where(pairs[1:2, :] == ids, 1.0, 0.0)
    signed = second - jnp.where(pairs[0:1, :] == ids, 1.0, 0.0)
    gap = jnp.sum(signed * score, axis=0, keepdims=True)
    fade = jnp.exp(-jnp.abs(gap))
    soft = jnp.maximum(gap, 0.0) + jnp.log1p(fade)
    loss[...] = jnp.sum(soft, axis=1, keepdims=True) * (1.0 / count)
    slope = jnp.where(gap >= 0.0, 1.0, fade) / (1.0 + fade)
    grad = jnp.sum(slope * signed, axis=1, keepdims=True) * (65536.0 * scale / count)
    column[...] = jnp.broadcast_to(grad, column.shape)
    coef[...] = column[pl.ds(pl.multiple_of(where[0] * configs, configs), configs), :]
    for d in range(half):
        copies[d].wait()
        weighted(coef, grads.at[d], out.at[d])


def ranking_of(scale, where, got, pairs, grads):
    groups, configs, chunk, hidden = grads.shape
    half = groups // 2
    return pl.pallas_call(
        functools.partial(ranking_kernel, scale),
        out_shape=(
            jax.ShapeDtypeStruct((1, 1), f32),
            jax.ShapeDtypeStruct((configs, hidden), f32),
            jax.ShapeDtypeStruct((half, chunk, hidden), bf16),
        ),
        in_specs=[SMEM, VMEM, VMEM, HBM],
        out_specs=(VMEM, VMEM, VMEM),
        scratch_shapes=[
            pltpu.VMEM((128, hidden), f32),
            pltpu.VMEM((half, configs, chunk, hidden), bf16),
            pltpu.SemaphoreType.DMA((half,)),
        ],
        cost_estimate=pl.CostEstimate(flops=1 << 24, transcendentals=0, bytes_accessed=6 << 20),
        compiler_params=pltpu.CompilerParams(vmem_limit_bytes=16 << 20),
        name="ranking",
    )(where, got, pairs, in_hbm(grads))


def rest_kernel(coef, grads_hbm, out, grads, sems):
    copies = fetches(grads_hbm, grads, sems, 0)
    for copy in copies:
        copy.start()
    for d, copy in enumerate(copies):
        copy.wait()
        weighted(coef, grads.at[d], out.at[d])


def rest_of(coef, grads):
    groups, configs, chunk, hidden = grads.shape
    half = groups // 2
    return pl.pallas_call(
        rest_kernel,
        out_shape=jax.ShapeDtypeStruct((half, chunk, hidden), bf16),
        in_specs=[VMEM, HBM],
        out_specs=VMEM,
        scratch_shapes=[
            pltpu.VMEM((half, configs, chunk, hidden), bf16),
            pltpu.SemaphoreType.DMA((half,)),
        ],
        cost_estimate=pl.CostEstimate(flops=1 << 24, transcendentals=0, bytes_accessed=6 << 20),
        compiler_params=pltpu.CompilerParams(vmem_limit_bytes=16 << 20),
        name="rest",
    )(coef, in_hbm(grads))


def shards(
    node_feats,
    neighbors,
    self_weight,
    neighbor_weight,
    sage_bias,
    conf_index,
    layout_ids,
    join_weight,
    layout_table,
    join_bias,
    mid_weight,
    mid_bias,
    score_weight,
    config_pairs,
):
    both = ("cfg", "node")
    devices = lax.axis_size(both)
    node_count = lax.axis_size("node")
    group_count = lax.axis_size("cfg")
    rings = group_count // 2
    local_conf = conf_index.shape[0]
    width = node_feats.shape[1]
    per_peer = local_conf // node_count
    scale = 1.0 / math.sqrt(layout_ids.shape[1] * node_count)
    group = lax.axis_index("cfg")

    nodes, near = neighbors.shape
    spot = lax.axis_index("node")
    flip = (spot & 1).reshape(1)

    def trade(odd, partner):
        rows = lax.dynamic_slice_in_dim(node_feats, odd * (nodes - HALO), HALO, 0)
        pairs = [(i, partner(i)) for i in range(devices) if 0 <= partner(i) < devices]
        return lax.ppermute(rows, both, pairs)

    outer = trade(spot & 1, lambda i: i + 1 if i % 2 else i - 1)
    inner = trade(1 - (spot & 1), lambda i: i ^ 1)
    nbrs = (2 * neighbors).T.reshape(near, nodes // 128, 128).transpose(1, 0, 2).reshape(-1)
    bias = sage_bias.reshape(1, -1)
    hold = lax.optimization_barrier

    table = table_of(node_feats)
    conf_src, _ = conf_rows_of(
        flip, nbrs, conf_index, inner, outer, self_weight, neighbor_weight, bias, table
    )

    def layer(first, steps, given):
        return layer_of(
            first,
            steps,
            flip,
            nbrs,
            inner,
            outer,
            node_feats,
            self_weight,
            neighbor_weight,
            bias,
            given,
        )

    swap = [(i, i ^ 1) for i in range(group_count)]

    def shift(value, by):
        return lax.ppermute(value, "cfg", [(i, i ^ (2 * by)) for i in range(group_count)])

    mine = lax.all_to_all(
        conf_src.reshape(node_count, per_peer, width), "node", 0, 0, tiled=True
    )
    embed = layer(0, 1, None)
    mine, embed = hold((mine, embed))
    mine = mine.reshape(local_conf, width)
    xs = [mine] + [shift(mine, by) for by in range(1, rings)]
    xs = xs + [lax.ppermute(x, "cfg", swap) for x in xs]
    where = group.reshape(1)

    grads, sent = scorer_of(
        where,
        xs,
        layout_ids,
        join_weight,
        layout_table,
        join_bias.reshape(1, -1),
        mid_weight,
        mid_bias.reshape(1, -1),
        score_weight.reshape(1, -1),
        devices,
    )
    sent, embed = hold((sent, embed))
    got = lax.all_to_all(sent.reshape(devices, 1, 128), both, 0, 0, tiled=True)
    embed = layer(1, 1, embed)
    got, embed = hold((got, embed))
    loss, coef, away = ranking_of(scale, where, got.reshape(devices, 128), config_pairs.T, grads)
    came = lax.ppermute(away, "cfg", swap)
    kept = rest_of(coef, grads)
    sums = [kept[d].astype(f32) + came[d].astype(f32) for d in range(rings)]
    arrived = [shift(sums[d].astype(bf16), d) for d in range(1, rings)]
    row_grad = sums[0]
    for part in arrived:
        row_grad = row_grad + part.astype(f32)
    local_grad = lax.dot_general(
        row_grad.astype(bf16),
        join_weight,
        (((1,), (1,)), ((), ())),
        preferred_element_type=f32,
    )
    local_grad, embed = hold((local_grad.astype(bf16), embed))
    conf_grad = lax.all_to_all(
        local_grad.reshape(node_count, per_peer, width), "node", 0, 0, tiled=True
    )
    embed = layer(2, 2, embed)
    conf_grad = conf_grad.astype(f32).reshape(local_conf, width)
    return (embed, loss.reshape(()), conf_grad)


def solution(mesh):
    split = P(("cfg", "node"), None)
    placed = (split, split, P(), P(), P(), P(("cfg", "node")), P("cfg", "node")) + (P(),) * 7
    return jax.shard_map(
        shards,
        mesh=mesh,
        in_specs=placed,
        out_specs=(split, P(), split),
        check_vma=False,
    )
```

```python
import functools
import math

import jax
import jax.numpy as jnp
from jax import lax
from jax.experimental import pallas as pl
from jax.experimental.pallas import tpu as pltpu
from jax.sharding import PartitionSpec as P

HALO = 512
f32 = jnp.float32
bf16 = jnp.bfloat16
VMEM = pl.BlockSpec(memory_space=pltpu.VMEM)
SMEM = pl.BlockSpec(memory_space=pltpu.SMEM)
HBM = pl.BlockSpec(memory_space=pltpu.HBM)


def in_hbm(value):
    return pltpu.with_memory_space_constraint(value, pltpu.HBM)


def half_silu(half):
    tanh = jnp.tanh(half)
    scaled = half * tanh
    return half + scaled, tanh, scaled


def twice_slope(half, tanh, scaled):
    inner = 1.0 + half - scaled
    return inner + tanh * inner


def put_rows(table, first, source):
    rows = source.shape[0]
    value = source[...].astype(f32)
    table[pl.ds(2 * first, rows, stride=2), :] = value[:, :128]
    table[pl.ds(2 * first + 1, rows, stride=2), :] = value[:, 128:]


def put_rims(table, flip, inner, outer):
    end = table.shape[0] // 2 - HALO
    put_rows(table, pl.multiple_of((1 - flip[0]) * end, HALO), inner)
    put_rows(table, pl.multiple_of(flip[0] * end, HALO), outer)


def pair_at(table, at):
    return table[pl.ds(pl.multiple_of(at, 2), 2), :]


def table_kernel(feats, table):
    rows = feats.shape[0]
    put_rows(table, HALO + pl.multiple_of(pl.program_id(0) * rows, rows), feats)


def table_of(feats):
    nodes, width = feats.shape
    tile = 512
    return pl.pallas_call(
        table_kernel,
        out_shape=jax.ShapeDtypeStruct((2 * (nodes + 2 * HALO), 128), f32),
        grid=(nodes // tile,),
        in_specs=[pl.BlockSpec((tile, width), lambda i: (i, 0))],
        out_specs=VMEM,
        cost_estimate=pl.CostEstimate(flops=1 << 20, transcendentals=0, bytes_accessed=6 << 20),
        compiler_params=pltpu.CompilerParams(vmem_limit_bytes=16 << 20),
        name="window_rows",
    )(feats)


def layer_rows(own_left, own_right, left, right, sw, nw, bias, kind=bf16):
    pre = jnp.dot(own_left, sw[:128, :], preferred_element_type=f32)
    pre += jnp.dot(own_right, sw[128:, :], preferred_element_type=f32)
    pre += jnp.dot(left, nw[:128, :], preferred_element_type=f32)
    pre += jnp.dot(right, nw[128:, :], preferred_element_type=f32)
    return half_silu(0.5 * (pre + bias[...]))[0].astype(kind)


def conf_kernel(flip, nbrs, picks, outer, inner, *refs):
    sw_hbm, nw_hbm, bias_hbm, given, out, table, own, acc, sw, nw, bias, sems = refs
    copies = [
        pltpu.make_async_copy(source, target, sems.at[i])
        for i, (source, target) in enumerate(((sw_hbm, sw), (nw_hbm, nw), (bias_hbm, bias)))
    ]
    for copy in copies:
        copy.start()
    put_rims(table, flip, inner, outer)
    count = picks.shape[0]
    own3 = own.reshape(count, 2, 128)
    acc3 = acc.reshape(count, 2, 128)

    def body(block, carry):
        values = []
        for j in range(8):
            g = picks[block * 8 + j]
            at = (g >> 7) * 512 + (g & 127)
            near = [pair_at(table, nbrs[at + 128 * k]) for k in range(4)]
            values.append((pair_at(table, 2 * (HALO + g)), (near[0] + near[1]) + (near[2] + near[3])))
        for j in range(8):
            own3[block * 8 + j], acc3[block * 8 + j] = values[j]
        return carry

    lax.fori_loop(0, count // 8, body, 0)
    halves = [ref[pl.ds(side, count, stride=2), :] for ref in (own, acc) for side in (0, 1)]
    for copy in copies:
        copy.wait()
    value = layer_rows(
        halves[0].astype(bf16),
        halves[1].astype(bf16),
        (halves[2] * 0.25).astype(bf16),
        (halves[3] * 0.25).astype(bf16),
        sw,
        nw,
        bias,
        f32,
    )
    share = out.shape[1]
    for peer in range(out.shape[0]):
        out[peer] = value[peer * share : (peer + 1) * share, :].astype(bf16)


def conf_rows_of(peers, flip, nbrs, picks, inner, outer, sw, nw, bias, table):
    count = picks.shape[0]
    width = sw.shape[0]
    return pl.pallas_call(
        conf_kernel,
        out_shape=(
            jax.ShapeDtypeStruct((peers, count // peers, width), bf16),
            jax.ShapeDtypeStruct(table.shape, f32),
        ),
        in_specs=[SMEM] * 3 + [VMEM] * 2 + [HBM] * 3 + [VMEM],
        out_specs=(VMEM, VMEM),
        input_output_aliases={8: 1},
        scratch_shapes=[
            pltpu.VMEM((2 * count, 128), f32),
            pltpu.VMEM((2 * count, 128), f32),
            pltpu.VMEM(sw.shape, bf16),
            pltpu.VMEM(nw.shape, bf16),
            pltpu.VMEM(bias.shape, f32),
            pltpu.SemaphoreType.DMA((3,)),
        ],
        cost_estimate=pl.CostEstimate(
            flops=4 * count * width * width, transcendentals=0, bytes_accessed=6 << 20
        ),
        compiler_params=pltpu.CompilerParams(vmem_limit_bytes=16 << 20),
        name="conf_rows",
    )(flip, nbrs, picks, outer, inner, in_hbm(sw), in_hbm(nw), in_hbm(bias), table)


def layer_kernel(flip, nbrs, outer, inner, feats, own, sw, nw, bias, *refs):
    out, table, acc = refs[-3:]
    tile = own.shape[0]
    nodes = feats.shape[0]

    @pl.when(pl.program_id(0) == 0)
    def _():
        put_rims(table, flip, inner, outer)
        for start in range(0, nodes, 512):
            put_rows(table, HALO + start, feats.at[start : start + 512, :])

    acc3 = acc.reshape(tile, 2, 128)

    def body(block, carry):
        values = []
        for j in range(128):
            near = [pair_at(table, nbrs[block * 512 + (128 * k + j)]) for k in range(4)]
            values.append((near[0] + near[1]) + (near[2] + near[3]))
        for j in range(128):
            acc3[block * 128 + j] = values[j]
        return carry

    lax.fori_loop(0, tile // 128, body, 0)
    rows = own[...]
    out[...] = layer_rows(
        rows[:, :128],
        rows[:, 128:],
        (acc[pl.ds(0, tile, stride=2), :] * 0.25).astype(bf16),
        (acc[pl.ds(1, tile, stride=2), :] * 0.25).astype(bf16),
        sw,
        nw,
        bias,
    )


def layer_of(first, steps, flip, nbrs, inner, outer, feats, sw, nw, bias, given):
    nodes, width = feats.shape
    tile = 512
    ahead = [] if given is None else [given]
    return pl.pallas_call(
        layer_kernel,
        out_shape=jax.ShapeDtypeStruct((nodes, width), bf16),
        grid=(steps,),
        in_specs=[
            SMEM,
            pl.BlockSpec((4 * tile,), lambda i: (first + i,), memory_space=pltpu.SMEM),
            VMEM,
            VMEM,
            VMEM,
            pl.BlockSpec((tile, width), lambda i: (first + i, 0)),
            VMEM,
            VMEM,
            VMEM,
        ]
        + [HBM] * len(ahead),
        out_specs=pl.BlockSpec((tile, width), lambda i: (first + i, 0)),
        input_output_aliases={9: 0} if ahead else {},
        scratch_shapes=[
            pltpu.VMEM((2 * (nodes + 2 * HALO), 128), f32),
            pltpu.VMEM((2 * tile, 128), f32),
        ],
        cost_estimate=pl.CostEstimate(
            flops=steps * 4 * tile * width * width, transcendentals=0, bytes_accessed=steps << 23
        ),
        compiler_params=pltpu.CompilerParams(vmem_limit_bytes=24 << 20),
        name="graph_layer",
    )(flip, nbrs, outer, inner, feats, feats, sw, nw, bias, *ahead)


def place_of(group, turn):
    return group ^ (2 * (turn & 3) + (turn >> 2))


def prepare_kernel(table, mid, weight, tabh, midh, back):
    tabh[...] = (table[...].astype(f32) * 0.5).astype(bf16)
    middle = mid[...].astype(f32)
    midh[...] = (middle * 0.5).astype(bf16)
    back[...] = jnp.transpose(middle * (weight[...] * 0.25)).astype(bf16)


def prepared(table, mid, weight):
    return pl.pallas_call(
        prepare_kernel,
        out_shape=tuple(jax.ShapeDtypeStruct(x.shape, bf16) for x in (table, mid, mid)),
        in_specs=[VMEM] * 3,
        out_specs=(VMEM,) * 3,
        cost_estimate=pl.CostEstimate(flops=1 << 20, transcendentals=0, bytes_accessed=1 << 19),
        compiler_params=pltpu.CompilerParams(vmem_limit_bytes=8 << 20),
        name="prepare",
    )(table, mid, weight)


def scorer_kernel(groups, final, where, *refs):
    xs, refs = refs[:groups], refs[groups:]
    ids, join, jbias, tabh, midh, back, mbias, weight = refs[:8]
    given, (grads_hbm, sent, base, total, grads, sems) = refs[8:-6], refs[-6:]
    step = pl.program_id(0)
    slot = step & 1
    chunk = xs[0].shape[0]
    configs = ids.shape[0]
    layouts = tabh.shape[0]
    one = jnp.asarray(1.0, bf16)

    @pl.when(step == 0)
    def _():
        for i in range(groups):
            base[i] = 0.5 * (
                jnp.dot(xs[i][...], join[...], preferred_element_type=f32) + jbias[...]
            )
        total[...] = given[0][...] if given else jnp.zeros_like(total)

    def copy_of(turn, place):
        return pltpu.make_async_copy(grads.at[place], grads_hbm.at[turn], sems.at[place])

    @pl.when(step >= 2)
    def _():
        copy_of(step - 2, slot).wait()

    columns = jnp.transpose(ids[...].astype(f32))
    lanes = lax.broadcasted_iota(jnp.int32, (chunk, layouts), 1).astype(f32)
    rows = base[step]
    some = 8
    for first in range(0, configs, some):
        picks = jnp.concatenate(
            [
                jnp.where(columns[:, k : k + 1] == lanes, 1.0, 0.0).astype(bf16)
                for k in range(first, first + some)
            ],
            axis=0,
        )
        half = jnp.dot(picks, tabh[...], preferred_element_type=f32)
        half = (half + jnp.concatenate([rows] * some, axis=0)).astype(bf16)
        tanh = jnp.tanh(half)
        above = one + tanh
        slope = above * (one + half * (one - tanh))
        outer = jnp.dot(half * above, midh[...], preferred_element_type=f32)
        outer = (outer + 0.5 * mbias[...]).astype(bf16)
        tanh2 = jnp.tanh(outer)
        above2 = one + tanh2
        act2 = (outer * above2).astype(f32)
        slope2 = above2 * (one + outer * (one - tanh2))
        for q in range(some):
            part = act2[q * chunk : (q + 1) * chunk, :]
            total[first + q : first + q + 1, :] += jnp.sum(part, axis=0, keepdims=True)
        grad = jnp.dot(slope2, back[...], preferred_element_type=f32).astype(bf16) * slope
        for q in range(some):
            grads[slot, first + q] = grad[q * chunk : (q + 1) * chunk, :]

    copy_of(step, slot).start()

    @pl.when(step == groups - 1)
    def _():
        if final:
            scores = jnp.sum(total[...] * weight[...], axis=1, keepdims=True)
            lane = lax.broadcasted_iota(jnp.int32, (configs, 128), 1)
            sub = lax.broadcasted_iota(jnp.int32, (configs, 128), 0)
            spread = jnp.where(lane == sub + where[0] * configs, scores, 0.0)
            sent[...] = jnp.broadcast_to(jnp.sum(spread, axis=0, keepdims=True), sent.shape)
        else:
            sent[...] = total[...]
        copy_of(step - 1, 1 - slot).wait()
        copy_of(step, slot).wait()


def scorer_of(final, turns, where, xs, ids, join, jbias, weights, mbias, weight, given):
    groups = len(xs)
    configs = ids.shape[0]
    chunk, width = xs[0].shape
    hidden = join.shape[1]
    start, stride = turns
    summed = final if final else (configs, hidden)
    return pl.pallas_call(
        functools.partial(scorer_kernel, groups, final),
        out_shape=(
            pltpu.HBM((groups, configs, chunk, hidden), bf16),
            jax.ShapeDtypeStruct(summed, f32),
        ),
        grid_spec=pltpu.PrefetchScalarGridSpec(
            num_scalar_prefetch=1,
            grid=(groups,),
            in_specs=[VMEM] * groups
            + [
                pl.BlockSpec(
                    (configs, chunk), lambda i, where: (0, place_of(where[0], start + stride * i))
                )
            ]
            + [VMEM] * (7 + len(given)),
            out_specs=(HBM, VMEM),
            scratch_shapes=[
                pltpu.VMEM((groups, chunk, hidden), f32),
                pltpu.VMEM((configs, hidden), f32),
                pltpu.VMEM((2, configs, chunk, hidden), bf16),
                pltpu.SemaphoreType.DMA((2,)),
            ],
        ),
        cost_estimate=pl.CostEstimate(
            flops=6 * groups * configs * chunk * width * width,
            transcendentals=2 * groups * configs * chunk * width,
            bytes_accessed=groups << 20,
        ),
        compiler_params=pltpu.CompilerParams(vmem_limit_bytes=24 << 20),
        name="scorer",
    )(where, *xs, ids, join, jbias, *weights, mbias, weight, *given)


def weighted(coef, grads, out):
    configs, chunk, hidden = grads.shape
    some = 32
    for start in range(0, chunk, some):
        rows = grads[0, start : start + some, :].astype(f32) * coef[0:1, :]
        for k in range(1, configs):
            rows = rows + grads[k, start : start + some, :].astype(f32) * coef[k : k + 1, :]
        out[start : start + some, :] = rows.astype(bf16)


def fetches(pair, later, which, grads, sems):
    sources = [pair.at[which]] + [later.at[d] for d in range(grads.shape[0] - 1)]
    return [
        pltpu.make_async_copy(source, grads.at[d], sems.at[d]) for d, source in enumerate(sources)
    ]


def ranking_kernel(scale, where, got, pairs, pair, later, loss, coef, out, column, grads, sems):
    half, configs, chunk, hidden = grads.shape
    copies = fetches(pair, later, 1, grads, sems)
    for copy in copies:
        copy.start()
    score = jnp.sum(got[...], axis=0, keepdims=True) * scale
    lane = lax.broadcasted_iota(jnp.int32, (128, 128), 1)
    sub = lax.broadcasted_iota(jnp.int32, (128, 128), 0)
    score = jnp.sum(jnp.where(lane == sub, score, 0.0), axis=1, keepdims=True)
    count = pairs.shape[1]
    ids = lax.broadcasted_iota(jnp.int32, (128, count), 0)
    second = jnp.where(pairs[1:2, :] == ids, 1.0, 0.0)
    signed = second - jnp.where(pairs[0:1, :] == ids, 1.0, 0.0)
    gap = jnp.sum(signed * score, axis=0, keepdims=True)
    fade = jnp.exp(-jnp.abs(gap))
    soft = jnp.maximum(gap, 0.0) + jnp.log1p(fade)
    loss[...] = jnp.sum(soft, axis=1, keepdims=True) * (1.0 / count)
    slope = jnp.where(gap >= 0.0, 1.0, fade) / (1.0 + fade)
    grad = jnp.sum(slope * signed, axis=1, keepdims=True) * (65536.0 * scale / count)
    column[...] = jnp.broadcast_to(grad, column.shape)
    coef[...] = column[pl.ds(pl.multiple_of(where[0] * configs, configs), configs), :]
    for d in range(half):
        copies[d].wait()
        weighted(coef, grads.at[d], out.at[d])


def ranking_of(scale, where, got, pairs, pair, later):
    half, configs, chunk, hidden = later.shape
    half += 1
    return pl.pallas_call(
        functools.partial(ranking_kernel, scale),
        out_shape=(
            jax.ShapeDtypeStruct((1, 1), f32),
            jax.ShapeDtypeStruct((configs, hidden), f32),
            jax.ShapeDtypeStruct((half, chunk, hidden), bf16),
        ),
        in_specs=[SMEM, VMEM, VMEM, HBM, HBM],
        out_specs=(VMEM, VMEM, VMEM),
        scratch_shapes=[
            pltpu.VMEM((128, hidden), f32),
            pltpu.VMEM((half, configs, chunk, hidden), bf16),
            pltpu.SemaphoreType.DMA((half,)),
        ],
        cost_estimate=pl.CostEstimate(flops=1 << 24, transcendentals=0, bytes_accessed=6 << 20),
        compiler_params=pltpu.CompilerParams(vmem_limit_bytes=16 << 20),
        name="ranking",
    )(where, got, pairs, in_hbm(pair), in_hbm(later))


def rest_kernel(coef, pair, later, out, grads, sems):
    copies = fetches(pair, later, 0, grads, sems)
    for copy in copies:
        copy.start()
    for d, copy in enumerate(copies):
        copy.wait()
        weighted(coef, grads.at[d], out.at[d])


def rest_of(coef, pair, later):
    half, configs, chunk, hidden = later.shape
    half += 1
    return pl.pallas_call(
        rest_kernel,
        out_shape=jax.ShapeDtypeStruct((half, chunk, hidden), bf16),
        in_specs=[VMEM, HBM, HBM],
        out_specs=VMEM,
        scratch_shapes=[
            pltpu.VMEM((half, configs, chunk, hidden), bf16),
            pltpu.SemaphoreType.DMA((half,)),
        ],
        cost_estimate=pl.CostEstimate(flops=1 << 24, transcendentals=0, bytes_accessed=6 << 20),
        compiler_params=pltpu.CompilerParams(vmem_limit_bytes=16 << 20),
        name="rest",
    )(coef, in_hbm(pair), in_hbm(later))


def shards(
    node_feats,
    neighbors,
    self_weight,
    neighbor_weight,
    sage_bias,
    conf_index,
    layout_ids,
    join_weight,
    layout_table,
    join_bias,
    mid_weight,
    mid_bias,
    score_weight,
    config_pairs,
):
    both = ("cfg", "node")
    devices = lax.axis_size(both)
    node_count = lax.axis_size("node")
    group_count = lax.axis_size("cfg")
    rings = group_count // 2
    local_conf = conf_index.shape[0]
    width = node_feats.shape[1]
    per_peer = local_conf // node_count
    scale = 1.0 / math.sqrt(layout_ids.shape[1] * node_count)
    group = lax.axis_index("cfg")

    nodes, near = neighbors.shape
    spot = lax.axis_index("node")
    flip = (spot & 1).reshape(1)

    def trade(rows, partner):
        pairs = [(i, partner(i)) for i in range(devices) if 0 <= partner(i) < devices]
        return lax.ppermute(rows, both, pairs)

    def rim(feats, odd):
        return lax.dynamic_slice_in_dim(feats, odd * (nodes - HALO), HALO, 0)

    outer = trade(rim(node_feats, spot & 1), lambda i: i + 1 if i % 2 else i - 1)
    inner = trade(rim(node_feats, 1 - (spot & 1)), lambda i: i ^ 1)
    nbrs = (2 * neighbors).T.reshape(near, nodes // 128, 128).transpose(1, 0, 2).reshape(-1)
    bias = sage_bias.reshape(1, -1)
    hold = lax.optimization_barrier

    table = table_of(node_feats)
    conf_src, _ = conf_rows_of(
        node_count,
        flip,
        nbrs,
        conf_index,
        inner,
        outer,
        self_weight,
        neighbor_weight,
        bias,
        table,
    )

    def layer(first, steps, given):
        return layer_of(
            first,
            steps,
            flip,
            nbrs,
            inner,
            outer,
            node_feats,
            self_weight,
            neighbor_weight,
            bias,
            given,
        )

    swap = [(i, i ^ 1) for i in range(group_count)]

    def shift(value, by):
        return lax.ppermute(value, "cfg", [(i, i ^ (2 * by)) for i in range(group_count)])

    mine = lax.all_to_all(conf_src, "node", 0, 0, tiled=True)
    embed = layer(0, 2, None)
    weight = score_weight.reshape(1, -1)
    weights = prepared(layout_table, mid_weight, weight)
    mine, embed, *weights = hold((mine, embed, *weights))
    mine = mine.reshape(local_conf, width)
    others = [shift(mine, by) for by in range(1, rings)]
    where = group.reshape(1)

    def scorer(final, turns, xs, given):
        return scorer_of(
            final,
            turns,
            where,
            xs,
            layout_ids,
            join_weight,
            join_bias.reshape(1, -1),
            weights,
            mid_bias.reshape(1, -1),
            weight,
            given,
        )

    pair, total = scorer(None, (0, rings), [mine, lax.ppermute(mine, "cfg", swap)], [])
    others = list(hold((*others, total)))
    total = others.pop()
    swapped = [lax.ppermute(x, "cfg", swap) for x in others]
    own, total = scorer(None, (1, 1), others, [total])
    swapped = list(hold((*swapped, total)))
    total = swapped.pop()
    other, sent = scorer((devices, 128), (rings + 1, 1), swapped, [total])
    sent, embed = hold((sent, embed))
    got = lax.all_to_all(sent.reshape(devices, 1, 128), both, 0, 0, tiled=True)
    embed = layer(2, 3, embed)
    got, embed = hold((got, embed))
    loss, coef, away = ranking_of(
        scale, where, got.reshape(devices, 128), config_pairs.T, pair, other
    )
    came = lax.ppermute(away, "cfg", swap)
    kept = rest_of(coef, pair, own)
    sums = [kept[d].astype(f32) + came[d].astype(f32) for d in range(rings)]
    arrived = [shift(sums[d].astype(bf16), d) for d in range(1, rings)]
    row_grad = sums[0]
    for part in arrived:
        row_grad = row_grad + part.astype(f32)
    local_grad = lax.dot_general(
        row_grad.astype(bf16),
        join_weight,
        (((1,), (1,)), ((), ())),
        preferred_element_type=f32,
    )
    local_grad, embed = hold((local_grad.astype(bf16), embed))
    conf_grad = lax.all_to_all(
        local_grad.reshape(node_count, per_peer, width), "node", 0, 0, tiled=True
    )
    embed = layer(5, 3, embed)
    conf_grad = conf_grad.astype(f32).reshape(local_conf, width)
    return (embed, loss.reshape(()), conf_grad)


def solution(mesh):
    split = P(("cfg", "node"), None)
    placed = (split, split, P(), P(), P(), P(("cfg", "node")), P("cfg", "node")) + (P(),) * 7
    return jax.shard_map(
        shards,
        mesh=mesh,
        in_specs=placed,
        out_specs=(split, P(), split),
        check_vma=False,
    )
```

```python
import functools
import math

import jax
import jax.numpy as jnp
from jax import lax
from jax.experimental import pallas as pl
from jax.experimental.pallas import tpu as pltpu
from jax.sharding import PartitionSpec as P

HALO = 512
f32 = jnp.float32
bf16 = jnp.bfloat16
VMEM = pl.BlockSpec(memory_space=pltpu.VMEM)
SMEM = pl.BlockSpec(memory_space=pltpu.SMEM)
HBM = pl.BlockSpec(memory_space=pltpu.HBM)


def in_hbm(value):
    return pltpu.with_memory_space_constraint(value, pltpu.HBM)


def half_silu(half):
    tanh = jnp.tanh(half)
    scaled = half * tanh
    return half + scaled, tanh, scaled


def twice_slope(half, tanh, scaled):
    inner = 1.0 + half - scaled
    return inner + tanh * inner


def put_rows(table, first, source):
    rows = source.shape[0]
    value = source[...].astype(f32)
    table[pl.ds(2 * first, rows, stride=2), :] = value[:, :128]
    table[pl.ds(2 * first + 1, rows, stride=2), :] = value[:, 128:]


def put_rims(table, flip, inner, outer):
    end = table.shape[0] // 2 - HALO
    put_rows(table, pl.multiple_of((1 - flip[0]) * end, HALO), inner)
    put_rows(table, pl.multiple_of(flip[0] * end, HALO), outer)


def pair_at(table, at):
    return table[pl.ds(pl.multiple_of(at, 2), 2), :]


def table_kernel(nbrs, picks, feats, sw, bias, table, spots, base, own):
    rows = feats.shape[0]
    step = pl.program_id(0)
    put_rows(table, HALO + pl.multiple_of(step * rows, rows), feats)

    @pl.when(step == pl.num_programs(0) - 1)
    def _():
        count = picks.shape[0]
        own3 = own.reshape(count, 2, 128)

        def body(block, carry):
            values = []
            for j in range(8):
                g = picks[block * 8 + j]
                at = (g >> 7) * 512 + (g & 127)
                for k in range(4):
                    spots[k * count + block * 8 + j] = nbrs[at + 128 * k]
                values.append(pair_at(table, 2 * (HALO + g)))
            for j in range(8):
                own3[block * 8 + j] = values[j]
            return carry

        lax.fori_loop(0, count // 8, body, 0)
        left, right = [own[pl.ds(side, count, stride=2), :].astype(bf16) for side in (0, 1)]
        pre = jnp.dot(left, sw[:128, :], preferred_element_type=f32)
        pre += jnp.dot(right, sw[128:, :], preferred_element_type=f32)
        base[...] = pre + bias[...]


def table_of(nbrs, picks, feats, sw, bias):
    nodes, width = feats.shape
    count = picks.shape[0]
    tile = 512
    return pl.pallas_call(
        table_kernel,
        out_shape=(
            jax.ShapeDtypeStruct((2 * (nodes + 2 * HALO), 128), f32),
            jax.ShapeDtypeStruct((4 * count,), jnp.int32),
            jax.ShapeDtypeStruct((count, width), f32),
        ),
        grid=(nodes // tile,),
        in_specs=[SMEM, SMEM, pl.BlockSpec((tile, width), lambda i: (i, 0)), VMEM, VMEM],
        out_specs=(VMEM, SMEM, VMEM),
        scratch_shapes=[pltpu.VMEM((2 * count, 128), f32)],
        cost_estimate=pl.CostEstimate(flops=1 << 24, transcendentals=0, bytes_accessed=6 << 20),
        compiler_params=pltpu.CompilerParams(vmem_limit_bytes=16 << 20),
        name="window_rows",
    )(nbrs, picks, feats, sw, bias)


def layer_rows(own, left, right, sw, nw, bias):
    pre = jnp.dot(own, sw[...], preferred_element_type=f32) + bias[...]
    pre += jnp.dot(left, nw[:128, :], preferred_element_type=f32)
    pre += jnp.dot(right, nw[128:, :], preferred_element_type=f32)
    return half_silu(0.5 * pre)[0].astype(bf16)


def conf_kernel(flip, spots, outer, inner, nw_hbm, base, given, out, table, acc, nw, sem):
    weights = pltpu.make_async_copy(nw_hbm, nw, sem)
    weights.start()
    put_rims(table, flip, inner, outer)
    count = base.shape[0]
    acc3 = acc.reshape(count, 2, 128)
    some = 16

    def body(block, carry):
        values = []
        for j in range(some):
            near = [pair_at(table, spots[k * count + block * some + j]) for k in range(4)]
            values.append((near[0] + near[1]) + (near[2] + near[3]))
        for j in range(some):
            acc3[block * some + j] = values[j]
        return carry

    lax.fori_loop(0, count // some, body, 0)
    left, right = [(acc[pl.ds(side, count, stride=2), :] * 0.25).astype(bf16) for side in (0, 1)]
    weights.wait()
    pre = base[...] + jnp.dot(left, nw[:128, :], preferred_element_type=f32)
    pre += jnp.dot(right, nw[128:, :], preferred_element_type=f32)
    value = half_silu(0.5 * pre)[0]
    share = out.shape[1]
    for peer in range(out.shape[0]):
        out[peer] = value[peer * share : (peer + 1) * share, :].astype(bf16)


def conf_rows_of(peers, flip, spots, inner, outer, nw, base, table):
    count, width = base.shape
    return pl.pallas_call(
        conf_kernel,
        out_shape=(
            jax.ShapeDtypeStruct((peers, count // peers, width), bf16),
            jax.ShapeDtypeStruct(table.shape, f32),
        ),
        in_specs=[SMEM] * 2 + [VMEM] * 2 + [HBM] + [VMEM] * 2,
        out_specs=(VMEM, VMEM),
        input_output_aliases={6: 1},
        scratch_shapes=[
            pltpu.VMEM((2 * count, 128), f32),
            pltpu.VMEM(nw.shape, bf16),
            pltpu.SemaphoreType.DMA,
        ],
        cost_estimate=pl.CostEstimate(
            flops=4 * count * width * width, transcendentals=0, bytes_accessed=6 << 20
        ),
        compiler_params=pltpu.CompilerParams(vmem_limit_bytes=16 << 20),
        name="conf_rows",
    )(flip, spots, outer, inner, in_hbm(nw), base, table)


def layer_kernel(flip, nbrs, inner, outer, feats, own, sw, nw, bias, *refs):
    out, table, acc = refs[-3:]
    tile = own.shape[0]
    nodes = feats.shape[0]

    @pl.when(pl.program_id(0) == 0)
    def _():
        put_rims(table, flip, inner, outer)
        for start in range(0, nodes, 512):
            put_rows(table, HALO + start, feats.at[start : start + 512, :])

    acc3 = acc.reshape(tile, 2, 128)

    def body(block, carry):
        values = []
        for j in range(128):
            near = [pair_at(table, nbrs[block * 512 + (128 * k + j)]) for k in range(4)]
            values.append((near[0] + near[1]) + (near[2] + near[3]))
        for j in range(128):
            acc3[block * 128 + j] = values[j]
        return carry

    lax.fori_loop(0, tile // 128, body, 0)
    out[...] = layer_rows(
        own[...],
        (acc[pl.ds(0, tile, stride=2), :] * 0.25).astype(bf16),
        (acc[pl.ds(1, tile, stride=2), :] * 0.25).astype(bf16),
        sw,
        nw,
        bias,
    )


def layer_of(first, steps, flip, nbrs, inner, outer, feats, sw, nw, bias, given):
    nodes, width = feats.shape
    tile = 512
    ahead = [] if given is None else [given]
    return pl.pallas_call(
        layer_kernel,
        out_shape=jax.ShapeDtypeStruct((nodes, width), bf16),
        grid=(steps,),
        in_specs=[
            SMEM,
            pl.BlockSpec((4 * tile,), lambda i: (first + i,), memory_space=pltpu.SMEM),
            VMEM,
            VMEM,
            VMEM,
            pl.BlockSpec((tile, width), lambda i: (first + i, 0)),
            VMEM,
            VMEM,
            VMEM,
        ]
        + [HBM] * len(ahead),
        out_specs=pl.BlockSpec((tile, width), lambda i: (first + i, 0)),
        input_output_aliases={9: 0} if ahead else {},
        scratch_shapes=[
            pltpu.VMEM((2 * (nodes + 2 * HALO), 128), f32),
            pltpu.VMEM((2 * tile, 128), f32),
        ],
        cost_estimate=pl.CostEstimate(
            flops=steps * 4 * tile * width * width, transcendentals=0, bytes_accessed=steps << 23
        ),
        compiler_params=pltpu.CompilerParams(vmem_limit_bytes=24 << 20),
        name="graph_layer",
    )(flip, nbrs, inner, outer, feats, feats, sw, nw, bias, *ahead)


def place_of(group, turn):
    return group ^ (2 * (turn & 3) + (turn >> 2))


def prepare_kernel(table, mid, weight, tabh, midh, back):
    tabh[...] = (table[...].astype(f32) * 0.5).astype(bf16)
    middle = mid[...].astype(f32)
    midh[...] = (middle * 0.5).astype(bf16)
    back[...] = jnp.transpose(middle * (weight[...] * 0.25)).astype(bf16)


def prepared(table, mid, weight):
    return pl.pallas_call(
        prepare_kernel,
        out_shape=tuple(jax.ShapeDtypeStruct(x.shape, bf16) for x in (table, mid, mid)),
        in_specs=[VMEM] * 3,
        out_specs=(VMEM,) * 3,
        cost_estimate=pl.CostEstimate(flops=1 << 20, transcendentals=0, bytes_accessed=1 << 19),
        compiler_params=pltpu.CompilerParams(vmem_limit_bytes=8 << 20),
        name="prepare",
    )(table, mid, weight)


def scorer_kernel(groups, final, where, *refs):
    xs, refs = refs[:groups], refs[groups:]
    ids, join, jbias, tabh, midh, back, mbias, weight = refs[:8]
    given, (grads_hbm, sent, base, total, grads, sems) = refs[8:-6], refs[-6:]
    step = pl.program_id(0)
    slot = step & 1
    chunk = xs[0].shape[0]
    configs = ids.shape[0]
    layouts = tabh.shape[0]
    one = jnp.asarray(1.0, bf16)

    @pl.when(step == 0)
    def _():
        for i in range(groups):
            base[i] = 0.5 * (
                jnp.dot(xs[i][...], join[...], preferred_element_type=f32) + jbias[...]
            )
        total[...] = given[0][...] if given else jnp.zeros_like(total)

    def copy_of(turn, place):
        return pltpu.make_async_copy(grads.at[place], grads_hbm.at[turn], sems.at[place])

    @pl.when(step >= 2)
    def _():
        copy_of(step - 2, slot).wait()

    columns = jnp.transpose(ids[...].astype(f32))
    lanes = lax.broadcasted_iota(jnp.int32, (chunk, layouts), 1).astype(f32)
    rows = base[step]
    some = 8
    for first in range(0, configs, some):
        picks = jnp.concatenate(
            [
                jnp.where(columns[:, k : k + 1] == lanes, 1.0, 0.0).astype(bf16)
                for k in range(first, first + some)
            ],
            axis=0,
        )
        half = jnp.dot(picks, tabh[...], preferred_element_type=f32)
        half = (half + jnp.concatenate([rows] * some, axis=0)).astype(bf16)
        tanh = jnp.tanh(half)
        above = one + tanh
        slope = above * (one + half * (one - tanh))
        outer = jnp.dot(half * above, midh[...], preferred_element_type=f32)
        outer = (outer + 0.5 * mbias[...]).astype(bf16)
        tanh2 = jnp.tanh(outer)
        above2 = one + tanh2
        act2 = (outer * above2).astype(f32)
        slope2 = above2 * (one + outer * (one - tanh2))
        for q in range(some):
            part = act2[q * chunk : (q + 1) * chunk, :]
            total[first + q : first + q + 1, :] += jnp.sum(part, axis=0, keepdims=True)
        grad = jnp.dot(slope2, back[...], preferred_element_type=f32).astype(bf16) * slope
        for q in range(some):
            grads[slot, first + q] = grad[q * chunk : (q + 1) * chunk, :]

    copy_of(step, slot).start()

    @pl.when(step == groups - 1)
    def _():
        if final:
            scores = jnp.sum(total[...] * weight[...], axis=1, keepdims=True)
            lane = lax.broadcasted_iota(jnp.int32, (configs, 128), 1)
            sub = lax.broadcasted_iota(jnp.int32, (configs, 128), 0)
            spread = jnp.where(lane == sub + where[0] * configs, scores, 0.0)
            sent[...] = jnp.broadcast_to(jnp.sum(spread, axis=0, keepdims=True), sent.shape)
        else:
            sent[...] = total[...]
        copy_of(step - 1, 1 - slot).wait()
        copy_of(step, slot).wait()


def scorer_of(final, turns, where, xs, ids, join, jbias, weights, mbias, weight, given):
    groups = len(xs)
    configs = ids.shape[0]
    chunk, width = xs[0].shape
    hidden = join.shape[1]
    start, stride = turns
    summed = final if final else (configs, hidden)
    return pl.pallas_call(
        functools.partial(scorer_kernel, groups, final),
        out_shape=(
            pltpu.HBM((groups, configs, chunk, hidden), bf16),
            jax.ShapeDtypeStruct(summed, f32),
        ),
        grid_spec=pltpu.PrefetchScalarGridSpec(
            num_scalar_prefetch=1,
            grid=(groups,),
            in_specs=[VMEM] * groups
            + [
                pl.BlockSpec(
                    (configs, chunk), lambda i, where: (0, place_of(where[0], start + stride * i))
                )
            ]
            + [VMEM] * (7 + len(given)),
            out_specs=(HBM, VMEM),
            scratch_shapes=[
                pltpu.VMEM((groups, chunk, hidden), f32),
                pltpu.VMEM((configs, hidden), f32),
                pltpu.VMEM((2, configs, chunk, hidden), bf16),
                pltpu.SemaphoreType.DMA((2,)),
            ],
        ),
        cost_estimate=pl.CostEstimate(
            flops=6 * groups * configs * chunk * width * width,
            transcendentals=2 * groups * configs * chunk * width,
            bytes_accessed=groups << 20,
        ),
        compiler_params=pltpu.CompilerParams(vmem_limit_bytes=24 << 20),
        name="scorer",
    )(where, *xs, ids, join, jbias, *weights, mbias, weight, *given)


def weighted(coef, grads, out):
    configs, chunk, hidden = grads.shape
    some = 32
    for start in range(0, chunk, some):
        rows = grads[0, start : start + some, :].astype(f32) * coef[0:1, :]
        for k in range(1, configs):
            rows = rows + grads[k, start : start + some, :].astype(f32) * coef[k : k + 1, :]
        out[start : start + some, :] = rows.astype(bf16)


def fetches(pair, later, which, grads, sems):
    sources = [pair.at[which]] + [later.at[d] for d in range(grads.shape[0] - 1)]
    return [
        pltpu.make_async_copy(source, grads.at[d], sems.at[d]) for d, source in enumerate(sources)
    ]


def ranking_kernel(scale, where, got, pairs, pair, later, loss, coef, out, column, grads, sems):
    half, configs, chunk, hidden = grads.shape
    copies = fetches(pair, later, 1, grads, sems)
    for copy in copies:
        copy.start()
    score = jnp.sum(got[...], axis=0, keepdims=True) * scale
    lane = lax.broadcasted_iota(jnp.int32, (128, 128), 1)
    sub = lax.broadcasted_iota(jnp.int32, (128, 128), 0)
    score = jnp.sum(jnp.where(lane == sub, score, 0.0), axis=1, keepdims=True)
    count = pairs.shape[1]
    ids = lax.broadcasted_iota(jnp.int32, (128, count), 0)
    second = jnp.where(pairs[1:2, :] == ids, 1.0, 0.0)
    signed = second - jnp.where(pairs[0:1, :] == ids, 1.0, 0.0)
    gap = jnp.sum(signed * score, axis=0, keepdims=True)
    fade = jnp.exp(-jnp.abs(gap))
    soft = jnp.maximum(gap, 0.0) + jnp.log1p(fade)
    loss[...] = jnp.sum(soft, axis=1, keepdims=True) * (1.0 / count)
    slope = jnp.where(gap >= 0.0, 1.0, fade) / (1.0 + fade)
    grad = jnp.sum(slope * signed, axis=1, keepdims=True) * (65536.0 * scale / count)
    column[...] = jnp.broadcast_to(grad, column.shape)
    coef[...] = column[pl.ds(pl.multiple_of(where[0] * configs, configs), configs), :]
    for d in range(half):
        copies[d].wait()
        weighted(coef, grads.at[d], out.at[d])


def ranking_of(scale, where, got, pairs, pair, later):
    half, configs, chunk, hidden = later.shape
    half += 1
    return pl.pallas_call(
        functools.partial(ranking_kernel, scale),
        out_shape=(
            jax.ShapeDtypeStruct((1, 1), f32),
            jax.ShapeDtypeStruct((configs, hidden), f32),
            jax.ShapeDtypeStruct((half, chunk, hidden), bf16),
        ),
        in_specs=[SMEM, VMEM, VMEM, HBM, HBM],
        out_specs=(VMEM, VMEM, VMEM),
        scratch_shapes=[
            pltpu.VMEM((128, hidden), f32),
            pltpu.VMEM((half, configs, chunk, hidden), bf16),
            pltpu.SemaphoreType.DMA((half,)),
        ],
        cost_estimate=pl.CostEstimate(flops=1 << 24, transcendentals=0, bytes_accessed=6 << 20),
        compiler_params=pltpu.CompilerParams(vmem_limit_bytes=16 << 20),
        name="ranking",
    )(where, got, pairs, in_hbm(pair), in_hbm(later))


def rest_kernel(coef, pair, later, out, grads, sems):
    copies = fetches(pair, later, 0, grads, sems)
    for copy in copies:
        copy.start()
    for d, copy in enumerate(copies):
        copy.wait()
        weighted(coef, grads.at[d], out.at[d])


def rest_of(coef, pair, later):
    half, configs, chunk, hidden = later.shape
    half += 1
    return pl.pallas_call(
        rest_kernel,
        out_shape=jax.ShapeDtypeStruct((half, chunk, hidden), bf16),
        in_specs=[VMEM, HBM, HBM],
        out_specs=VMEM,
        scratch_shapes=[
            pltpu.VMEM((half, configs, chunk, hidden), bf16),
            pltpu.SemaphoreType.DMA((half,)),
        ],
        cost_estimate=pl.CostEstimate(flops=1 << 24, transcendentals=0, bytes_accessed=6 << 20),
        compiler_params=pltpu.CompilerParams(vmem_limit_bytes=16 << 20),
        name="rest",
    )(coef, in_hbm(pair), in_hbm(later))


def shards(
    node_feats,
    neighbors,
    self_weight,
    neighbor_weight,
    sage_bias,
    conf_index,
    layout_ids,
    join_weight,
    layout_table,
    join_bias,
    mid_weight,
    mid_bias,
    score_weight,
    config_pairs,
):
    both = ("cfg", "node")
    devices = lax.axis_size(both)
    node_count = lax.axis_size("node")
    group_count = lax.axis_size("cfg")
    rings = group_count // 2
    local_conf = conf_index.shape[0]
    width = node_feats.shape[1]
    per_peer = local_conf // node_count
    scale = 1.0 / math.sqrt(layout_ids.shape[1] * node_count)
    group = lax.axis_index("cfg")

    nodes, near = neighbors.shape
    spot = lax.axis_index("node")
    flip = (spot & 1).reshape(1)

    def trade(rows, partner):
        pairs = [(i, partner(i)) for i in range(devices) if 0 <= partner(i) < devices]
        return lax.ppermute(rows, both, pairs)

    def rim(feats, odd):
        return lax.dynamic_slice_in_dim(feats, odd * (nodes - HALO), HALO, 0)

    outer = trade(rim(node_feats, spot & 1), lambda i: i + 1 if i % 2 else i - 1)
    inner = trade(rim(node_feats, 1 - (spot & 1)), lambda i: i ^ 1)
    nbrs = (2 * neighbors).T.reshape(near, nodes // 128, 128).transpose(1, 0, 2).reshape(-1)
    bias = sage_bias.reshape(1, -1)
    hold = lax.optimization_barrier

    table, spots, base = table_of(nbrs, conf_index, node_feats, self_weight, bias)
    conf_src, _ = conf_rows_of(
        node_count, flip, spots, inner, outer, neighbor_weight, base, table
    )

    def layer(first, steps, given):
        return layer_of(
            first,
            steps,
            flip,
            nbrs,
            inner,
            outer,
            node_feats,
            self_weight,
            neighbor_weight,
            bias,
            given,
        )

    swap = [(i, i ^ 1) for i in range(group_count)]

    def shift(value, by):
        return lax.ppermute(value, "cfg", [(i, i ^ (2 * by)) for i in range(group_count)])

    mine = lax.all_to_all(conf_src, "node", 0, 0, tiled=True)
    embed = layer(0, 2, None)
    weight = score_weight.reshape(1, -1)
    weights = prepared(layout_table, mid_weight, weight)
    mine, embed, *weights = hold((mine, embed, *weights))
    mine = mine.reshape(local_conf, width)
    others = [shift(mine, by) for by in range(1, rings)]
    where = group.reshape(1)

    def scorer(final, turns, xs, given):
        return scorer_of(
            final,
            turns,
            where,
            xs,
            layout_ids,
            join_weight,
            join_bias.reshape(1, -1),
            weights,
            mid_bias.reshape(1, -1),
            weight,
            given,
        )

    pair, total = scorer(None, (0, rings), [mine, lax.ppermute(mine, "cfg", swap)], [])
    others = list(hold((*others, total)))
    total = others.pop()
    swapped = [lax.ppermute(x, "cfg", swap) for x in others]
    own, total = scorer(None, (1, 1), others, [total])
    swapped = list(hold((*swapped, total)))
    total = swapped.pop()
    other, sent = scorer((devices, 128), (rings + 1, 1), swapped, [total])
    sent, embed = hold((sent, embed))
    got = lax.all_to_all(sent.reshape(devices, 1, 128), both, 0, 0, tiled=True)
    embed = layer(2, 4, embed)
    got, embed = hold((got, embed))
    loss, coef, away = ranking_of(
        scale, where, got.reshape(devices, 128), config_pairs.T, pair, other
    )
    came = lax.ppermute(away, "cfg", swap)
    kept = rest_of(coef, pair, own)
    sums = [kept[d].astype(f32) + came[d].astype(f32) for d in range(rings)]
    arrived = [shift(sums[d].astype(bf16), d) for d in range(1, rings)]
    row_grad = sums[0]
    for part in arrived:
        row_grad = row_grad + part.astype(f32)
    local_grad = lax.dot_general(
        row_grad.astype(bf16),
        join_weight,
        (((1,), (1,)), ((), ())),
        preferred_element_type=f32,
    )
    local_grad, embed = hold((local_grad.astype(bf16), embed))
    conf_grad = lax.all_to_all(
        local_grad.reshape(node_count, per_peer, width), "node", 0, 0, tiled=True
    )
    embed = layer(6, 2, embed)
    conf_grad = conf_grad.astype(f32).reshape(local_conf, width)
    return (embed, loss.reshape(()), conf_grad)


def solution(mesh):
    split = P(("cfg", "node"), None)
    placed = (split, split, P(), P(), P(), P(("cfg", "node")), P("cfg", "node")) + (P(),) * 7
    return jax.shard_map(
        shards,
        mesh=mesh,
        in_specs=placed,
        out_specs=(split, P(), split),
        check_vma=False,
    )
```

```python
import functools
import math

import jax
import jax.numpy as jnp
from jax import lax
from jax.experimental import pallas as pl
from jax.experimental.pallas import tpu as pltpu
from jax.sharding import PartitionSpec as P

HALO = 512
f32 = jnp.float32
bf16 = jnp.bfloat16
VMEM = pl.BlockSpec(memory_space=pltpu.VMEM)
SMEM = pl.BlockSpec(memory_space=pltpu.SMEM)
HBM = pl.BlockSpec(memory_space=pltpu.HBM)


def in_hbm(value):
    return pltpu.with_memory_space_constraint(value, pltpu.HBM)


def half_silu(half):
    tanh = jnp.tanh(half)
    scaled = half * tanh
    return half + scaled, tanh, scaled


def twice_slope(half, tanh, scaled):
    inner = 1.0 + half - scaled
    return inner + tanh * inner


def halves_swapped(first, second):
    low = lax.broadcasted_iota(jnp.int32, first.shape, 1) < 4
    upper = jnp.where(low, first, pltpu.roll(second, 4, 1))
    lower = jnp.where(low, pltpu.roll(first, 4, 1), second)
    return upper, lower


def pack(value):
    rows = value.shape[0]
    sides = [value[:, at : at + 128].reshape(rows // 8, 8, 128) for at in (0, 128)]
    even, odd = halves_swapped(*sides)
    return jnp.stack([even, odd], axis=1).reshape(rows // 4, 8, 128)


def unpack(value):
    groups = value.shape[0]
    pairs = value.reshape(groups // 2, 2, 8, 128)
    left, right = halves_swapped(pairs[:, 0], pairs[:, 1])
    return jnp.concatenate([x.reshape(groups * 4, 128) for x in (left, right)], axis=1)


def put_rows(table, first, source):
    rows = source.shape[0]
    value = source[...].astype(f32)
    table[pl.ds(2 * first, rows, stride=2), :] = value[:, :128]
    table[pl.ds(2 * first + 1, rows, stride=2), :] = value[:, 128:]


def put_rims(table, flip, inner, outer):
    end = table.shape[0] // 2 - HALO
    put_rows(table, pl.multiple_of((1 - flip[0]) * end, HALO), inner)
    put_rows(table, pl.multiple_of(flip[0] * end, HALO), outer)


def pair_at(table, at):
    return table[pl.ds(pl.multiple_of(at, 2), 2), :]


def table_kernel(feats, table):
    rows = feats.shape[0]
    put_rows(table, HALO + pl.multiple_of(pl.program_id(0) * rows, rows), feats)


def table_of(feats):
    nodes, width = feats.shape
    tile = 512
    return pl.pallas_call(
        table_kernel,
        out_shape=jax.ShapeDtypeStruct((2 * (nodes + 2 * HALO), 128), f32),
        grid=(nodes // tile,),
        in_specs=[pl.BlockSpec((tile, width), lambda i: (i, 0))],
        out_specs=VMEM,
        cost_estimate=pl.CostEstimate(flops=1 << 20, transcendentals=0, bytes_accessed=6 << 20),
        compiler_params=pltpu.CompilerParams(vmem_limit_bytes=16 << 20),
        name="window_rows",
    )(feats)


def layer_rows(own_left, own_right, left, right, sw, nw, bias, kind=bf16):
    pre = jnp.dot(own_left, sw[:128, :], preferred_element_type=f32)
    pre += jnp.dot(own_right, sw[128:, :], preferred_element_type=f32)
    pre += jnp.dot(left, nw[:128, :], preferred_element_type=f32)
    pre += jnp.dot(right, nw[128:, :], preferred_element_type=f32)
    return half_silu(0.5 * (pre + bias[...]))[0].astype(kind)


def conf_kernel(flip, nbrs, picks, outer, inner, *refs):
    sw_hbm, nw_hbm, bias_hbm, given, out, table, own, acc, sw, nw, bias, sems = refs
    copies = [
        pltpu.make_async_copy(source, target, sems.at[i])
        for i, (source, target) in enumerate(((sw_hbm, sw), (nw_hbm, nw), (bias_hbm, bias)))
    ]
    for copy in copies:
        copy.start()
    put_rims(table, flip, inner, outer)
    count = picks.shape[0]
    own3 = own.reshape(count, 2, 128)
    acc3 = acc.reshape(count, 2, 128)

    def body(block, carry):
        values = []
        for j in range(8):
            g = picks[block * 8 + j]
            at = (g >> 7) * 512 + (g & 127)
            near = [pair_at(table, nbrs[at + 128 * k]) for k in range(4)]
            values.append((pair_at(table, 2 * (HALO + g)), (near[0] + near[1]) + (near[2] + near[3])))
        for j in range(8):
            own3[block * 8 + j], acc3[block * 8 + j] = values[j]
        return carry

    lax.fori_loop(0, count // 8, body, 0)
    halves = [ref[pl.ds(side, count, stride=2), :] for ref in (own, acc) for side in (0, 1)]
    for copy in copies:
        copy.wait()
    value = layer_rows(
        halves[0].astype(bf16),
        halves[1].astype(bf16),
        (halves[2] * 0.25).astype(bf16),
        (halves[3] * 0.25).astype(bf16),
        sw,
        nw,
        bias,
        f32,
    )
    out[...] = pack(value).astype(bf16)


def conf_rows_of(flip, nbrs, picks, inner, outer, sw, nw, bias, table):
    count = picks.shape[0]
    width = sw.shape[0]
    return pl.pallas_call(
        conf_kernel,
        out_shape=(
            jax.ShapeDtypeStruct((count // 4, 8, width // 2), bf16),
            jax.ShapeDtypeStruct(table.shape, f32),
        ),
        in_specs=[SMEM] * 3 + [VMEM] * 2 + [HBM] * 3 + [VMEM],
        out_specs=(VMEM, VMEM),
        input_output_aliases={8: 1},
        scratch_shapes=[
            pltpu.VMEM((2 * count, 128), f32),
            pltpu.VMEM((2 * count, 128), f32),
            pltpu.VMEM(sw.shape, bf16),
            pltpu.VMEM(nw.shape, bf16),
            pltpu.VMEM(bias.shape, f32),
            pltpu.SemaphoreType.DMA((3,)),
        ],
        cost_estimate=pl.CostEstimate(
            flops=4 * count * width * width, transcendentals=0, bytes_accessed=6 << 20
        ),
        compiler_params=pltpu.CompilerParams(vmem_limit_bytes=16 << 20),
        name="conf_rows",
    )(flip, nbrs, picks, outer, inner, in_hbm(sw), in_hbm(nw), in_hbm(bias), table)


def layer_kernel(flip, nbrs, inner, outer, feats, own, sw, nw, bias, *refs):
    out, table, acc = refs[-3:]
    tile = own.shape[0]
    nodes = feats.shape[0]

    @pl.when(pl.program_id(0) == 0)
    def _():
        put_rims(table, flip, inner, outer)
        for start in range(0, nodes, 512):
            put_rows(table, HALO + start, feats.at[start : start + 512, :])

    acc3 = acc.reshape(tile, 2, 128)

    def body(block, carry):
        values = []
        for j in range(128):
            near = [pair_at(table, nbrs[block * 512 + (128 * k + j)]) for k in range(4)]
            values.append((near[0] + near[1]) + (near[2] + near[3]))
        for j in range(128):
            acc3[block * 128 + j] = values[j]
        return carry

    lax.fori_loop(0, tile // 128, body, 0)
    rows = own[...]
    out[...] = layer_rows(
        rows[:, :128],
        rows[:, 128:],
        (acc[pl.ds(0, tile, stride=2), :] * 0.25).astype(bf16),
        (acc[pl.ds(1, tile, stride=2), :] * 0.25).astype(bf16),
        sw,
        nw,
        bias,
    )


def layer_of(first, steps, flip, nbrs, inner, outer, feats, sw, nw, bias, given):
    nodes, width = feats.shape
    tile = 512
    ahead = [] if given is None else [given]
    return pl.pallas_call(
        layer_kernel,
        out_shape=jax.ShapeDtypeStruct((nodes, width), bf16),
        grid=(steps,),
        in_specs=[
            SMEM,
            pl.BlockSpec((4 * tile,), lambda i: (first + i,), memory_space=pltpu.SMEM),
            VMEM,
            VMEM,
            VMEM,
            pl.BlockSpec((tile, width), lambda i: (first + i, 0)),
            VMEM,
            VMEM,
            VMEM,
        ]
        + [HBM] * len(ahead),
        out_specs=pl.BlockSpec((tile, width), lambda i: (first + i, 0)),
        input_output_aliases={9: 0} if ahead else {},
        scratch_shapes=[
            pltpu.VMEM((2 * (nodes + 2 * HALO), 128), f32),
            pltpu.VMEM((2 * tile, 128), f32),
        ],
        cost_estimate=pl.CostEstimate(
            flops=steps * 4 * tile * width * width, transcendentals=0, bytes_accessed=steps << 23
        ),
        compiler_params=pltpu.CompilerParams(vmem_limit_bytes=24 << 20),
        name="graph_layer",
    )(flip, nbrs, inner, outer, feats, feats, sw, nw, bias, *ahead)


def place_of(group, turn):
    return group ^ (2 * (turn & 3) + (turn >> 2))


def prepare_kernel(table, mid, weight, tabh, midh, back):
    tabh[...] = (table[...].astype(f32) * 0.5).astype(bf16)
    middle = mid[...].astype(f32)
    midh[...] = (middle * 0.5).astype(bf16)
    back[...] = jnp.transpose(middle * (weight[...] * 0.25)).astype(bf16)


def prepared(table, mid, weight):
    return pl.pallas_call(
        prepare_kernel,
        out_shape=tuple(jax.ShapeDtypeStruct(x.shape, bf16) for x in (table, mid, mid)),
        in_specs=[VMEM] * 3,
        out_specs=(VMEM,) * 3,
        cost_estimate=pl.CostEstimate(flops=1 << 20, transcendentals=0, bytes_accessed=1 << 19),
        compiler_params=pltpu.CompilerParams(vmem_limit_bytes=8 << 20),
        name="prepare",
    )(table, mid, weight)


def scorer_kernel(groups, final, where, *refs):
    xs, refs = refs[:groups], refs[groups:]
    ids, join, jbias, tabh, midh, back, mbias, weight = refs[:8]
    given, (grads_hbm, sent, base, total, grads, sems) = refs[8:-6], refs[-6:]
    step = pl.program_id(0)
    slot = step & 1
    chunk = base.shape[1]
    configs = ids.shape[0]
    layouts = tabh.shape[0]
    one = jnp.asarray(1.0, bf16)

    @pl.when(step == 0)
    def _():
        for i in range(groups):
            base[i] = 0.5 * (
                jnp.dot(
                    unpack(xs[i][...].astype(f32)).astype(bf16),
                    join[...],
                    preferred_element_type=f32,
                )
                + jbias[...]
            )
        total[...] = given[0][...] if given else jnp.zeros_like(total)

    def copy_of(turn, place):
        return pltpu.make_async_copy(grads.at[place], grads_hbm.at[turn], sems.at[place])

    @pl.when(step >= 2)
    def _():
        copy_of(step - 2, slot).wait()

    columns = jnp.transpose(ids[...].astype(f32))
    lanes = lax.broadcasted_iota(jnp.int32, (chunk, layouts), 1).astype(f32)
    rows = base[step]
    some = 8
    for first in range(0, configs, some):
        picks = jnp.concatenate(
            [
                jnp.where(columns[:, k : k + 1] == lanes, 1.0, 0.0).astype(bf16)
                for k in range(first, first + some)
            ],
            axis=0,
        )
        half = jnp.dot(picks, tabh[...], preferred_element_type=f32)
        half = (half + jnp.concatenate([rows] * some, axis=0)).astype(bf16)
        tanh = jnp.tanh(half)
        above = one + tanh
        slope = above * (one + half * (one - tanh))
        outer = jnp.dot(half * above, midh[...], preferred_element_type=f32)
        outer = (outer + 0.5 * mbias[...]).astype(bf16)
        tanh2 = jnp.tanh(outer)
        above2 = one + tanh2
        act2 = (outer * above2).astype(f32)
        slope2 = above2 * (one + outer * (one - tanh2))
        for q in range(some):
            part = act2[q * chunk : (q + 1) * chunk, :]
            total[first + q : first + q + 1, :] += jnp.sum(part, axis=0, keepdims=True)
        grad = jnp.dot(slope2, back[...], preferred_element_type=f32).astype(bf16) * slope
        for q in range(some):
            grads[slot, first + q] = grad[q * chunk : (q + 1) * chunk, :]

    copy_of(step, slot).start()

    @pl.when(step == groups - 1)
    def _():
        if final:
            scores = jnp.sum(total[...] * weight[...], axis=1, keepdims=True)
            lane = lax.broadcasted_iota(jnp.int32, (configs, 128), 1)
            sub = lax.broadcasted_iota(jnp.int32, (configs, 128), 0)
            spread = jnp.where(lane == sub + where[0] * configs, scores, 0.0)
            sent[...] = jnp.broadcast_to(jnp.sum(spread, axis=0, keepdims=True), sent.shape)
        else:
            sent[...] = total[...]
        copy_of(step - 1, 1 - slot).wait()
        copy_of(step, slot).wait()


def scorer_of(final, turns, where, xs, ids, join, jbias, weights, mbias, weight, given):
    groups = len(xs)
    configs = ids.shape[0]
    chunk = xs[0].shape[0] * 4
    width, hidden = join.shape
    start, stride = turns
    summed = final if final else (configs, hidden)
    return pl.pallas_call(
        functools.partial(scorer_kernel, groups, final),
        out_shape=(
            pltpu.HBM((groups, configs, chunk, hidden), bf16),
            jax.ShapeDtypeStruct(summed, f32),
        ),
        grid_spec=pltpu.PrefetchScalarGridSpec(
            num_scalar_prefetch=1,
            grid=(groups,),
            in_specs=[VMEM] * groups
            + [
                pl.BlockSpec(
                    (configs, chunk), lambda i, where: (0, place_of(where[0], start + stride * i))
                )
            ]
            + [VMEM] * (7 + len(given)),
            out_specs=(HBM, VMEM),
            scratch_shapes=[
                pltpu.VMEM((groups, chunk, hidden), f32),
                pltpu.VMEM((configs, hidden), f32),
                pltpu.VMEM((2, configs, chunk, hidden), bf16),
                pltpu.SemaphoreType.DMA((2,)),
            ],
        ),
        cost_estimate=pl.CostEstimate(
            flops=6 * groups * configs * chunk * width * width,
            transcendentals=2 * groups * configs * chunk * width,
            bytes_accessed=groups << 20,
        ),
        compiler_params=pltpu.CompilerParams(vmem_limit_bytes=24 << 20),
        name="scorer",
    )(where, *xs, ids, join, jbias, *weights, mbias, weight, *given)


def weighted(coef, grads, out):
    configs, chunk, hidden = grads.shape
    some = 32
    for start in range(0, chunk, some):
        rows = grads[0, start : start + some, :].astype(f32) * coef[0:1, :]
        for k in range(1, configs):
            rows = rows + grads[k, start : start + some, :].astype(f32) * coef[k : k + 1, :]
        out[start : start + some, :] = rows.astype(bf16)


def fetches(pair, later, which, grads, sems):
    sources = [pair.at[which]] + [later.at[d] for d in range(grads.shape[0] - 1)]
    return [
        pltpu.make_async_copy(source, grads.at[d], sems.at[d]) for d, source in enumerate(sources)
    ]


def ranking_kernel(scale, where, got, pairs, pair, later, loss, coef, out, column, grads, sems):
    half, configs, chunk, hidden = grads.shape
    copies = fetches(pair, later, 1, grads, sems)
    for copy in copies:
        copy.start()
    score = jnp.sum(got[...], axis=0, keepdims=True) * scale
    lane = lax.broadcasted_iota(jnp.int32, (128, 128), 1)
    sub = lax.broadcasted_iota(jnp.int32, (128, 128), 0)
    score = jnp.sum(jnp.where(lane == sub, score, 0.0), axis=1, keepdims=True)
    count = pairs.shape[1]
    ids = lax.broadcasted_iota(jnp.int32, (128, count), 0)
    second = jnp.where(pairs[1:2, :] == ids, 1.0, 0.0)
    signed = second - jnp.where(pairs[0:1, :] == ids, 1.0, 0.0)
    gap = jnp.sum(signed * score, axis=0, keepdims=True)
    fade = jnp.exp(-jnp.abs(gap))
    soft = jnp.maximum(gap, 0.0) + jnp.log1p(fade)
    loss[...] = jnp.sum(soft, axis=1, keepdims=True) * (1.0 / count)
    slope = jnp.where(gap >= 0.0, 1.0, fade) / (1.0 + fade)
    grad = jnp.sum(slope * signed, axis=1, keepdims=True) * (65536.0 * scale / count)
    column[...] = jnp.broadcast_to(grad, column.shape)
    coef[...] = column[pl.ds(pl.multiple_of(where[0] * configs, configs), configs), :]
    for d in range(half):
        copies[d].wait()
        weighted(coef, grads.at[d], out.at[d])


def ranking_of(scale, where, got, pairs, pair, later):
    half, configs, chunk, hidden = later.shape
    half += 1
    return pl.pallas_call(
        functools.partial(ranking_kernel, scale),
        out_shape=(
            jax.ShapeDtypeStruct((1, 1), f32),
            jax.ShapeDtypeStruct((configs, hidden), f32),
            jax.ShapeDtypeStruct((half, chunk, hidden), bf16),
        ),
        in_specs=[SMEM, VMEM, VMEM, HBM, HBM],
        out_specs=(VMEM, VMEM, VMEM),
        scratch_shapes=[
            pltpu.VMEM((128, hidden), f32),
            pltpu.VMEM((half, configs, chunk, hidden), bf16),
            pltpu.SemaphoreType.DMA((half,)),
        ],
        cost_estimate=pl.CostEstimate(flops=1 << 24, transcendentals=0, bytes_accessed=6 << 20),
        compiler_params=pltpu.CompilerParams(vmem_limit_bytes=16 << 20),
        name="ranking",
    )(where, got, pairs, in_hbm(pair), in_hbm(later))


def rest_kernel(coef, pair, later, out, grads, sems):
    copies = fetches(pair, later, 0, grads, sems)
    for copy in copies:
        copy.start()
    for d, copy in enumerate(copies):
        copy.wait()
        weighted(coef, grads.at[d], out.at[d])


def rest_of(coef, pair, later):
    half, configs, chunk, hidden = later.shape
    half += 1
    return pl.pallas_call(
        rest_kernel,
        out_shape=jax.ShapeDtypeStruct((half, chunk, hidden), bf16),
        in_specs=[VMEM, HBM, HBM],
        out_specs=VMEM,
        scratch_shapes=[
            pltpu.VMEM((half, configs, chunk, hidden), bf16),
            pltpu.SemaphoreType.DMA((half,)),
        ],
        cost_estimate=pl.CostEstimate(flops=1 << 24, transcendentals=0, bytes_accessed=6 << 20),
        compiler_params=pltpu.CompilerParams(vmem_limit_bytes=16 << 20),
        name="rest",
    )(coef, in_hbm(pair), in_hbm(later))


def finish_kernel(kept, came, *refs):
    arrived, (join, out) = refs[:-2], refs[-2:]
    rows = kept[0].astype(f32) + came[0].astype(f32)
    for part in arrived:
        rows = rows + part[...].astype(f32)
    value = lax.dot_general(
        rows.astype(bf16), join[...], (((1,), (1,)), ((), ())), preferred_element_type=f32
    )
    out[...] = pack(value).astype(bf16)


def finish_of(kept, came, arrived, join):
    rows, width = kept.shape[1], join.shape[0]
    return pl.pallas_call(
        finish_kernel,
        out_shape=jax.ShapeDtypeStruct((rows // 4, 8, width // 2), bf16),
        in_specs=[VMEM] * (3 + len(arrived)),
        out_specs=VMEM,
        cost_estimate=pl.CostEstimate(flops=1 << 24, transcendentals=0, bytes_accessed=1 << 19),
        compiler_params=pltpu.CompilerParams(vmem_limit_bytes=8 << 20),
        name="finish",
    )(kept, came, *arrived, join)


def returned_kernel(value, out):
    out[...] = unpack(value[...].astype(f32))


def returned_of(value):
    groups = value.shape[0]
    return pl.pallas_call(
        returned_kernel,
        out_shape=jax.ShapeDtypeStruct((groups * 4, 256), f32),
        in_specs=[VMEM],
        out_specs=VMEM,
        cost_estimate=pl.CostEstimate(flops=1 << 16, transcendentals=0, bytes_accessed=1 << 18),
        compiler_params=pltpu.CompilerParams(vmem_limit_bytes=8 << 20),
        name="returned",
    )(value)


def shards(
    node_feats,
    neighbors,
    self_weight,
    neighbor_weight,
    sage_bias,
    conf_index,
    layout_ids,
    join_weight,
    layout_table,
    join_bias,
    mid_weight,
    mid_bias,
    score_weight,
    config_pairs,
):
    both = ("cfg", "node")
    devices = lax.axis_size(both)
    node_count = lax.axis_size("node")
    group_count = lax.axis_size("cfg")
    rings = group_count // 2
    scale = 1.0 / math.sqrt(layout_ids.shape[1] * node_count)
    group = lax.axis_index("cfg")

    nodes, near = neighbors.shape
    spot = lax.axis_index("node")
    flip = (spot & 1).reshape(1)

    def trade(rows, partner):
        pairs = [(i, partner(i)) for i in range(devices) if 0 <= partner(i) < devices]
        return lax.ppermute(rows, both, pairs)

    def rim(feats, odd):
        return lax.dynamic_slice_in_dim(feats, odd * (nodes - HALO), HALO, 0)

    outer = trade(rim(node_feats, spot & 1), lambda i: i + 1 if i % 2 else i - 1)
    inner = trade(rim(node_feats, 1 - (spot & 1)), lambda i: i ^ 1)
    nbrs = (2 * neighbors).T.reshape(near, nodes // 128, 128).transpose(1, 0, 2).reshape(-1)
    bias = sage_bias.reshape(1, -1)
    hold = lax.optimization_barrier

    table = table_of(node_feats)
    conf_src, _ = conf_rows_of(
        flip,
        nbrs,
        conf_index,
        inner,
        outer,
        self_weight,
        neighbor_weight,
        bias,
        table,
    )

    def layer(first, steps, given):
        return layer_of(
            first,
            steps,
            flip,
            nbrs,
            inner,
            outer,
            node_feats,
            self_weight,
            neighbor_weight,
            bias,
            given,
        )

    swap = [(i, i ^ 1) for i in range(group_count)]

    def shift(value, by):
        return lax.ppermute(value, "cfg", [(i, i ^ (2 * by)) for i in range(group_count)])

    mine = lax.all_to_all(conf_src, "node", 0, 0, tiled=True)
    embed = layer(0, 2, None)
    weight = score_weight.reshape(1, -1)
    weights = prepared(layout_table, mid_weight, weight)
    mine, embed, *weights = hold((mine, embed, *weights))
    others = [shift(mine, by) for by in range(1, rings)]
    where = group.reshape(1)

    def scorer(final, turns, xs, given):
        return scorer_of(
            final,
            turns,
            where,
            xs,
            layout_ids,
            join_weight,
            join_bias.reshape(1, -1),
            weights,
            mid_bias.reshape(1, -1),
            weight,
            given,
        )

    pair, total = scorer(None, (0, rings), [mine, lax.ppermute(mine, "cfg", swap)], [])
    others = list(hold((*others, total)))
    total = others.pop()
    swapped = [lax.ppermute(x, "cfg", swap) for x in others]
    own, total = scorer(None, (1, 1), others, [total])
    swapped = list(hold((*swapped, total)))
    total = swapped.pop()
    other, sent = scorer((devices, 128), (rings + 1, 1), swapped, [total])
    sent, embed = hold((sent, embed))
    got = lax.all_to_all(sent.reshape(devices, 1, 128), both, 0, 0, tiled=True)
    embed = layer(2, 4, embed)
    got, embed = hold((got, embed))
    loss, coef, away = ranking_of(
        scale, where, got.reshape(devices, 128), config_pairs.T, pair, other
    )
    came = lax.ppermute(away, "cfg", swap)
    kept = rest_of(coef, pair, own)
    sums = [(kept[d].astype(f32) + came[d].astype(f32)).astype(bf16) for d in range(1, rings)]
    arrived = [shift(part, by) for by, part in enumerate(sums, 1)]
    local_grad, embed = hold((finish_of(kept, came, arrived, join_weight), embed))
    conf_grad = lax.all_to_all(local_grad, "node", 0, 0, tiled=True)
    embed = layer(6, 2, embed)
    conf_grad = returned_of(conf_grad)
    return (embed, loss.reshape(()), conf_grad)


def solution(mesh):
    split = P(("cfg", "node"), None)
    placed = (split, split, P(), P(), P(), P(("cfg", "node")), P("cfg", "node")) + (P(),) * 7
    return jax.shard_map(
        shards,
        mesh=mesh,
        in_specs=placed,
        out_specs=(split, P(), split),
        check_vma=False,
    )
```

```python
import functools
import math

import jax
import jax.numpy as jnp
from jax import lax
from jax.experimental import pallas as pl
from jax.experimental.pallas import tpu as pltpu
from jax.sharding import PartitionSpec as P

HALO = 512
f32 = jnp.float32
bf16 = jnp.bfloat16
VMEM = pl.BlockSpec(memory_space=pltpu.VMEM)
SMEM = pl.BlockSpec(memory_space=pltpu.SMEM)
HBM = pl.BlockSpec(memory_space=pltpu.HBM)


def in_hbm(value):
    return pltpu.with_memory_space_constraint(value, pltpu.HBM)


def half_silu(half):
    tanh = jnp.tanh(half)
    scaled = half * tanh
    return half + scaled, tanh, scaled


def twice_slope(half, tanh, scaled):
    inner = 1.0 + half - scaled
    return inner + tanh * inner


def halves_swapped(first, second):
    low = lax.broadcasted_iota(jnp.int32, first.shape, 1) < 4
    upper = jnp.where(low, first, pltpu.roll(second, 4, 1))
    lower = jnp.where(low, pltpu.roll(first, 4, 1), second)
    return upper, lower


def pack(value):
    rows = value.shape[0]
    sides = [value[:, at : at + 128].reshape(rows // 8, 8, 128) for at in (0, 128)]
    even, odd = halves_swapped(*sides)
    return jnp.stack([even, odd], axis=1).reshape(rows // 4, 8, 128)


def unpack(value):
    groups = value.shape[0]
    pairs = value.reshape(groups // 2, 2, 8, 128)
    left, right = halves_swapped(pairs[:, 0], pairs[:, 1])
    return jnp.concatenate([x.reshape(groups * 4, 128) for x in (left, right)], axis=1)


def put_rows(table, first, source):
    rows = source.shape[0]
    value = source[...].astype(f32)
    table[pl.ds(2 * first, rows, stride=2), :] = value[:, :128]
    table[pl.ds(2 * first + 1, rows, stride=2), :] = value[:, 128:]


def put_rims(table, flip, inner, outer):
    end = table.shape[0] // 2 - HALO
    put_rows(table, pl.multiple_of((1 - flip[0]) * end, HALO), inner)
    put_rows(table, pl.multiple_of(flip[0] * end, HALO), outer)


def pair_at(table, at):
    return table[pl.ds(pl.multiple_of(at, 2), 2), :]


def table_kernel(feats, table):
    rows = feats.shape[0]
    put_rows(table, HALO + pl.multiple_of(pl.program_id(0) * rows, rows), feats)


def table_of(feats):
    nodes, width = feats.shape
    tile = 512
    return pl.pallas_call(
        table_kernel,
        out_shape=jax.ShapeDtypeStruct((2 * (nodes + 2 * HALO), 128), f32),
        grid=(nodes // tile,),
        in_specs=[pl.BlockSpec((tile, width), lambda i: (i, 0))],
        out_specs=VMEM,
        cost_estimate=pl.CostEstimate(flops=1 << 20, transcendentals=0, bytes_accessed=6 << 20),
        compiler_params=pltpu.CompilerParams(vmem_limit_bytes=16 << 20),
        name="window_rows",
    )(feats)


def layer_rows(own_left, own_right, left, right, sw, nw, bias, kind=bf16):
    pre = jnp.dot(own_left, sw[:128, :], preferred_element_type=f32)
    pre += jnp.dot(own_right, sw[128:, :], preferred_element_type=f32)
    pre += jnp.dot(left, nw[:128, :], preferred_element_type=f32)
    pre += jnp.dot(right, nw[128:, :], preferred_element_type=f32)
    return half_silu(0.5 * (pre + bias[...]))[0].astype(kind)


def conf_kernel(flip, nbrs, picks, outer, inner, *refs):
    sw_hbm, nw_hbm, bias_hbm, given, out, table, own, acc, sw, nw, bias, sems = refs
    copies = [
        pltpu.make_async_copy(source, target, sems.at[i])
        for i, (source, target) in enumerate(((sw_hbm, sw), (nw_hbm, nw), (bias_hbm, bias)))
    ]
    for copy in copies:
        copy.start()
    put_rims(table, flip, inner, outer)
    count = picks.shape[0]
    own3 = own.reshape(count, 2, 128)
    acc3 = acc.reshape(count, 2, 128)

    def body(block, carry):
        values = []
        for j in range(8):
            g = picks[block * 8 + j]
            at = (g >> 7) * 512 + (g & 127)
            near = [pair_at(table, nbrs[at + 128 * k]) for k in range(4)]
            values.append((pair_at(table, 2 * (HALO + g)), (near[0] + near[1]) + (near[2] + near[3])))
        for j in range(8):
            own3[block * 8 + j], acc3[block * 8 + j] = values[j]
        return carry

    lax.fori_loop(0, count // 8, body, 0)
    halves = [ref[pl.ds(side, count, stride=2), :] for ref in (own, acc) for side in (0, 1)]
    for copy in copies:
        copy.wait()
    value = layer_rows(
        halves[0].astype(bf16),
        halves[1].astype(bf16),
        (halves[2] * 0.25).astype(bf16),
        (halves[3] * 0.25).astype(bf16),
        sw,
        nw,
        bias,
        f32,
    )
    out[...] = pack(value).astype(bf16)


def conf_rows_of(flip, nbrs, picks, inner, outer, sw, nw, bias, table):
    count = picks.shape[0]
    width = sw.shape[0]
    return pl.pallas_call(
        conf_kernel,
        out_shape=(
            jax.ShapeDtypeStruct((count // 4, 8, width // 2), bf16),
            jax.ShapeDtypeStruct(table.shape, f32),
        ),
        in_specs=[SMEM] * 3 + [VMEM] * 2 + [HBM] * 3 + [VMEM],
        out_specs=(VMEM, VMEM),
        input_output_aliases={8: 1},
        scratch_shapes=[
            pltpu.VMEM((2 * count, 128), f32),
            pltpu.VMEM((2 * count, 128), f32),
            pltpu.VMEM(sw.shape, bf16),
            pltpu.VMEM(nw.shape, bf16),
            pltpu.VMEM(bias.shape, f32),
            pltpu.SemaphoreType.DMA((3,)),
        ],
        cost_estimate=pl.CostEstimate(
            flops=4 * count * width * width, transcendentals=0, bytes_accessed=6 << 20
        ),
        compiler_params=pltpu.CompilerParams(vmem_limit_bytes=16 << 20),
        name="conf_rows",
    )(flip, nbrs, picks, outer, inner, in_hbm(sw), in_hbm(nw), in_hbm(bias), table)


def layer_kernel(flip, nbrs, inner, outer, feats, own, sw, nw, bias, *refs):
    out, table, acc = refs[-3:]
    tile = own.shape[0]
    nodes = feats.shape[0]

    @pl.when(pl.program_id(0) == 0)
    def _():
        put_rims(table, flip, inner, outer)
        for start in range(0, nodes, 512):
            put_rows(table, HALO + start, feats.at[start : start + 512, :])

    acc3 = acc.reshape(tile, 2, 128)

    def body(block, carry):
        values = []
        for j in range(128):
            near = [pair_at(table, nbrs[block * 512 + (128 * k + j)]) for k in range(4)]
            values.append((near[0] + near[1]) + (near[2] + near[3]))
        for j in range(128):
            acc3[block * 128 + j] = values[j]
        return carry

    lax.fori_loop(0, tile // 128, body, 0)
    rows = own[...]
    out[...] = layer_rows(
        rows[:, :128],
        rows[:, 128:],
        (acc[pl.ds(0, tile, stride=2), :] * 0.25).astype(bf16),
        (acc[pl.ds(1, tile, stride=2), :] * 0.25).astype(bf16),
        sw,
        nw,
        bias,
    )


def layer_of(first, steps, flip, nbrs, inner, outer, feats, sw, nw, bias, given):
    nodes, width = feats.shape
    tile = 512
    ahead = [] if given is None else [given]
    return pl.pallas_call(
        layer_kernel,
        out_shape=jax.ShapeDtypeStruct((nodes, width), bf16),
        grid=(steps,),
        in_specs=[
            SMEM,
            pl.BlockSpec((4 * tile,), lambda i: (first + i,), memory_space=pltpu.SMEM),
            VMEM,
            VMEM,
            VMEM,
            pl.BlockSpec((tile, width), lambda i: (first + i, 0)),
            VMEM,
            VMEM,
            VMEM,
        ]
        + [HBM] * len(ahead),
        out_specs=pl.BlockSpec((tile, width), lambda i: (first + i, 0)),
        input_output_aliases={9: 0} if ahead else {},
        scratch_shapes=[
            pltpu.VMEM((2 * (nodes + 2 * HALO), 128), f32),
            pltpu.VMEM((2 * tile, 128), f32),
        ],
        cost_estimate=pl.CostEstimate(
            flops=steps * 4 * tile * width * width, transcendentals=0, bytes_accessed=steps << 23
        ),
        compiler_params=pltpu.CompilerParams(vmem_limit_bytes=24 << 20),
        name="graph_layer",
    )(flip, nbrs, inner, outer, feats, feats, sw, nw, bias, *ahead)


def place_of(group, turn):
    return group ^ (2 * (turn & 3) + (turn >> 2))


def prepare_kernel(mid, weight, back):
    back[...] = jnp.transpose(mid[...].astype(f32) * (weight[...] * 0.25)).astype(bf16)


def prepared(mid, weight):
    return pl.pallas_call(
        prepare_kernel,
        out_shape=jax.ShapeDtypeStruct(mid.shape, bf16),
        in_specs=[VMEM] * 2,
        out_specs=VMEM,
        cost_estimate=pl.CostEstimate(flops=1 << 20, transcendentals=0, bytes_accessed=1 << 19),
        compiler_params=pltpu.CompilerParams(vmem_limit_bytes=8 << 20),
        name="prepare",
    )(mid, weight)


def scorer_kernel(groups, final, where, *refs):
    xs, refs = refs[:groups], refs[groups:]
    ids, join, jbias, table, mid, back, mbias, weight = refs[:8]
    given, refs = refs[8:-8], refs[-8:]
    grads_hbm, sent, base, tabh, midh, total, grads, sems = refs
    step = pl.program_id(0)
    slot = step & 1
    chunk = base.shape[1]
    configs = ids.shape[0]
    layouts = table.shape[0]
    one = jnp.asarray(1.0, bf16)

    @pl.when(step == 0)
    def _():
        for i in range(groups):
            base[i] = 0.5 * (
                jnp.dot(
                    unpack(xs[i][...].astype(f32)).astype(bf16),
                    join[...],
                    preferred_element_type=f32,
                )
                + jbias[...]
            )
        tabh[...] = (table[...].astype(f32) * 0.5).astype(bf16)
        midh[...] = (mid[...].astype(f32) * 0.5).astype(bf16)
        total[...] = given[0][...] if given else jnp.zeros_like(total)

    some = 8

    def copy_of(turn, place, first):
        part = pl.ds(first, some)
        return pltpu.make_async_copy(
            grads.at[place, part], grads_hbm.at[turn, part], sems.at[place, first // some]
        )

    def wait_for(turn, place):
        for first in range(0, configs, some):
            copy_of(turn, place, first).wait()

    @pl.when(step >= 2)
    def _():
        wait_for(step - 2, slot)

    columns = jnp.transpose(ids[...].astype(f32))
    lanes = lax.broadcasted_iota(jnp.int32, (chunk, layouts), 1).astype(f32)
    rows = base[step]
    for first in range(0, configs, some):
        picks = jnp.concatenate(
            [
                jnp.where(columns[:, k : k + 1] == lanes, 1.0, 0.0).astype(bf16)
                for k in range(first, first + some)
            ],
            axis=0,
        )
        half = jnp.dot(picks, tabh[...], preferred_element_type=f32)
        half = (half + jnp.concatenate([rows] * some, axis=0)).astype(bf16)
        tanh = jnp.tanh(half)
        above = one + tanh
        slope = above * (one + half * (one - tanh))
        outer = jnp.dot(half * above, midh[...], preferred_element_type=f32)
        outer = (outer + 0.5 * mbias[...]).astype(bf16)
        tanh2 = jnp.tanh(outer)
        above2 = one + tanh2
        act2 = (outer * above2).astype(f32)
        slope2 = above2 * (one + outer * (one - tanh2))
        for q in range(some):
            part = act2[q * chunk : (q + 1) * chunk, :]
            total[first + q : first + q + 1, :] += jnp.sum(part, axis=0, keepdims=True)
        grad = jnp.dot(slope2, back[...], preferred_element_type=f32).astype(bf16) * slope
        for q in range(some):
            grads[slot, first + q] = grad[q * chunk : (q + 1) * chunk, :]
        copy_of(step, slot, first).start()

    @pl.when(step == groups - 1)
    def _():
        if final:
            scores = jnp.sum(total[...] * weight[...], axis=1, keepdims=True)
            lane = lax.broadcasted_iota(jnp.int32, (configs, 128), 1)
            sub = lax.broadcasted_iota(jnp.int32, (configs, 128), 0)
            spread = jnp.where(lane == sub + where[0] * configs, scores, 0.0)
            sent[...] = jnp.broadcast_to(jnp.sum(spread, axis=0, keepdims=True), sent.shape)
        else:
            sent[...] = total[...]
        wait_for(step - 1, 1 - slot)
        wait_for(step, slot)


def scorer_of(final, turns, where, xs, ids, join, jbias, weights, mbias, weight, given):
    groups = len(xs)
    configs = ids.shape[0]
    chunk = xs[0].shape[0] * 4
    width, hidden = join.shape
    start, stride = turns
    summed = final if final else (configs, hidden)
    return pl.pallas_call(
        functools.partial(scorer_kernel, groups, final),
        out_shape=(
            pltpu.HBM((groups, configs, chunk, hidden), bf16),
            jax.ShapeDtypeStruct(summed, f32),
        ),
        grid_spec=pltpu.PrefetchScalarGridSpec(
            num_scalar_prefetch=1,
            grid=(groups,),
            in_specs=[VMEM] * groups
            + [
                pl.BlockSpec(
                    (configs, chunk), lambda i, where: (0, place_of(where[0], start + stride * i))
                )
            ]
            + [VMEM] * (7 + len(given)),
            out_specs=(HBM, VMEM),
            scratch_shapes=[
                pltpu.VMEM((groups, chunk, hidden), f32),
                pltpu.VMEM(weights[0].shape, bf16),
                pltpu.VMEM(weights[1].shape, bf16),
                pltpu.VMEM((configs, hidden), f32),
                pltpu.VMEM((2, configs, chunk, hidden), bf16),
                pltpu.SemaphoreType.DMA((2, 2)),
            ],
        ),
        cost_estimate=pl.CostEstimate(
            flops=6 * groups * configs * chunk * width * width,
            transcendentals=2 * groups * configs * chunk * width,
            bytes_accessed=groups << 20,
        ),
        compiler_params=pltpu.CompilerParams(vmem_limit_bytes=24 << 20),
        name="scorer",
    )(where, *xs, ids, join, jbias, *weights, mbias, weight, *given)


def weighted(coef, grads, out):
    configs, chunk, hidden = grads.shape
    some = 32
    for start in range(0, chunk, some):
        rows = grads[0, start : start + some, :].astype(f32) * coef[0:1, :]
        for k in range(1, configs):
            rows = rows + grads[k, start : start + some, :].astype(f32) * coef[k : k + 1, :]
        out[start : start + some, :] = rows.astype(bf16)


def fetches(pair, later, which, grads, sems):
    sources = [pair.at[which]] + [later.at[d] for d in range(grads.shape[0] - 1)]
    return [
        pltpu.make_async_copy(source, grads.at[d], sems.at[d]) for d, source in enumerate(sources)
    ]


def ranking_kernel(scale, where, got, pairs, pair, later, loss, coef, out, column, grads, sems):
    half, configs, chunk, hidden = grads.shape
    copies = fetches(pair, later, 1, grads, sems)
    for copy in copies:
        copy.start()
    score = jnp.sum(got[...], axis=0, keepdims=True) * scale
    lane = lax.broadcasted_iota(jnp.int32, (128, 128), 1)
    sub = lax.broadcasted_iota(jnp.int32, (128, 128), 0)
    score = jnp.sum(jnp.where(lane == sub, score, 0.0), axis=1, keepdims=True)
    count = pairs.shape[1]
    ids = lax.broadcasted_iota(jnp.int32, (128, count), 0)
    second = jnp.where(pairs[1:2, :] == ids, 1.0, 0.0)
    signed = second - jnp.where(pairs[0:1, :] == ids, 1.0, 0.0)
    gap = jnp.sum(signed * score, axis=0, keepdims=True)
    fade = jnp.exp(-jnp.abs(gap))
    soft = jnp.maximum(gap, 0.0) + jnp.log1p(fade)
    loss[...] = jnp.sum(soft, axis=1, keepdims=True) * (1.0 / count)
    slope = jnp.where(gap >= 0.0, 1.0, fade) / (1.0 + fade)
    grad = jnp.sum(slope * signed, axis=1, keepdims=True) * (65536.0 * scale / count)
    column[...] = jnp.broadcast_to(grad, column.shape)
    coef[...] = column[pl.ds(pl.multiple_of(where[0] * configs, configs), configs), :]
    for d in range(half):
        copies[d].wait()
        weighted(coef, grads.at[d], out.at[d])


def ranking_of(scale, where, got, pairs, pair, later):
    half, configs, chunk, hidden = later.shape
    half += 1
    return pl.pallas_call(
        functools.partial(ranking_kernel, scale),
        out_shape=(
            jax.ShapeDtypeStruct((1, 1), f32),
            jax.ShapeDtypeStruct((configs, hidden), f32),
            jax.ShapeDtypeStruct((half, chunk, hidden), bf16),
        ),
        in_specs=[SMEM, VMEM, VMEM, HBM, HBM],
        out_specs=(VMEM, VMEM, VMEM),
        scratch_shapes=[
            pltpu.VMEM((128, hidden), f32),
            pltpu.VMEM((half, configs, chunk, hidden), bf16),
            pltpu.SemaphoreType.DMA((half,)),
        ],
        cost_estimate=pl.CostEstimate(flops=1 << 24, transcendentals=0, bytes_accessed=6 << 20),
        compiler_params=pltpu.CompilerParams(vmem_limit_bytes=16 << 20),
        name="ranking",
    )(where, got, pairs, in_hbm(pair), in_hbm(later))


def rest_kernel(coef, pair, later, out, grads, sems):
    copies = fetches(pair, later, 0, grads, sems)
    for copy in copies:
        copy.start()
    for d, copy in enumerate(copies):
        copy.wait()
        weighted(coef, grads.at[d], out.at[d])


def rest_of(coef, pair, later):
    half, configs, chunk, hidden = later.shape
    half += 1
    return pl.pallas_call(
        rest_kernel,
        out_shape=jax.ShapeDtypeStruct((half, chunk, hidden), bf16),
        in_specs=[VMEM, HBM, HBM],
        out_specs=VMEM,
        scratch_shapes=[
            pltpu.VMEM((half, configs, chunk, hidden), bf16),
            pltpu.SemaphoreType.DMA((half,)),
        ],
        cost_estimate=pl.CostEstimate(flops=1 << 24, transcendentals=0, bytes_accessed=6 << 20),
        compiler_params=pltpu.CompilerParams(vmem_limit_bytes=16 << 20),
        name="rest",
    )(coef, in_hbm(pair), in_hbm(later))


def finish_kernel(kept, came, *refs):
    arrived, (join, out) = refs[:-2], refs[-2:]
    rows = kept[0].astype(f32) + came[0].astype(f32)
    for part in arrived:
        rows = rows + part[...].astype(f32)
    value = lax.dot_general(
        rows.astype(bf16), join[...], (((1,), (1,)), ((), ())), preferred_element_type=f32
    )
    out[...] = pack(value).astype(bf16)


def finish_of(kept, came, arrived, join):
    rows, width = kept.shape[1], join.shape[0]
    return pl.pallas_call(
        finish_kernel,
        out_shape=jax.ShapeDtypeStruct((rows // 4, 8, width // 2), bf16),
        in_specs=[VMEM] * (3 + len(arrived)),
        out_specs=VMEM,
        cost_estimate=pl.CostEstimate(flops=1 << 24, transcendentals=0, bytes_accessed=1 << 19),
        compiler_params=pltpu.CompilerParams(vmem_limit_bytes=8 << 20),
        name="finish",
    )(kept, came, *arrived, join)


def returned_kernel(value, out):
    out[...] = unpack(value[...].astype(f32))


def returned_of(value):
    groups = value.shape[0]
    return pl.pallas_call(
        returned_kernel,
        out_shape=jax.ShapeDtypeStruct((groups * 4, 256), f32),
        in_specs=[VMEM],
        out_specs=VMEM,
        cost_estimate=pl.CostEstimate(flops=1 << 16, transcendentals=0, bytes_accessed=1 << 18),
        compiler_params=pltpu.CompilerParams(vmem_limit_bytes=8 << 20),
        name="returned",
    )(value)


def shards(
    node_feats,
    neighbors,
    self_weight,
    neighbor_weight,
    sage_bias,
    conf_index,
    layout_ids,
    join_weight,
    layout_table,
    join_bias,
    mid_weight,
    mid_bias,
    score_weight,
    config_pairs,
):
    both = ("cfg", "node")
    devices = lax.axis_size(both)
    node_count = lax.axis_size("node")
    group_count = lax.axis_size("cfg")
    rings = group_count // 2
    scale = 1.0 / math.sqrt(layout_ids.shape[1] * node_count)
    group = lax.axis_index("cfg")

    nodes, near = neighbors.shape
    spot = lax.axis_index("node")
    flip = (spot & 1).reshape(1)

    def trade(rows, partner):
        pairs = [(i, partner(i)) for i in range(devices) if 0 <= partner(i) < devices]
        return lax.ppermute(rows, both, pairs)

    def rim(feats, odd):
        return lax.dynamic_slice_in_dim(feats, odd * (nodes - HALO), HALO, 0)

    outer = trade(rim(node_feats, spot & 1), lambda i: i + 1 if i % 2 else i - 1)
    inner = trade(rim(node_feats, 1 - (spot & 1)), lambda i: i ^ 1)
    nbrs = (2 * neighbors).T.reshape(near, nodes // 128, 128).transpose(1, 0, 2).reshape(-1)
    bias = sage_bias.reshape(1, -1)
    hold = lax.optimization_barrier

    table = table_of(node_feats)
    conf_src, _ = conf_rows_of(
        flip,
        nbrs,
        conf_index,
        inner,
        outer,
        self_weight,
        neighbor_weight,
        bias,
        table,
    )

    def layer(first, steps, given):
        return layer_of(
            first,
            steps,
            flip,
            nbrs,
            inner,
            outer,
            node_feats,
            self_weight,
            neighbor_weight,
            bias,
            given,
        )

    swap = [(i, i ^ 1) for i in range(group_count)]

    def shift(value, by):
        return lax.ppermute(value, "cfg", [(i, i ^ (2 * by)) for i in range(group_count)])

    mine = lax.all_to_all(conf_src, "node", 0, 0, tiled=True)
    embed = layer(0, 2, None)
    weight = score_weight.reshape(1, -1)
    mine, embed, back = hold((mine, embed, prepared(mid_weight, weight)))
    weights = (layout_table, mid_weight, back)
    others = [shift(mine, by) for by in range(1, rings)]
    where = group.reshape(1)

    def scorer(final, turns, xs, given):
        return scorer_of(
            final,
            turns,
            where,
            xs,
            layout_ids,
            join_weight,
            join_bias.reshape(1, -1),
            weights,
            mid_bias.reshape(1, -1),
            weight,
            given,
        )

    pair, total = scorer(None, (0, rings), [mine, lax.ppermute(mine, "cfg", swap)], [])
    others = list(hold((*others, total)))
    total = others.pop()
    swapped = [lax.ppermute(x, "cfg", swap) for x in others]
    own, total = scorer(None, (1, 1), others, [total])
    swapped = list(hold((*swapped, total)))
    total = swapped.pop()
    other, sent = scorer((devices, 128), (rings + 1, 1), swapped, [total])
    sent, embed = hold((sent, embed))
    got = lax.all_to_all(sent.reshape(devices, 1, 128), both, 0, 0, tiled=True)
    embed = layer(2, 3, embed)
    got, embed = hold((got, embed))
    loss, coef, away = ranking_of(
        scale, where, got.reshape(devices, 128), config_pairs.T, pair, other
    )
    came = lax.ppermute(away, "cfg", swap)
    kept = rest_of(coef, pair, own)
    sums = [(kept[d].astype(f32) + came[d].astype(f32)).astype(bf16) for d in range(1, rings)]
    arrived = [shift(part, by) for by, part in enumerate(sums, 1)]
    local_grad, embed = hold((finish_of(kept, came, arrived, join_weight), embed))
    conf_grad = lax.all_to_all(local_grad, "node", 0, 0, tiled=True)
    embed = layer(5, 3, embed)
    conf_grad = returned_of(conf_grad)
    return (embed, loss.reshape(()), conf_grad)


def solution(mesh):
    split = P(("cfg", "node"), None)
    placed = (split, split, P(), P(), P(), P(("cfg", "node")), P("cfg", "node")) + (P(),) * 7
    return jax.shard_map(
        shards,
        mesh=mesh,
        in_specs=placed,
        out_specs=(split, P(), split),
        check_vma=False,
    )
```

```python
import functools
import math

import jax
import jax.numpy as jnp
from jax import lax
from jax.experimental import pallas as pl
from jax.experimental.pallas import tpu as pltpu
from jax.sharding import PartitionSpec as P

HALO = 512
f32 = jnp.float32
bf16 = jnp.bfloat16
VMEM = pl.BlockSpec(memory_space=pltpu.VMEM)
SMEM = pl.BlockSpec(memory_space=pltpu.SMEM)
HBM = pl.BlockSpec(memory_space=pltpu.HBM)


def in_hbm(value):
    return pltpu.with_memory_space_constraint(value, pltpu.HBM)


def half_silu(half):
    tanh = jnp.tanh(half)
    scaled = half * tanh
    return half + scaled, tanh, scaled


def twice_slope(half, tanh, scaled):
    inner = 1.0 + half - scaled
    return inner + tanh * inner


def halves_swapped(first, second):
    low = lax.broadcasted_iota(jnp.int32, first.shape, 1) < 4
    upper = jnp.where(low, first, pltpu.roll(second, 4, 1))
    lower = jnp.where(low, pltpu.roll(first, 4, 1), second)
    return upper, lower


def pack(value):
    rows = value.shape[0]
    sides = [value[:, at : at + 128].reshape(rows // 8, 8, 128) for at in (0, 128)]
    even, odd = halves_swapped(*sides)
    return jnp.stack([even, odd], axis=1).reshape(rows // 4, 8, 128)


def unpack(value):
    groups = value.shape[0]
    pairs = value.reshape(groups // 2, 2, 8, 128)
    left, right = halves_swapped(pairs[:, 0], pairs[:, 1])
    return jnp.concatenate([x.reshape(groups * 4, 128) for x in (left, right)], axis=1)


def put_rows(table, first, source):
    rows = source.shape[0]
    value = source[...].astype(f32)
    table[pl.ds(2 * first, rows, stride=2), :] = value[:, :128]
    table[pl.ds(2 * first + 1, rows, stride=2), :] = value[:, 128:]


def put_rims(table, flip, inner, outer):
    end = table.shape[0] // 2 - HALO
    put_rows(table, pl.multiple_of((1 - flip[0]) * end, HALO), inner)
    put_rows(table, pl.multiple_of(flip[0] * end, HALO), outer)


def pair_at(table, at):
    return table[pl.ds(pl.multiple_of(at, 2), 2), :]


def table_kernel(feats, table):
    rows = feats.shape[0]
    put_rows(table, HALO + pl.multiple_of(pl.program_id(0) * rows, rows), feats)


def table_of(feats):
    nodes, width = feats.shape
    tile = 512
    return pl.pallas_call(
        table_kernel,
        out_shape=jax.ShapeDtypeStruct((2 * (nodes + 2 * HALO), 128), f32),
        grid=(nodes // tile,),
        in_specs=[pl.BlockSpec((tile, width), lambda i: (i, 0))],
        out_specs=VMEM,
        cost_estimate=pl.CostEstimate(flops=1 << 20, transcendentals=0, bytes_accessed=6 << 20),
        compiler_params=pltpu.CompilerParams(vmem_limit_bytes=16 << 20),
        name="window_rows",
    )(feats)


def layer_rows(own_left, own_right, left, right, sw, nw, bias, kind=bf16):
    pre = jnp.dot(own_left, sw[:128, :], preferred_element_type=f32)
    pre += jnp.dot(own_right, sw[128:, :], preferred_element_type=f32)
    pre += jnp.dot(left, nw[:128, :], preferred_element_type=f32)
    pre += jnp.dot(right, nw[128:, :], preferred_element_type=f32)
    return half_silu(0.5 * (pre + bias[...]))[0].astype(kind)


def conf_kernel(flip, nbrs, picks, outer, inner, *refs):
    sw_hbm, nw_hbm, bias_hbm, given, out, table, own, acc, sw, nw, bias, sems = refs
    copies = [
        pltpu.make_async_copy(source, target, sems.at[i])
        for i, (source, target) in enumerate(((sw_hbm, sw), (nw_hbm, nw), (bias_hbm, bias)))
    ]
    for copy in copies:
        copy.start()
    put_rims(table, flip, inner, outer)
    count = picks.shape[0]
    own3 = own.reshape(count, 2, 128)
    acc3 = acc.reshape(count, 2, 128)

    def body(block, carry):
        values = []
        for j in range(8):
            g = picks[block * 8 + j]
            at = (g >> 7) * 512 + (g & 127)
            near = [pair_at(table, nbrs[at + 128 * k]) for k in range(4)]
            values.append((pair_at(table, 2 * (HALO + g)), (near[0] + near[1]) + (near[2] + near[3])))
        for j in range(8):
            own3[block * 8 + j], acc3[block * 8 + j] = values[j]
        return carry

    lax.fori_loop(0, count // 8, body, 0)
    halves = [ref[pl.ds(side, count, stride=2), :] for ref in (own, acc) for side in (0, 1)]
    for copy in copies:
        copy.wait()
    value = layer_rows(
        halves[0].astype(bf16),
        halves[1].astype(bf16),
        (halves[2] * 0.25).astype(bf16),
        (halves[3] * 0.25).astype(bf16),
        sw,
        nw,
        bias,
        f32,
    )
    out[...] = pack(value).astype(bf16)


def conf_rows_of(flip, nbrs, picks, inner, outer, sw, nw, bias, table):
    count = picks.shape[0]
    width = sw.shape[0]
    return pl.pallas_call(
        conf_kernel,
        out_shape=(
            jax.ShapeDtypeStruct((count // 4, 8, width // 2), bf16),
            jax.ShapeDtypeStruct(table.shape, f32),
        ),
        in_specs=[SMEM] * 3 + [VMEM] * 2 + [HBM] * 3 + [VMEM],
        out_specs=(VMEM, VMEM),
        input_output_aliases={8: 1},
        scratch_shapes=[
            pltpu.VMEM((2 * count, 128), f32),
            pltpu.VMEM((2 * count, 128), f32),
            pltpu.VMEM(sw.shape, bf16),
            pltpu.VMEM(nw.shape, bf16),
            pltpu.VMEM(bias.shape, f32),
            pltpu.SemaphoreType.DMA((3,)),
        ],
        cost_estimate=pl.CostEstimate(
            flops=4 * count * width * width, transcendentals=0, bytes_accessed=6 << 20
        ),
        compiler_params=pltpu.CompilerParams(vmem_limit_bytes=16 << 20),
        name="conf_rows",
    )(flip, nbrs, picks, outer, inner, in_hbm(sw), in_hbm(nw), in_hbm(bias), table)


def layer_kernel(flip, nbrs, inner, outer, feats, own, sw, nw, bias, *refs):
    out, table, acc = refs[-3:]
    tile = own.shape[0]
    nodes = feats.shape[0]

    @pl.when(pl.program_id(0) == 0)
    def _():
        put_rims(table, flip, inner, outer)
        for start in range(0, nodes, 512):
            put_rows(table, HALO + start, feats.at[start : start + 512, :])

    acc3 = acc.reshape(tile, 2, 128)
    some = 128

    part = 32

    def gather(block, first):
        values = []
        for j in range(first, first + part):
            near = [pair_at(table, nbrs[block * 512 + (128 * k + j)]) for k in range(4)]
            values.append((near[0] + near[1]) + (near[2] + near[3]))
        for j, value in enumerate(values, first):
            acc3[block * some + j] = value

    def products(block):
        start = block * some
        sides = [
            (acc[pl.ds(2 * start + side, some, stride=2), :] * 0.25).astype(bf16)
            for side in (0, 1)
        ]
        pre = jnp.dot(own[start : start + some, :], sw[...], preferred_element_type=f32)
        pre += jnp.dot(sides[0], nw[:128, :], preferred_element_type=f32)
        return pre + jnp.dot(sides[1], nw[128:, :], preferred_element_type=f32)

    blocks = tile // some
    for block in range(blocks + 1):
        pre = products(block - 1) if block > 0 else None
        for first in range(0, some, part):
            if block < blocks:
                gather(block, first)
            if block > 0:
                start = (block - 1) * some + first
                half = 0.5 * (pre[first : first + part, :] + bias[...])
                out[start : start + part, :] = half_silu(half)[0].astype(bf16)


def layer_of(first, steps, flip, nbrs, inner, outer, feats, sw, nw, bias, given):
    nodes, width = feats.shape
    tile = 512
    ahead = [] if given is None else [given]
    return pl.pallas_call(
        layer_kernel,
        out_shape=jax.ShapeDtypeStruct((nodes, width), bf16),
        grid=(steps,),
        in_specs=[
            SMEM,
            pl.BlockSpec((4 * tile,), lambda i: (first + i,), memory_space=pltpu.SMEM),
            VMEM,
            VMEM,
            VMEM,
            pl.BlockSpec((tile, width), lambda i: (first + i, 0)),
            VMEM,
            VMEM,
            VMEM,
        ]
        + [HBM] * len(ahead),
        out_specs=pl.BlockSpec((tile, width), lambda i: (first + i, 0)),
        input_output_aliases={9: 0} if ahead else {},
        scratch_shapes=[
            pltpu.VMEM((2 * (nodes + 2 * HALO), 128), f32),
            pltpu.VMEM((2 * tile, 128), f32),
        ],
        cost_estimate=pl.CostEstimate(
            flops=steps * 4 * tile * width * width, transcendentals=0, bytes_accessed=steps << 23
        ),
        compiler_params=pltpu.CompilerParams(vmem_limit_bytes=24 << 20),
        name="graph_layer",
    )(flip, nbrs, inner, outer, feats, feats, sw, nw, bias, *ahead)


def place_of(group, turn):
    return group ^ (2 * (turn & 3) + (turn >> 2))


def prepare_kernel(mid, weight, back):
    back[...] = jnp.transpose(mid[...].astype(f32) * (weight[...] * 0.25)).astype(bf16)


def prepared(mid, weight):
    return pl.pallas_call(
        prepare_kernel,
        out_shape=jax.ShapeDtypeStruct(mid.shape, bf16),
        in_specs=[VMEM] * 2,
        out_specs=VMEM,
        cost_estimate=pl.CostEstimate(flops=1 << 20, transcendentals=0, bytes_accessed=1 << 19),
        compiler_params=pltpu.CompilerParams(vmem_limit_bytes=8 << 20),
        name="prepare",
    )(mid, weight)


def scorer_kernel(groups, final, where, *refs):
    xs, refs = refs[:groups], refs[groups:]
    ids, join, jbias, table, mid, back, mbias, weight = refs[:8]
    given, refs = refs[8:-8], refs[-8:]
    grads_hbm, sent, base, tabh, midh, total, grads, sems = refs
    step = pl.program_id(0)
    slot = step & 1
    chunk = base.shape[1]
    configs = ids.shape[0]
    layouts = table.shape[0]
    one = jnp.asarray(1.0, bf16)

    @pl.when(step == 0)
    def _():
        for i in range(groups):
            base[i] = 0.5 * (
                jnp.dot(
                    unpack(xs[i][...].astype(f32)).astype(bf16),
                    join[...],
                    preferred_element_type=f32,
                )
                + jbias[...]
            )
        tabh[...] = (table[...].astype(f32) * 0.5).astype(bf16)
        midh[...] = (mid[...].astype(f32) * 0.5).astype(bf16)
        total[...] = given[0][...] if given else jnp.zeros_like(total)

    some = 8

    def copy_of(turn, place, first):
        part = pl.ds(first, some)
        return pltpu.make_async_copy(
            grads.at[place, part], grads_hbm.at[turn, part], sems.at[place, first // some]
        )

    def wait_for(turn, place):
        for first in range(0, configs, some):
            copy_of(turn, place, first).wait()

    @pl.when(step >= 2)
    def _():
        wait_for(step - 2, slot)

    columns = jnp.transpose(ids[...].astype(f32))
    lanes = lax.broadcasted_iota(jnp.int32, (chunk, layouts), 1).astype(f32)
    rows = base[step]
    for first in range(0, configs, some):
        picks = jnp.concatenate(
            [
                jnp.where(columns[:, k : k + 1] == lanes, 1.0, 0.0).astype(bf16)
                for k in range(first, first + some)
            ],
            axis=0,
        )
        half = jnp.dot(picks, tabh[...], preferred_element_type=f32)
        half = (half + jnp.concatenate([rows] * some, axis=0)).astype(bf16)
        tanh = jnp.tanh(half)
        above = one + tanh
        slope = above * (one + half * (one - tanh))
        outer = jnp.dot(half * above, midh[...], preferred_element_type=f32)
        outer = (outer + 0.5 * mbias[...]).astype(bf16)
        tanh2 = jnp.tanh(outer)
        above2 = one + tanh2
        act2 = (outer * above2).astype(f32)
        slope2 = above2 * (one + outer * (one - tanh2))
        for q in range(some):
            part = act2[q * chunk : (q + 1) * chunk, :]
            total[first + q : first + q + 1, :] += jnp.sum(part, axis=0, keepdims=True)
        grad = jnp.dot(slope2, back[...], preferred_element_type=f32).astype(bf16) * slope
        for q in range(some):
            grads[slot, first + q] = grad[q * chunk : (q + 1) * chunk, :]
        copy_of(step, slot, first).start()

    @pl.when(step == groups - 1)
    def _():
        if final:
            scores = jnp.sum(total[...] * weight[...], axis=1, keepdims=True)
            lane = lax.broadcasted_iota(jnp.int32, (configs, 128), 1)
            sub = lax.broadcasted_iota(jnp.int32, (configs, 128), 0)
            spread = jnp.where(lane == sub + where[0] * configs, scores, 0.0)
            sent[...] = jnp.broadcast_to(jnp.sum(spread, axis=0, keepdims=True), sent.shape)
        else:
            sent[...] = total[...]
        wait_for(step - 1, 1 - slot)
        wait_for(step, slot)


def scorer_of(final, turns, where, xs, ids, join, jbias, weights, mbias, weight, given):
    groups = len(xs)
    configs = ids.shape[0]
    chunk = xs[0].shape[0] * 4
    width, hidden = join.shape
    start, stride = turns
    summed = final if final else (configs, hidden)
    return pl.pallas_call(
        functools.partial(scorer_kernel, groups, final),
        out_shape=(
            pltpu.HBM((groups, configs, chunk, hidden), bf16),
            jax.ShapeDtypeStruct(summed, f32),
        ),
        grid_spec=pltpu.PrefetchScalarGridSpec(
            num_scalar_prefetch=1,
            grid=(groups,),
            in_specs=[VMEM] * groups
            + [
                pl.BlockSpec(
                    (configs, chunk), lambda i, where: (0, place_of(where[0], start + stride * i))
                )
            ]
            + [VMEM] * (7 + len(given)),
            out_specs=(HBM, VMEM),
            scratch_shapes=[
                pltpu.VMEM((groups, chunk, hidden), f32),
                pltpu.VMEM(weights[0].shape, bf16),
                pltpu.VMEM(weights[1].shape, bf16),
                pltpu.VMEM((configs, hidden), f32),
                pltpu.VMEM((2, configs, chunk, hidden), bf16),
                pltpu.SemaphoreType.DMA((2, 2)),
            ],
        ),
        cost_estimate=pl.CostEstimate(
            flops=6 * groups * configs * chunk * width * width,
            transcendentals=2 * groups * configs * chunk * width,
            bytes_accessed=groups << 20,
        ),
        compiler_params=pltpu.CompilerParams(vmem_limit_bytes=24 << 20),
        name="scorer",
    )(where, *xs, ids, join, jbias, *weights, mbias, weight, *given)


def weighted(coef, grads, out):
    configs, chunk, hidden = grads.shape
    some = 32
    for start in range(0, chunk, some):
        rows = grads[0, start : start + some, :].astype(f32) * coef[0:1, :]
        for k in range(1, configs):
            rows = rows + grads[k, start : start + some, :].astype(f32) * coef[k : k + 1, :]
        out[start : start + some, :] = rows.astype(bf16)


def fetches(pair, later, which, grads, sems):
    sources = [pair.at[which]] + [later.at[d] for d in range(grads.shape[0] - 1)]
    return [
        pltpu.make_async_copy(source, grads.at[d], sems.at[d]) for d, source in enumerate(sources)
    ]


def ranking_kernel(scale, where, got, pairs, pair, later, loss, coef, out, column, grads, sems):
    half, configs, chunk, hidden = grads.shape
    copies = fetches(pair, later, 1, grads, sems)
    for copy in copies:
        copy.start()
    score = jnp.sum(got[...], axis=0, keepdims=True) * scale
    lane = lax.broadcasted_iota(jnp.int32, (128, 128), 1)
    sub = lax.broadcasted_iota(jnp.int32, (128, 128), 0)
    score = jnp.sum(jnp.where(lane == sub, score, 0.0), axis=1, keepdims=True)
    count = pairs.shape[1]
    ids = lax.broadcasted_iota(jnp.int32, (128, count), 0)
    second = jnp.where(pairs[1:2, :] == ids, 1.0, 0.0)
    signed = second - jnp.where(pairs[0:1, :] == ids, 1.0, 0.0)
    gap = jnp.sum(signed * score, axis=0, keepdims=True)
    fade = jnp.exp(-jnp.abs(gap))
    soft = jnp.maximum(gap, 0.0) + jnp.log1p(fade)
    loss[...] = jnp.sum(soft, axis=1, keepdims=True) * (1.0 / count)
    slope = jnp.where(gap >= 0.0, 1.0, fade) / (1.0 + fade)
    grad = jnp.sum(slope * signed, axis=1, keepdims=True) * (65536.0 * scale / count)
    column[...] = jnp.broadcast_to(grad, column.shape)
    coef[...] = column[pl.ds(pl.multiple_of(where[0] * configs, configs), configs), :]
    for d in range(half):
        copies[d].wait()
        weighted(coef, grads.at[d], out.at[d])


def ranking_of(scale, where, got, pairs, pair, later):
    half, configs, chunk, hidden = later.shape
    half += 1
    return pl.pallas_call(
        functools.partial(ranking_kernel, scale),
        out_shape=(
            jax.ShapeDtypeStruct((1, 1), f32),
            jax.ShapeDtypeStruct((configs, hidden), f32),
            jax.ShapeDtypeStruct((half, chunk, hidden), bf16),
        ),
        in_specs=[SMEM, VMEM, VMEM, HBM, HBM],
        out_specs=(VMEM, VMEM, VMEM),
        scratch_shapes=[
            pltpu.VMEM((128, hidden), f32),
            pltpu.VMEM((half, configs, chunk, hidden), bf16),
            pltpu.SemaphoreType.DMA((half,)),
        ],
        cost_estimate=pl.CostEstimate(flops=1 << 24, transcendentals=0, bytes_accessed=6 << 20),
        compiler_params=pltpu.CompilerParams(vmem_limit_bytes=16 << 20),
        name="ranking",
    )(where, got, pairs, in_hbm(pair), in_hbm(later))


def rest_kernel(coef, pair, later, out, grads, sems):
    copies = fetches(pair, later, 0, grads, sems)
    for copy in copies:
        copy.start()
    for d, copy in enumerate(copies):
        copy.wait()
        weighted(coef, grads.at[d], out.at[d])


def rest_of(coef, pair, later):
    half, configs, chunk, hidden = later.shape
    half += 1
    return pl.pallas_call(
        rest_kernel,
        out_shape=jax.ShapeDtypeStruct((half, chunk, hidden), bf16),
        in_specs=[VMEM, HBM, HBM],
        out_specs=VMEM,
        scratch_shapes=[
            pltpu.VMEM((half, configs, chunk, hidden), bf16),
            pltpu.SemaphoreType.DMA((half,)),
        ],
        cost_estimate=pl.CostEstimate(flops=1 << 24, transcendentals=0, bytes_accessed=6 << 20),
        compiler_params=pltpu.CompilerParams(vmem_limit_bytes=16 << 20),
        name="rest",
    )(coef, in_hbm(pair), in_hbm(later))


def finish_kernel(kept, came, *refs):
    arrived, (join, out) = refs[:-2], refs[-2:]
    rows = kept[0].astype(f32) + came[0].astype(f32)
    for part in arrived:
        rows = rows + part[...].astype(f32)
    value = lax.dot_general(
        rows.astype(bf16), join[...], (((1,), (1,)), ((), ())), preferred_element_type=f32
    )
    out[...] = pack(value).astype(bf16)


def finish_of(kept, came, arrived, join):
    rows, width = kept.shape[1], join.shape[0]
    return pl.pallas_call(
        finish_kernel,
        out_shape=jax.ShapeDtypeStruct((rows // 4, 8, width // 2), bf16),
        in_specs=[VMEM] * (3 + len(arrived)),
        out_specs=VMEM,
        cost_estimate=pl.CostEstimate(flops=1 << 24, transcendentals=0, bytes_accessed=1 << 19),
        compiler_params=pltpu.CompilerParams(vmem_limit_bytes=8 << 20),
        name="finish",
    )(kept, came, *arrived, join)


def returned_kernel(value, out):
    out[...] = unpack(value[...].astype(f32))


def returned_of(value):
    groups = value.shape[0]
    return pl.pallas_call(
        returned_kernel,
        out_shape=jax.ShapeDtypeStruct((groups * 4, 256), f32),
        in_specs=[VMEM],
        out_specs=VMEM,
        cost_estimate=pl.CostEstimate(flops=1 << 16, transcendentals=0, bytes_accessed=1 << 18),
        compiler_params=pltpu.CompilerParams(vmem_limit_bytes=8 << 20),
        name="returned",
    )(value)


def shards(
    node_feats,
    neighbors,
    self_weight,
    neighbor_weight,
    sage_bias,
    conf_index,
    layout_ids,
    join_weight,
    layout_table,
    join_bias,
    mid_weight,
    mid_bias,
    score_weight,
    config_pairs,
):
    both = ("cfg", "node")
    devices = lax.axis_size(both)
    node_count = lax.axis_size("node")
    group_count = lax.axis_size("cfg")
    rings = group_count // 2
    scale = 1.0 / math.sqrt(layout_ids.shape[1] * node_count)
    group = lax.axis_index("cfg")

    nodes, near = neighbors.shape
    spot = lax.axis_index("node")
    flip = (spot & 1).reshape(1)

    def trade(rows, partner):
        pairs = [(i, partner(i)) for i in range(devices) if 0 <= partner(i) < devices]
        return lax.ppermute(rows, both, pairs)

    def rim(feats, odd):
        return lax.dynamic_slice_in_dim(feats, odd * (nodes - HALO), HALO, 0)

    outer = trade(rim(node_feats, spot & 1), lambda i: i + 1 if i % 2 else i - 1)
    inner = trade(rim(node_feats, 1 - (spot & 1)), lambda i: i ^ 1)
    nbrs = (2 * neighbors).T.reshape(near, nodes // 128, 128).transpose(1, 0, 2).reshape(-1)
    bias = sage_bias.reshape(1, -1)
    hold = lax.optimization_barrier

    table = table_of(node_feats)
    conf_src, _ = conf_rows_of(
        flip,
        nbrs,
        conf_index,
        inner,
        outer,
        self_weight,
        neighbor_weight,
        bias,
        table,
    )

    def layer(first, steps, given):
        return layer_of(
            first,
            steps,
            flip,
            nbrs,
            inner,
            outer,
            node_feats,
            self_weight,
            neighbor_weight,
            bias,
            given,
        )

    swap = [(i, i ^ 1) for i in range(group_count)]

    def shift(value, by):
        return lax.ppermute(value, "cfg", [(i, i ^ (2 * by)) for i in range(group_count)])

    mine = lax.all_to_all(conf_src, "node", 0, 0, tiled=True)
    embed = layer(0, 2, None)
    weight = score_weight.reshape(1, -1)
    mine, embed, back = hold((mine, embed, prepared(mid_weight, weight)))
    weights = (layout_table, mid_weight, back)
    others = [shift(mine, by) for by in range(1, rings)]
    where = group.reshape(1)

    def scorer(final, turns, xs, given):
        return scorer_of(
            final,
            turns,
            where,
            xs,
            layout_ids,
            join_weight,
            join_bias.reshape(1, -1),
            weights,
            mid_bias.reshape(1, -1),
            weight,
            given,
        )

    pair, total = scorer(None, (0, rings), [mine, lax.ppermute(mine, "cfg", swap)], [])
    others = list(hold((*others, total)))
    total = others.pop()
    swapped = [lax.ppermute(x, "cfg", swap) for x in others]
    own, total = scorer(None, (1, 1), others, [total])
    swapped = list(hold((*swapped, total)))
    total = swapped.pop()
    other, sent = scorer((devices, 128), (rings + 1, 1), swapped, [total])
    sent, embed = hold((sent, embed))
    got = lax.all_to_all(sent.reshape(devices, 1, 128), both, 0, 0, tiled=True)
    embed = layer(2, 3, embed)
    got, embed = hold((got, embed))
    loss, coef, away = ranking_of(
        scale, where, got.reshape(devices, 128), config_pairs.T, pair, other
    )
    came = lax.ppermute(away, "cfg", swap)
    kept = rest_of(coef, pair, own)
    sums = [(kept[d].astype(f32) + came[d].astype(f32)).astype(bf16) for d in range(1, rings)]
    arrived = [shift(part, by) for by, part in enumerate(sums, 1)]
    local_grad, embed = hold((finish_of(kept, came, arrived, join_weight), embed))
    conf_grad = lax.all_to_all(local_grad, "node", 0, 0, tiled=True)
    embed = layer(5, 3, embed)
    conf_grad = returned_of(conf_grad)
    return (embed, loss.reshape(()), conf_grad)


def solution(mesh):
    split = P(("cfg", "node"), None)
    placed = (split, split, P(), P(), P(), P(("cfg", "node")), P("cfg", "node")) + (P(),) * 7
    return jax.shard_map(
        shards,
        mesh=mesh,
        in_specs=placed,
        out_specs=(split, P(), split),
        check_vma=False,
    )
```

```python
import functools
import math

import jax
import jax.numpy as jnp
from jax import lax
from jax.experimental import pallas as pl
from jax.experimental.pallas import tpu as pltpu
from jax.sharding import PartitionSpec as P

HALO = 512
f32 = jnp.float32
bf16 = jnp.bfloat16
VMEM = pl.BlockSpec(memory_space=pltpu.VMEM)
SMEM = pl.BlockSpec(memory_space=pltpu.SMEM)
HBM = pl.BlockSpec(memory_space=pltpu.HBM)


def in_hbm(value):
    return pltpu.with_memory_space_constraint(value, pltpu.HBM)


def half_silu(half):
    tanh = jnp.tanh(half)
    scaled = half * tanh
    return half + scaled, tanh, scaled


def twice_slope(half, tanh, scaled):
    inner = 1.0 + half - scaled
    return inner + tanh * inner


def halves_swapped(first, second):
    low = lax.broadcasted_iota(jnp.int32, first.shape, 1) < 4
    upper = jnp.where(low, first, pltpu.roll(second, 4, 1))
    lower = jnp.where(low, pltpu.roll(first, 4, 1), second)
    return upper, lower


def pack(value):
    rows = value.shape[0]
    sides = [value[:, at : at + 128].reshape(rows // 8, 8, 128) for at in (0, 128)]
    even, odd = halves_swapped(*sides)
    return jnp.stack([even, odd], axis=1).reshape(rows // 4, 8, 128)


def unpack(value):
    groups = value.shape[0]
    pairs = value.reshape(groups // 2, 2, 8, 128)
    left, right = halves_swapped(pairs[:, 0], pairs[:, 1])
    return jnp.concatenate([x.reshape(groups * 4, 128) for x in (left, right)], axis=1)


def put_rows(table, first, source):
    rows = source.shape[0]
    value = source[...].astype(f32)
    table[pl.ds(2 * first, rows, stride=2), :] = value[:, :128]
    table[pl.ds(2 * first + 1, rows, stride=2), :] = value[:, 128:]


def put_rims(table, flip, inner, outer):
    end = table.shape[0] // 2 - HALO
    put_rows(table, pl.multiple_of((1 - flip[0]) * end, HALO), inner)
    put_rows(table, pl.multiple_of(flip[0] * end, HALO), outer)


def pair_at(table, at):
    return table[pl.ds(pl.multiple_of(at, 2), 2), :]


def table_kernel(feats, table):
    rows = feats.shape[0]
    put_rows(table, HALO + pl.multiple_of(pl.program_id(0) * rows, rows), feats)


def table_of(feats):
    nodes, width = feats.shape
    tile = 512
    return pl.pallas_call(
        table_kernel,
        out_shape=jax.ShapeDtypeStruct((2 * (nodes + 2 * HALO), 128), f32),
        grid=(nodes // tile,),
        in_specs=[pl.BlockSpec((tile, width), lambda i: (i, 0))],
        out_specs=VMEM,
        cost_estimate=pl.CostEstimate(flops=1 << 20, transcendentals=0, bytes_accessed=6 << 20),
        compiler_params=pltpu.CompilerParams(vmem_limit_bytes=16 << 20),
        name="window_rows",
    )(feats)


def layer_rows(own_left, own_right, left, right, sw, nw, bias, kind=bf16):
    pre = jnp.dot(own_left, sw[:128, :], preferred_element_type=f32)
    pre += jnp.dot(own_right, sw[128:, :], preferred_element_type=f32)
    pre += jnp.dot(left, nw[:128, :], preferred_element_type=f32)
    pre += jnp.dot(right, nw[128:, :], preferred_element_type=f32)
    return half_silu(0.5 * (pre + bias[...]))[0].astype(kind)


def conf_kernel(flip, nbrs, picks, outer, inner, *refs):
    sw_hbm, nw_hbm, bias_hbm, given, out, table, own, acc, sw, nw, bias, sems = refs
    copies = [
        pltpu.make_async_copy(source, target, sems.at[i])
        for i, (source, target) in enumerate(((sw_hbm, sw), (nw_hbm, nw), (bias_hbm, bias)))
    ]
    for copy in copies:
        copy.start()
    put_rims(table, flip, inner, outer)
    count = picks.shape[0]
    own3 = own.reshape(count, 2, 128)
    acc3 = acc.reshape(count, 2, 128)

    def body(block, carry):
        values = []
        for j in range(8):
            g = picks[block * 8 + j]
            at = (g >> 7) * 512 + (g & 127)
            near = [pair_at(table, nbrs[at + 128 * k]) for k in range(4)]
            values.append((pair_at(table, 2 * (HALO + g)), (near[0] + near[1]) + (near[2] + near[3])))
        for j in range(8):
            own3[block * 8 + j], acc3[block * 8 + j] = values[j]
        return carry

    lax.fori_loop(0, count // 8, body, 0)
    halves = [ref[pl.ds(side, count, stride=2), :] for ref in (own, acc) for side in (0, 1)]
    for copy in copies:
        copy.wait()
    value = layer_rows(
        halves[0].astype(bf16),
        halves[1].astype(bf16),
        (halves[2] * 0.25).astype(bf16),
        (halves[3] * 0.25).astype(bf16),
        sw,
        nw,
        bias,
        f32,
    )
    out[...] = pack(value).astype(bf16)


def conf_rows_of(flip, nbrs, picks, inner, outer, sw, nw, bias, table):
    count = picks.shape[0]
    width = sw.shape[0]
    return pl.pallas_call(
        conf_kernel,
        out_shape=(
            jax.ShapeDtypeStruct((count // 4, 8, width // 2), bf16),
            jax.ShapeDtypeStruct(table.shape, f32),
        ),
        in_specs=[SMEM] * 3 + [VMEM] * 2 + [HBM] * 3 + [VMEM],
        out_specs=(VMEM, VMEM),
        input_output_aliases={8: 1},
        scratch_shapes=[
            pltpu.VMEM((2 * count, 128), f32),
            pltpu.VMEM((2 * count, 128), f32),
            pltpu.VMEM(sw.shape, bf16),
            pltpu.VMEM(nw.shape, bf16),
            pltpu.VMEM(bias.shape, f32),
            pltpu.SemaphoreType.DMA((3,)),
        ],
        cost_estimate=pl.CostEstimate(
            flops=4 * count * width * width, transcendentals=0, bytes_accessed=6 << 20
        ),
        compiler_params=pltpu.CompilerParams(vmem_limit_bytes=16 << 20),
        name="conf_rows",
    )(flip, nbrs, picks, outer, inner, in_hbm(sw), in_hbm(nw), in_hbm(bias), table)


def layer_kernel(flip, nbrs, inner, outer, feats, own, sw, nw, bias, *refs):
    out, table, acc = refs[-3:]
    tile = own.shape[0]
    nodes = feats.shape[0]

    @pl.when(pl.program_id(0) == 0)
    def _():
        put_rims(table, flip, inner, outer)
        for start in range(0, nodes, 512):
            put_rows(table, HALO + start, feats.at[start : start + 512, :])

    acc3 = acc.reshape(tile, 2, 128)
    some = 128

    part = 32

    def gather(block, first):
        values = []
        for j in range(first, first + part):
            near = [pair_at(table, nbrs[block * 512 + (128 * k + j)]) for k in range(4)]
            values.append((near[0] + near[1]) + (near[2] + near[3]))
        for j, value in enumerate(values, first):
            acc3[block * some + j] = value

    def products(block):
        start = block * some
        sides = [
            (acc[pl.ds(2 * start + side, some, stride=2), :] * 0.25).astype(bf16)
            for side in (0, 1)
        ]
        pre = jnp.dot(own[start : start + some, :], sw[...], preferred_element_type=f32)
        pre += jnp.dot(sides[0], nw[:128, :], preferred_element_type=f32)
        return pre + jnp.dot(sides[1], nw[128:, :], preferred_element_type=f32)

    blocks = tile // some
    for block in range(blocks + 1):
        pre = products(block - 1) if block > 0 else None
        for first in range(0, some, part):
            if block < blocks:
                gather(block, first)
            if block > 0:
                start = (block - 1) * some + first
                half = 0.5 * (pre[first : first + part, :] + bias[...])
                out[start : start + part, :] = half_silu(half)[0].astype(bf16)


def layer_of(first, steps, flip, nbrs, inner, outer, feats, sw, nw, bias, given):
    nodes, width = feats.shape
    tile = 512
    ahead = [] if given is None else [given]
    return pl.pallas_call(
        layer_kernel,
        out_shape=jax.ShapeDtypeStruct((nodes, width), bf16),
        grid=(steps,),
        in_specs=[
            SMEM,
            pl.BlockSpec((4 * tile,), lambda i: (first + i,), memory_space=pltpu.SMEM),
            VMEM,
            VMEM,
            VMEM,
            pl.BlockSpec((tile, width), lambda i: (first + i, 0)),
            VMEM,
            VMEM,
            VMEM,
        ]
        + [HBM] * len(ahead),
        out_specs=pl.BlockSpec((tile, width), lambda i: (first + i, 0)),
        input_output_aliases={9: 0} if ahead else {},
        scratch_shapes=[
            pltpu.VMEM((2 * (nodes + 2 * HALO), 128), f32),
            pltpu.VMEM((2 * tile, 128), f32),
        ],
        cost_estimate=pl.CostEstimate(
            flops=steps * 4 * tile * width * width, transcendentals=0, bytes_accessed=steps << 23
        ),
        compiler_params=pltpu.CompilerParams(vmem_limit_bytes=24 << 20),
        name="graph_layer",
    )(flip, nbrs, inner, outer, feats, feats, sw, nw, bias, *ahead)


def place_of(group, turn):
    return group ^ (2 * (turn & 3) + (turn >> 2))


def prepare_kernel(mid, weight, back):
    back[...] = jnp.transpose(mid[...].astype(f32) * (weight[...] * 0.25)).astype(bf16)


def prepared(mid, weight):
    return pl.pallas_call(
        prepare_kernel,
        out_shape=jax.ShapeDtypeStruct(mid.shape, bf16),
        in_specs=[VMEM] * 2,
        out_specs=VMEM,
        cost_estimate=pl.CostEstimate(flops=1 << 20, transcendentals=0, bytes_accessed=1 << 19),
        compiler_params=pltpu.CompilerParams(vmem_limit_bytes=8 << 20),
        name="prepare",
    )(mid, weight)


def scorer_kernel(groups, final, where, *refs):
    xs, refs = refs[:groups], refs[groups:]
    ids, join, jbias, table, mid, back, mbias, weight = refs[:8]
    given, refs = refs[8:-8], refs[-8:]
    grads_hbm, sent, base, tabh, midh, total, grads, sems = refs
    step = pl.program_id(0)
    slot = step & 1
    chunk = base.shape[1]
    configs = ids.shape[0]
    layouts = table.shape[0]
    one = jnp.asarray(1.0, bf16)

    @pl.when(step == 0)
    def _():
        for i in range(groups):
            base[i] = 0.5 * (
                jnp.dot(
                    unpack(xs[i][...].astype(f32)).astype(bf16),
                    join[...],
                    preferred_element_type=f32,
                )
                + jbias[...]
            )
        tabh[...] = (table[...].astype(f32) * 0.5).astype(bf16)
        midh[...] = (mid[...].astype(f32) * 0.5).astype(bf16)
        total[...] = given[0][...] if given else jnp.zeros_like(total)

    some = 8

    def copy_of(turn, place, first):
        part = pl.ds(first, some)
        return pltpu.make_async_copy(
            grads.at[place, part], grads_hbm.at[turn, part], sems.at[place, first // some]
        )

    def wait_for(turn, place):
        for first in range(0, configs, some):
            copy_of(turn, place, first).wait()

    @pl.when(step >= 2)
    def _():
        wait_for(step - 2, slot)

    columns = jnp.transpose(ids[...].astype(f32))
    lanes = lax.broadcasted_iota(jnp.int32, (chunk, layouts), 1).astype(f32)
    rows = base[step]
    for first in range(0, configs, some):
        picks = jnp.concatenate(
            [
                jnp.where(columns[:, k : k + 1] == lanes, 1.0, 0.0).astype(bf16)
                for k in range(first, first + some)
            ],
            axis=0,
        )
        half = jnp.dot(picks, tabh[...], preferred_element_type=f32)
        half = (half + jnp.concatenate([rows] * some, axis=0)).astype(bf16)
        tanh = jnp.tanh(half)
        above = one + tanh
        slope = above * (one + half * (one - tanh))
        outer = jnp.dot(half * above, midh[...], preferred_element_type=f32)
        outer = (outer + 0.5 * mbias[...]).astype(bf16)
        tanh2 = jnp.tanh(outer)
        above2 = one + tanh2
        act2 = (outer * above2).astype(f32)
        slope2 = above2 * (one + outer * (one - tanh2))
        for q in range(some):
            part = act2[q * chunk : (q + 1) * chunk, :]
            total[first + q : first + q + 1, :] += jnp.sum(part, axis=0, keepdims=True)
        grad = jnp.dot(slope2, back[...], preferred_element_type=f32).astype(bf16) * slope
        for q in range(some):
            grads[slot, first + q] = grad[q * chunk : (q + 1) * chunk, :]
        copy_of(step, slot, first).start()

    @pl.when(step == groups - 1)
    def _():
        if final:
            scores = jnp.sum(total[...] * weight[...], axis=1, keepdims=True)
            lane = lax.broadcasted_iota(jnp.int32, (configs, 128), 1)
            sub = lax.broadcasted_iota(jnp.int32, (configs, 128), 0)
            spread = jnp.where(lane == sub + where[0] * configs, scores, 0.0)
            sent[...] = jnp.broadcast_to(jnp.sum(spread, axis=0, keepdims=True), sent.shape)
        else:
            sent[...] = total[...]
        wait_for(step - 1, 1 - slot)
        wait_for(step, slot)


def scorer_of(final, turns, where, xs, ids, join, jbias, weights, mbias, weight, given):
    groups = len(xs)
    configs = ids.shape[0]
    chunk = xs[0].shape[0] * 4
    width, hidden = join.shape
    start, stride = turns
    summed = final if final else (configs, hidden)
    return pl.pallas_call(
        functools.partial(scorer_kernel, groups, final),
        out_shape=(
            pltpu.HBM((groups, configs, chunk, hidden), bf16),
            jax.ShapeDtypeStruct(summed, f32),
        ),
        grid_spec=pltpu.PrefetchScalarGridSpec(
            num_scalar_prefetch=1,
            grid=(groups,),
            in_specs=[VMEM] * groups
            + [
                pl.BlockSpec(
                    (configs, chunk), lambda i, where: (0, place_of(where[0], start + stride * i))
                )
            ]
            + [VMEM] * (7 + len(given)),
            out_specs=(HBM, VMEM),
            scratch_shapes=[
                pltpu.VMEM((groups, chunk, hidden), f32),
                pltpu.VMEM(weights[0].shape, bf16),
                pltpu.VMEM(weights[1].shape, bf16),
                pltpu.VMEM((configs, hidden), f32),
                pltpu.VMEM((2, configs, chunk, hidden), bf16),
                pltpu.SemaphoreType.DMA((2, 2)),
            ],
        ),
        cost_estimate=pl.CostEstimate(
            flops=6 * groups * configs * chunk * width * width,
            transcendentals=2 * groups * configs * chunk * width,
            bytes_accessed=groups << 20,
        ),
        compiler_params=pltpu.CompilerParams(vmem_limit_bytes=24 << 20),
        name="scorer",
    )(where, *xs, ids, join, jbias, *weights, mbias, weight, *given)


def weighted(coef, grads, out):
    configs, chunk, hidden = grads.shape
    some = 32
    for start in range(0, chunk, some):
        rows = grads[0, start : start + some, :].astype(f32) * coef[0:1, :]
        for k in range(1, configs):
            rows = rows + grads[k, start : start + some, :].astype(f32) * coef[k : k + 1, :]
        out[start : start + some, :] = rows.astype(bf16)


def fetches(pair, later, which, grads, sems):
    sources = [pair.at[which]] + [later.at[d] for d in range(grads.shape[0] - 1)]
    return [
        pltpu.make_async_copy(source, grads.at[d], sems.at[d]) for d, source in enumerate(sources)
    ]


def ranking_kernel(scale, where, got, pairs, pair, later, loss, coef, out, column, grads, sems):
    half, configs, chunk, hidden = grads.shape
    copies = fetches(pair, later, 1, grads, sems)
    for copy in copies:
        copy.start()
    score = jnp.sum(got[...], axis=0, keepdims=True) * scale
    lane = lax.broadcasted_iota(jnp.int32, (128, 128), 1)
    sub = lax.broadcasted_iota(jnp.int32, (128, 128), 0)
    score = jnp.sum(jnp.where(lane == sub, score, 0.0), axis=1, keepdims=True)
    count = pairs.shape[1]
    ids = lax.broadcasted_iota(jnp.int32, (128, count), 0)
    second = jnp.where(pairs[1:2, :] == ids, 1.0, 0.0)
    signed = second - jnp.where(pairs[0:1, :] == ids, 1.0, 0.0)
    gap = jnp.sum(signed * score, axis=0, keepdims=True)
    fade = jnp.exp(-jnp.abs(gap))
    soft = jnp.maximum(gap, 0.0) + jnp.log1p(fade)
    loss[...] = jnp.sum(soft, axis=1, keepdims=True) * (1.0 / count)
    slope = jnp.where(gap >= 0.0, 1.0, fade) / (1.0 + fade)
    grad = jnp.sum(slope * signed, axis=1, keepdims=True) * (65536.0 * scale / count)
    column[...] = jnp.broadcast_to(grad, column.shape)
    coef[...] = column[pl.ds(pl.multiple_of(where[0] * configs, configs), configs), :]
    for d in range(half):
        copies[d].wait()
        weighted(coef, grads.at[d], out.at[d])


def ranking_of(scale, where, got, pairs, pair, later):
    half, configs, chunk, hidden = later.shape
    half += 1
    return pl.pallas_call(
        functools.partial(ranking_kernel, scale),
        out_shape=(
            jax.ShapeDtypeStruct((1, 1), f32),
            jax.ShapeDtypeStruct((configs, hidden), f32),
            jax.ShapeDtypeStruct((half, chunk, hidden), bf16),
        ),
        in_specs=[SMEM, VMEM, VMEM, HBM, HBM],
        out_specs=(VMEM, VMEM, VMEM),
        scratch_shapes=[
            pltpu.VMEM((128, hidden), f32),
            pltpu.VMEM((half, configs, chunk, hidden), bf16),
            pltpu.SemaphoreType.DMA((half,)),
        ],
        cost_estimate=pl.CostEstimate(flops=1 << 24, transcendentals=0, bytes_accessed=6 << 20),
        compiler_params=pltpu.CompilerParams(vmem_limit_bytes=16 << 20),
        name="ranking",
    )(where, got, pairs, in_hbm(pair), in_hbm(later))


def rest_kernel(coef, pair, later, out, grads, sems):
    copies = fetches(pair, later, 0, grads, sems)
    for copy in copies:
        copy.start()
    for d, copy in enumerate(copies):
        copy.wait()
        weighted(coef, grads.at[d], out.at[d])


def rest_of(coef, pair, later):
    half, configs, chunk, hidden = later.shape
    half += 1
    return pl.pallas_call(
        rest_kernel,
        out_shape=jax.ShapeDtypeStruct((half, chunk, hidden), bf16),
        in_specs=[VMEM, HBM, HBM],
        out_specs=VMEM,
        scratch_shapes=[
            pltpu.VMEM((half, configs, chunk, hidden), bf16),
            pltpu.SemaphoreType.DMA((half,)),
        ],
        cost_estimate=pl.CostEstimate(flops=1 << 24, transcendentals=0, bytes_accessed=6 << 20),
        compiler_params=pltpu.CompilerParams(vmem_limit_bytes=16 << 20),
        name="rest",
    )(coef, in_hbm(pair), in_hbm(later))


def finish_kernel(kept, came, *refs):
    arrived, (join, out) = refs[:-2], refs[-2:]
    rows = kept[0].astype(f32) + came[0].astype(f32)
    for part in arrived:
        rows = rows + part[...].astype(f32)
    value = lax.dot_general(
        rows.astype(bf16), join[...], (((1,), (1,)), ((), ())), preferred_element_type=f32
    )
    out[...] = pack(value).astype(bf16)


def finish_of(kept, came, arrived, join):
    rows, width = kept.shape[1], join.shape[0]
    return pl.pallas_call(
        finish_kernel,
        out_shape=jax.ShapeDtypeStruct((rows // 4, 8, width // 2), bf16),
        in_specs=[VMEM] * (3 + len(arrived)),
        out_specs=VMEM,
        cost_estimate=pl.CostEstimate(flops=1 << 24, transcendentals=0, bytes_accessed=1 << 19),
        compiler_params=pltpu.CompilerParams(vmem_limit_bytes=8 << 20),
        name="finish",
    )(kept, came, *arrived, join)


def returned_kernel(value, out):
    out[...] = unpack(value[...].astype(f32))


def returned_of(value):
    groups = value.shape[0]
    return pl.pallas_call(
        returned_kernel,
        out_shape=jax.ShapeDtypeStruct((groups * 4, 256), f32),
        in_specs=[VMEM],
        out_specs=VMEM,
        cost_estimate=pl.CostEstimate(flops=1 << 16, transcendentals=0, bytes_accessed=1 << 18),
        compiler_params=pltpu.CompilerParams(vmem_limit_bytes=8 << 20),
        name="returned",
    )(value)


def shards(
    node_feats,
    neighbors,
    self_weight,
    neighbor_weight,
    sage_bias,
    conf_index,
    layout_ids,
    join_weight,
    layout_table,
    join_bias,
    mid_weight,
    mid_bias,
    score_weight,
    config_pairs,
):
    both = ("cfg", "node")
    devices = lax.axis_size(both)
    node_count = lax.axis_size("node")
    group_count = lax.axis_size("cfg")
    rings = group_count // 2
    scale = 1.0 / math.sqrt(layout_ids.shape[1] * node_count)
    group = lax.axis_index("cfg")

    nodes, near = neighbors.shape
    spot = lax.axis_index("node")
    flip = (spot & 1).reshape(1)

    def trade(rows, partner):
        pairs = [(i, partner(i)) for i in range(devices) if 0 <= partner(i) < devices]
        return lax.ppermute(rows, both, pairs)

    def rim(feats, odd):
        return lax.dynamic_slice_in_dim(feats, odd * (nodes - HALO), HALO, 0)

    outer = trade(rim(node_feats, spot & 1), lambda i: i + 1 if i % 2 else i - 1)
    inner = trade(rim(node_feats, 1 - (spot & 1)), lambda i: i ^ 1)
    nbrs = (2 * neighbors).T.reshape(near, nodes // 128, 128).transpose(1, 0, 2).reshape(-1)
    bias = sage_bias.reshape(1, -1)
    hold = lax.optimization_barrier

    table = table_of(node_feats)
    conf_src, _ = conf_rows_of(
        flip,
        nbrs,
        conf_index,
        inner,
        outer,
        self_weight,
        neighbor_weight,
        bias,
        table,
    )

    def layer(first, steps, given):
        return layer_of(
            first,
            steps,
            flip,
            nbrs,
            inner,
            outer,
            node_feats,
            self_weight,
            neighbor_weight,
            bias,
            given,
        )

    swap = [(i, i ^ 1) for i in range(group_count)]

    def shift(value, by):
        return lax.ppermute(value, "cfg", [(i, i ^ (2 * by)) for i in range(group_count)])

    mine = lax.all_to_all(conf_src, "node", 0, 0, tiled=True)
    embed = layer(0, 2, None)
    weight = score_weight.reshape(1, -1)
    mine, embed, back = hold((mine, embed, prepared(mid_weight, weight)))
    weights = (layout_table, mid_weight, back)
    others = [shift(mine, by) for by in range(1, rings)]
    where = group.reshape(1)

    def scorer(final, turns, xs, given):
        return scorer_of(
            final,
            turns,
            where,
            xs,
            layout_ids,
            join_weight,
            join_bias.reshape(1, -1),
            weights,
            mid_bias.reshape(1, -1),
            weight,
            given,
        )

    pair, total = scorer(None, (0, rings), [mine, lax.ppermute(mine, "cfg", swap)], [])
    others = list(hold((*others, total)))
    total = others.pop()
    swapped = [lax.ppermute(x, "cfg", swap) for x in others]
    own, total = scorer(None, (1, 1), others, [total])
    swapped = list(hold((*swapped, total)))
    total = swapped.pop()
    other, sent = scorer((devices, 128), (rings + 1, 1), swapped, [total])
    sent, embed = hold((sent, embed))
    got = lax.all_to_all(sent.reshape(devices, 1, 128), both[::-1], 0, 0, tiled=True)
    embed = layer(2, 3, embed)
    got, embed = hold((got, embed))
    loss, coef, away = ranking_of(
        scale, where, got.reshape(devices, 128), config_pairs.T, pair, other
    )
    came = lax.ppermute(away, "cfg", swap)
    kept = rest_of(coef, pair, own)
    sums = [(kept[d].astype(f32) + came[d].astype(f32)).astype(bf16) for d in range(1, rings)]
    arrived = [shift(part, by) for by, part in enumerate(sums, 1)]
    local_grad, embed = hold((finish_of(kept, came, arrived, join_weight), embed))
    conf_grad = lax.all_to_all(local_grad, "node", 0, 0, tiled=True)
    embed = layer(5, 3, embed)
    conf_grad = returned_of(conf_grad)
    return (embed, loss.reshape(()), conf_grad)


def solution(mesh):
    split = P(("cfg", "node"), None)
    placed = (split, split, P(), P(), P(), P(("cfg", "node")), P("cfg", "node")) + (P(),) * 7
    return jax.shard_map(
        shards,
        mesh=mesh,
        in_specs=placed,
        out_specs=(split, P(), split),
        check_vma=False,
    )
```
